32 devices in a mesh: dp: 8 (over y, x, core), ctx: 4 (over z).
Axes of the slice: x: 2, y: 2, z: 4, core: 2. Of those that a mesh axis runs over, the one named last changes fastest.
Arguments:
- tokens: bfloat16 [8192, 768], P(('dp', 'ctx')), may hold values from -6 to 6
- cotangent: bfloat16 [8192, 768], P(('dp', 'ctx')), may hold values from -6 to 6
- token_order: int32 [8192], P(('dp', 'ctx')), may hold values from 0 to 8191, as said below
- sequence_ids: int32 [8, 1024], P('dp'), may hold values from 0 to 3, never falling along the last dimension, each value on 1 to 512 neighbouring positions
- valid: int32 [8192], P(('dp', 'ctx')), may hold values from 0 to 1
- teacher: float32 [8192, 768], P(('dp', 'ctx')), may hold values from -6 to 6
- w_query: bfloat16 [768, 768], P('dp'), may hold values from -0.3125 to 0.3125
- b_query: bfloat16 [768], P('dp'), may hold values from -1.75 to 1.75
- w_key: bfloat16 [768, 768], P('dp'), may hold values from -0.3125 to 0.3125
- w_value: bfloat16 [768, 768], P('dp'), may hold values from -0.21875 to 0.21875
- b_value: bfloat16 [768], P('dp'), may hold values from -1.75 to 1.75
- w_out: bfloat16 [768, 768], P('dp'), may hold values from -0.875 to 0.875
- b_out: bfloat16 [768], P('dp'), may hold values from -3 to 3
- norm1_gain: bfloat16 [768], P('dp'), may hold values from 0.25 to 1.75
- norm1_bias: bfloat16 [768], P('dp'), may hold values from -1.75 to 1.75
- w_up: bfloat16 [768, 3072], P('dp'), may hold values from -0.21875 to 0.21875
- b_up: bfloat16 [3072], P('dp'), may hold values from -3 to 3
- w_down: bfloat16 [3072, 768], P('dp'), may hold values from -0.109375 to 0.109375
- b_down: bfloat16 [768], P('dp'), may hold values from -1.75 to 1.75
- norm2_gain: bfloat16 [768], P('dp'), may hold values from 0.25 to 1.75
- norm2_bias: bfloat16 [768], P('dp'), may hold values from -1.75 to 1.75
Outputs:
- output: float32 [8192, 768], P(('dp', 'ctx'))
- loss: float32 [], replicated
- input_grad: float32 [8192, 768], P(('dp', 'ctx'))
- grad_w_query: float32 [768, 768], P('dp')
- grad_b_query: float32 [768], P('dp')
- grad_w_key: float32 [768, 768], P('dp')
- grad_w_value: float32 [768, 768], P('dp')
- grad_b_value: float32 [768], P('dp')
- grad_w_out: float32 [768, 768], P('dp')
- grad_b_out: float32 [768], P('dp')
- grad_norm1_gain: float32 [768], P('dp')
- grad_norm1_bias: float32 [768], P('dp')
- grad_w_up: float32 [768, 3072], P('dp')
- grad_b_up: float32 [3072], P('dp')
- grad_w_down: float32 [3072, 768], P('dp')
- grad_b_down: float32 [768], P('dp')
- grad_norm2_gain: float32 [768], P('dp')
- grad_norm2_bias: float32 [768], P('dp')
The draws below stay inside these ranges and needn't reach their ends.
Inputs may be any that keep to these rules, and one draw needn't show every extreme that they name: `token_order`: a permutation of the 8192 tokens; each aligned block of 256 packed positions takes exactly 8 tokens from each aligned block of 256 given tokens. `sequence_ids`: ids of a row never fall; a sequence has at most 512 tokens, and some has exactly that many.
All inputs are finite; a program needn't handle non-finite values.
Results may differ from the reference program's by a relative error of at most 0.023.
Values may be sent and summed in bfloat16 or wider, within the bound.
A program may use at most 128 MiB of HBM per device.

```python
import math
import jax
import jax.numpy as jnp
import numpy as np
from jax import lax

D = 768
HEADS = 12
HEAD = 64
FF = 3072
TOK_DEV = 256
SEQS = 4
GROUP = 1024
TOKENS = 8192
N_DP = 8


def draw_token_order(key, part):
    blocks = TOKENS // TOK_DEV
    per_block = TOK_DEV // blocks
    slot_keys = jax.random.split(jax.random.fold_in(key, 11), blocks)
    token_keys = jax.random.split(jax.random.fold_in(key, 23), blocks)
    slot_perm = jax.vmap(lambda item_key: jax.random.permutation(item_key, TOK_DEV))(slot_keys).astype(jnp.int32)
    token_perm = jax.vmap(lambda item_key: jax.random.permutation(item_key, TOK_DEV))(token_keys).astype(jnp.int32)
    source = slot_perm // per_block
    within = slot_perm % per_block
    target = jnp.arange(blocks, dtype=jnp.int32)[:, None]
    local_index = token_perm[source, target * per_block + within]
    return (source * TOK_DEV + local_index).reshape(TOKENS).astype(jnp.int32)


def draw_valid(key, part):
    ranks = jax.random.randint(key, (TOKENS,), 0, 1000, dtype=jnp.int32)
    threshold = 250 + 500 * jnp.arange(TOKENS, dtype=jnp.int32) // TOKENS
    return (ranks < threshold).astype(jnp.int32)


def shard_levels(own_key, shape, cuts, low, top_value):
    loudness, own = 1.0, jax.random.fold_in(own_key, 6)
    for position, parts in cuts:
        heights = jnp.exp(jax.random.uniform(jax.random.fold_in(own, position), (parts,), jnp.float32, low / len(cuts), top_value / len(cuts)))
        loudness = loudness * jnp.repeat(heights, shape[position] // parts).reshape([-1 if axis == position else 1 for axis in range(len(shape))])
    return loudness


def profile(count, total, most, lean):
    portions = [(1 << 20) // math.isqrt(grade ** lean) + 1 for grade in range(2, count + 1)]
    surplus, holding = total - most - (count - 1), [1] * (count - 1)
    while surplus > 0:
        free = [i for i in range(count - 1) if holding[i] < most]
        pool, left = sum([portions[i] for i in free]), surplus
        for i in free:
            more = min(most - holding[i], max(1, left * portions[i] // pool), surplus)
            holding[i] = holding[i] + more
            surplus = surplus - more
    return np.array([most] + holding)


def ragged_sizes(key, number_of, total, limit, slope):
    if number_of == 2:
        one = jax.random.randint(key, (), max(1, total - limit), min(limit, total - 1) + 1)
        return jnp.stack([one, total - one])
    sizes = jnp.asarray(profile(number_of, total, limit, slope), jnp.int32)
    couples = (number_of - 1) // 2
    donor, sink = sizes[1:1 + 2 * couples:2], sizes[2:2 + 2 * couples:2]
    margin = jnp.minimum(donor - 1, limit - sink)
    shifted = jax.random.randint(jax.random.fold_in(key, 1), (couples,), 0, 1 << 20) % (margin + 1)
    sizes = sizes.at[1:1 + 2 * couples:2].set(donor - shifted).at[2:2 + 2 * couples:2].set(sink + shifted)
    return sizes[jax.random.permutation(jax.random.fold_in(key, 2), number_of)]


def normal_values(stream_key, extent, width, limit, shards=(), kind=jnp.bfloat16):
    values = jax.random.normal(stream_key, extent, jnp.float32) * width
    if len(shards) > 0:
        values = shard_levels(stream_key, extent, shards, -0.22, 0.18) * values
    return jnp.clip(values, min=-limit, max=limit).astype(kind)


def setup_inputs(seed: int = 0) -> dict:
    splits = jax.random.split(jax.random.key(seed), 22)
    tokens = normal_values(splits[0], (TOKENS, D), 1.0, 6.0, ((0, 32),))
    cotangent = normal_values(splits[1], (TOKENS, D), 1.0, 6.0, ((0, 32),))
    token_order = draw_token_order(jax.random.fold_in(splits[21], 71), 0)
    sequence_ids = jax.vmap(lambda own: jnp.searchsorted(jnp.cumsum(ragged_sizes(own, SEQS, GROUP, GROUP // 2, 1)), jnp.arange(GROUP), side="right"))(jax.random.split(splits[3], N_DP)).reshape((N_DP, GROUP)).astype(jnp.int32)
    valid = draw_valid(jax.random.fold_in(splits[21], 71), 0)
    teacher = normal_values(splits[5], (TOKENS, D), 1.0, 6.0, ((0, 32),), jnp.float32)
    w_query = normal_values(splits[6], (D, D), (D // 2) ** -0.5, 0.3125, ((0, 8),))
    b_query = normal_values(splits[7], (D,), 0.3, 1.75, ((0, 8),))
    w_key = normal_values(splits[8], (D, D), (D // 2) ** -0.5, 0.3125, ((0, 8),))
    w_value = normal_values(splits[9], (D, D), D ** -0.5, 0.21875, ((0, 8),))
    b_value = normal_values(splits[10], (D,), 0.3, 1.75, ((0, 8),))
    w_out = normal_values(splits[11], (D, D), (D // 16) ** -0.5, 0.875, ((0, 8),))
    b_out = normal_values(splits[12], (D,), 0.5, 3.0, ((0, 8),))
    norm1_gain = jnp.clip(1.0 + 0.15 * jax.random.normal(splits[13], (D,), jnp.float32), 0.25, 1.75).astype(jnp.bfloat16)
    norm1_bias = normal_values(splits[14], (D,), 0.3, 1.75, ((0, 8),))
    w_up = normal_values(splits[15], (D, FF), D ** -0.5, 0.21875, ((0, 8),))
    b_up = normal_values(splits[16], (FF,), 0.5, 3.0, ((0, 8),))
    w_down = normal_values(splits[17], (FF, D), FF ** -0.5, 0.109375, ((0, 8),))
    b_down = normal_values(splits[18], (D,), 0.3, 1.75, ((0, 8),))
    norm2_gain = jnp.clip(1.0 + 0.15 * jax.random.normal(splits[19], (D,), jnp.float32), 0.25, 1.75).astype(jnp.bfloat16)
    norm2_bias = normal_values(splits[20], (D,), 0.3, 1.75, ((0, 8),))
    return {"tokens": tokens, "cotangent": cotangent, "token_order": token_order, "sequence_ids": sequence_ids, "valid": valid, "teacher": teacher, "w_query": w_query, "b_query": b_query, "w_key": w_key, "w_value": w_value, "b_value": b_value, "w_out": w_out, "b_out": b_out, "norm1_gain": norm1_gain, "norm1_bias": norm1_bias, "w_up": w_up, "b_up": b_up, "w_down": w_down, "b_down": b_down, "norm2_gain": norm2_gain, "norm2_bias": norm2_bias}


@jax.custom_vjp
def low(v):
    return lax.optimization_barrier(v.astype(jnp.bfloat16)).astype(jnp.float32)

@jax.custom_vjp
def low_back(v):
    return v

def low_keep(v):
    return (low(v), None)

def low_pass(kept, grad):
    return (grad,)

def back_keep(v):
    return (v, None)

def back_low(kept, grad):
    return (low(grad),)
low.defvjp(low_keep, low_pass)
low_back.defvjp(back_keep, back_low)
precise = lax.Precision.HIGHEST
norm_eps = 1e-12

def matmul(left, right):
    return jnp.dot(left, right, precision=precise)

def both_ways(value):
    return low(low_back(value))

def layer_norm(value, gain, shift):
    centre = value - lax.optimization_barrier(jnp.mean(value, -1, keepdims=True))
    spread = lax.optimization_barrier(jnp.mean(centre * centre, -1, keepdims=True))
    return centre * lax.rsqrt(spread + norm_eps) * gain + shift

def block_attention(queries, query_ids, key_rows, values, key_ids):
    scores = jnp.einsum('qhd,khd->hqk', queries, key_rows, precision=precise) * HEAD ** (-0.5)
    scores = jnp.where((query_ids[:, None] == key_ids[None, :])[None], scores, -1e+30)
    scores = low_back(scores)
    highest = lax.optimization_barrier(jnp.max(scores, -1, keepdims=True))
    weights = jnp.exp(scores - highest)
    weights = low(weights / lax.optimization_barrier(jnp.sum(weights, -1, keepdims=True)))
    return jnp.einsum('hqk,khd->qhd', weights, values, precision=precise)

def group_attention(inputs):
    queries, key_rows, values, group_ids = inputs
    rows_block = math.gcd(GROUP, 512)
    count_blocks = GROUP // rows_block
    blocked = jax.checkpoint(block_attention)

    def one_block(pieces):
        return blocked(pieces[0], pieces[1], key_rows, values, group_ids)
    result = lax.map(one_block, (queries.reshape(count_blocks, rows_block, HEADS, HEAD), group_ids.reshape(count_blocks, rows_block)))
    return result.reshape(GROUP, HEADS, HEAD)

def reference(tokens, cotangent, token_order, sequence_ids, valid, teacher, w_query, b_query, w_key, w_value, b_value, w_out, b_out, norm1_gain, norm1_bias, w_up, b_up, w_down, b_down, norm2_gain, norm2_bias):
    params = tuple((item.astype(jnp.float32) for item in (w_query, b_query, w_key, w_value, b_value, w_out, b_out, norm1_gain, norm1_bias, w_up, b_up, w_down, b_down, norm2_gain, norm2_bias)))
    inverse = jnp.argsort(token_order).astype(jnp.int32)
    valid_rows = valid.astype(jnp.float32)
    target = teacher.astype(jnp.float32)

    def forward(inputs, weights):
        query_weight, query_bias, key_weight, value_weight, value_bias, out_weight, out_bias, gain_one, shift_one, up_weight, up_bias, down_weight, down_bias, gain_two, shift_two = weights
        packed = inputs[token_order]
        queries = both_ways(matmul(packed, query_weight) + query_bias)
        key_rows = both_ways(matmul(packed, key_weight))
        values = both_ways(matmul(packed, value_weight) + value_bias)
        attended = lax.map(group_attention, (queries.reshape(N_DP, GROUP, HEADS, HEAD), key_rows.reshape(N_DP, GROUP, HEADS, HEAD), values.reshape(N_DP, GROUP, HEADS, HEAD), sequence_ids))
        context = both_ways(attended.reshape(TOKENS, D))
        branch = low_back(matmul(context, out_weight) + out_bias)
        normed = layer_norm(packed + branch, gain_one, shift_one)
        pre_act = low_back(matmul(low(normed), up_weight) + up_bias)
        activated = low(jax.nn.gelu(pre_act, approximate=False))
        ffn_out = low_back(matmul(activated, down_weight) + down_bias)
        result = layer_norm(normed + ffn_out, gain_two, shift_two)
        difference = result - target
        valid_total = jnp.sum(valid_rows)
        loss_value = jnp.sum(valid_rows[:, None] * difference * difference) / (valid_total * D)
        return (result[inverse], loss_value)
    (output, loss_value), pullback = jax.vjp(forward, tokens.astype(jnp.float32), params)
    input_grad, grads = pullback((cotangent.astype(jnp.float32), jnp.ones((), jnp.float32)))
    return (output, loss_value, input_grad, grads[0], grads[1], grads[2], grads[3], grads[4], grads[5], grads[6], grads[7], grads[8], grads[9], grads[10], grads[11], grads[12], grads[13], grads[14])
```

```python
import math
from functools import partial
import jax
import jax.numpy as jnp
from jax import lax
from jax.experimental import pallas as pl
from jax.experimental.pallas import tpu as pltpu
from jax.sharding import PartitionSpec as P

MESH = pl.DeviceIdType.MESH
F32, BF16 = jnp.float32, jnp.bfloat16


class Place:
    def __init__(self, z_size):
        dp, z = lax.axis_index("dp"), lax.axis_index("ctx")
        self.dp, self.z, self.z_size = dp, z, z_size
        core, x, y = dp % 2, dp // 2 % 2, dp // 4
        self.core = core
        self.mate = {"dp": dp + 1 - 2 * core}
        self.across = {"dp": dp + 2 - 4 * x}
        self.along = {"dp": dp + 4 - 8 * y}
        self.j_own = y * 2 + x
        self.j_x = y * 2 + 1 - x
        self.j_y = (1 - y) * 2 + x
        self.j_d = (1 - y) * 2 + 1 - x


def greet(place):
    barrier = pltpu.get_barrier_semaphore()
    for other in (place.mate, place.across, place.along):
        pl.semaphore_signal(barrier, inc=1, device_id=other, device_id_type=MESH)

    @pl.when(place.z > 0)
    def _():
        pl.semaphore_signal(barrier, inc=1, device_id={"ctx": place.z - 1}, device_id_type=MESH)

    @pl.when(place.z < place.z_size - 1)
    def _():
        pl.semaphore_signal(barrier, inc=1, device_id={"ctx": place.z + 1}, device_id_type=MESH)

    last = place.z_size - 1
    neighbours = (place.z + last) // place.z_size + (2 * last - place.z) // place.z_size
    pl.semaphore_wait(barrier, 3 + neighbours)


def remote(src, dst, send, recv, to):
    return pltpu.make_async_remote_copy(
        src_ref=src, dst_ref=dst, send_sem=send, recv_sem=recv, device_id=to, device_id_type=MESH
    )


UNITS = 12
BLOCK = 96
LEFT = (0, 1, 2, 3, 4, 4, 4, 4, 5, 6, 6, 6)


def grad_scratch(tok_rows, width):
    unit = (UNITS, BLOCK, width)
    half = (UNITS, BLOCK // 2, width)
    return [
        pltpu.VMEM((7, 4 * BLOCK, 2 * tok_rows), BF16),
        pltpu.VMEM((UNITS, 2 * tok_rows, width), BF16),
        pltpu.VMEM((3, 4 * BLOCK, width), F32),
        pltpu.VMEM(unit, BF16),
        pltpu.VMEM(unit, BF16),
        pltpu.VMEM(unit, BF16),
        pltpu.VMEM(half, BF16),
        pltpu.VMEM(half, BF16),
        pltpu.VMEM(unit, BF16),
        pltpu.VMEM(unit, BF16),
        pltpu.VMEM(unit, F32),
        pltpu.VMEM((2,) + unit, BF16),
        pltpu.VMEM((2,) + unit, BF16),
        pltpu.SemaphoreType.DMA((UNITS, 8)),
        pltpu.SemaphoreType.DMA((UNITS, 8)),
        pltpu.SemaphoreType.DMA((7, 4)),
        pltpu.SemaphoreType.DMA((7, 4)),
        pltpu.SemaphoreType.DMA((UNITS,)),
        pltpu.SemaphoreType.DMA((UNITS,)),
    ]


class Grads:
    def __init__(self, place, scratch):
        self.place = place
        (
            self.left,
            self.right,
            self.partial,
            self.out_d,
            self.out_x,
            self.out_y,
            self.in_dx,
            self.in_dy,
            self.in_x,
            self.in_y,
            self.total,
            self.out_z,
            self.in_z,
            self.send,
            self.recv,
            self.left_send,
            self.left_recv,
            self.right_send,
            self.right_recv,
        ) = scratch
        self.tok_rows = self.left.shape[2] // 2
        half = BLOCK // 2
        self.low, self.high = slice(0, half), slice(half, BLOCK)

    def rows(self, group, j, core):
        shard = 2 * j + core
        if group < 4:
            return pl.ds(pl.multiple_of(4 * BLOCK * shard + BLOCK * group, 32), BLOCK)
        return pl.ds(pl.multiple_of(BLOCK * shard, 32), BLOCK)

    def left_copy(self, group, j, source):
        mine, theirs = self.tok_rows, 2 * self.tok_rows
        return remote(
            source.at[self.rows(group, j, 1 - self.place.core), :],
            self.left.at[group, BLOCK * j : BLOCK * (j + 1), mine:theirs],
            self.left_send.at[group, j],
            self.left_recv.at[group, j],
            self.place.mate,
        )

    def right_copy(self, unit, source):
        return remote(
            source,
            self.right.at[unit, self.tok_rows :, :],
            self.right_send.at[unit],
            self.right_recv.at[unit],
            self.place.mate,
        )

    def give_left(self, group, source):
        for j in range(4):
            self.left_copy(group, j, source).start()
            self.left[group, BLOCK * j : BLOCK * (j + 1), : self.tok_rows] = source[
                self.rows(group, j, self.place.core), :
            ]

    def give_right(self, unit, source, value):
        self.right_copy(unit, source).start()
        self.right[unit, : self.tok_rows, :] = value

    def copy(self, unit, kind):
        place, low, high = self.place, self.low, self.high
        source, target, to = (
            (self.out_d.at[unit, low], self.in_dx.at[unit], place.across),
            (self.out_d.at[unit, high], self.in_dy.at[unit], place.along),
            (self.out_x.at[unit, low], self.in_x.at[unit, low], place.across),
            (self.out_x.at[unit, high], self.in_x.at[unit, high], place.across),
            (self.out_y.at[unit, low], self.in_y.at[unit, low], place.along),
            (self.out_y.at[unit, high], self.in_y.at[unit, high], place.along),
            (self.out_z.at[0, unit], self.in_z.at[0, unit], {"ctx": place.z + 1}),
            (self.out_z.at[1, unit], self.in_z.at[1, unit], {"ctx": place.z - 1}),
        )[kind]
        return remote(source, target, self.send.at[unit, kind], self.recv.at[unit, kind], to)

    def part(self, j):
        return pl.ds(pl.multiple_of(BLOCK * j, 32), BLOCK)

    def multiply(self, unit, left_source, right_source):
        place, low, high = self.place, self.low, self.high
        group, slot = LEFT[unit], unit % 3
        if group not in LEFT[:unit]:
            for j in range(4):
                self.left_copy(group, j, left_source).wait_recv()
        self.right_copy(unit, right_source).wait_recv()
        self.partial[slot] = jnp.dot(
            self.left[group], self.right[unit], preferred_element_type=F32
        )
        self.out_d[unit] = self.partial[slot, self.part(place.j_d), :].astype(BF16)
        x_part = self.partial[slot, self.part(place.j_x), :]
        y_part = self.partial[slot, self.part(place.j_y), :]
        self.out_x[unit, low] = x_part[low].astype(BF16)
        self.out_y[unit, high] = y_part[high].astype(BF16)
        for kind in (0, 1, 2, 5):
            self.copy(unit, kind).start()

    def pass_on(self, unit):
        place, low, high = self.place, self.low, self.high
        slot = unit % 3
        self.copy(unit, 0).wait_recv()
        y_part = self.partial[slot, self.part(place.j_y), :][low]
        self.out_y[unit, low] = (y_part + self.in_dx[unit].astype(F32)).astype(BF16)
        self.copy(unit, 1).wait_recv()
        x_part = self.partial[slot, self.part(place.j_x), :][high]
        self.out_x[unit, high] = (x_part + self.in_dy[unit].astype(F32)).astype(BF16)
        self.copy(unit, 4).start()
        self.copy(unit, 3).start()

    def gather(self, unit):
        slot = unit % 3
        own = self.partial[slot, self.part(self.place.j_own), :]
        for kind in (2, 3, 4, 5):
            self.copy(unit, kind).wait_recv()
        self.total[unit] = own + self.in_x[unit].astype(F32) + self.in_y[unit].astype(F32)

    def hop(self, unit, step):
        place = self.place
        for way, turn in ((0, step), (1, place.z_size - 1 - step)):

            @pl.when(place.z == turn)
            def _():
                value = self.total[unit]
                if step > 0:
                    self.copy(unit, 6 + way).wait_recv()
                    value = value + self.in_z[way, unit].astype(F32)
                self.out_z[way, unit] = value.astype(BF16)
                self.copy(unit, 6 + way).start()

    def finish(self, unit, store):
        place = self.place
        last = place.z_size - 1

        @pl.when(place.z == last)
        def _():
            self.copy(unit, 6).wait_recv()
            store(self.total[unit] + self.in_z[0, unit].astype(F32))

        @pl.when(place.z == 0)
        def _():
            self.copy(unit, 7).wait_recv()
            store(self.total[unit] + self.in_z[1, unit].astype(F32))

        @pl.when((place.z > 0) * (place.z < last) == 1)
        def _():
            store(
                self.total[unit]
                + self.in_z[0, unit].astype(F32)
                + self.in_z[1, unit].astype(F32)
            )

    def drain(self, lefts, rights):
        place = self.place
        for unit in range(UNITS):
            for kind in range(6):
                self.copy(unit, kind).wait_send()
            self.right_copy(unit, rights[unit]).wait_send()

        @pl.when(place.z < place.z_size - 1)
        def _():
            for unit in range(UNITS):
                self.copy(unit, 6).wait_send()

        @pl.when(place.z > 0)
        def _():
            for unit in range(UNITS):
                self.copy(unit, 7).wait_send()

        for group in range(7):
            for j in range(4):
                self.left_copy(group, j, lefts[group]).wait_send()


def grad_kernel(
    z_size,
    act_t,
    normed_t,
    context_t,
    packed_t,
    g_ffn,
    g_pre,
    g_branch,
    g_query,
    g_key,
    g_value,
    d_query,
    d_key,
    d_value,
    d_out,
    d_up,
    d_down,
    *scratch,
):
    place = Place(z_size)
    greet(place)
    grads = Grads(place, scratch)
    lefts = (act_t,) * 4 + (normed_t, context_t, packed_t)
    width = packed_t.shape[0]
    columns = [slice(width * i, width * (i + 1)) for i in range(4)]
    rights = (
        [g_ffn] * 4
        + [g_pre.at[:, part] for part in columns]
        + [g_branch, g_query, g_key, g_value]
    )

    def store(unit, value):
        if unit < 4:
            d_down[BLOCK * unit : BLOCK * (unit + 1), :] = value
        elif unit < 8:
            d_up[:, columns[unit - 4]] = value
        else:
            (d_out, d_query, d_key, d_value)[unit - 8][...] = value

    for unit in range(UNITS):
        if LEFT[unit] not in LEFT[:unit]:
            grads.give_left(LEFT[unit], lefts[LEFT[unit]])
        grads.give_right(unit, rights[unit], rights[unit][...])
    hops = z_size - 1
    for tick in range(UNITS + 3 + hops):
        if tick < UNITS:
            unit = tick
            grads.multiply(unit, lefts[LEFT[unit]], rights[unit])
        if 0 <= tick - 1 < UNITS:
            grads.pass_on(tick - 1)
        if 0 <= tick - 2 < UNITS:
            grads.gather(tick - 2)
        for step in range(hops):
            unit = tick - 2 - step
            if 0 <= unit < UNITS:
                grads.hop(unit, step)
        unit = tick - 2 - hops
        if 0 <= unit < UNITS:
            grads.finish(unit, partial(store, unit))
    grads.drain(lefts, rights)


def weight_grads(z_size, *sources):
    act_t, _, _, packed_t = sources[:4]
    width, tok_rows = packed_t.shape
    hidden = act_t.shape[0]
    shard = width // 8
    square = jax.ShapeDtypeStruct((shard, width), F32)
    vmem = pl.BlockSpec(memory_space=pltpu.VMEM)
    return pl.pallas_call(
        partial(grad_kernel, z_size),
        out_shape=(
            square,
            square,
            square,
            square,
            jax.ShapeDtypeStruct((shard, hidden), F32),
            jax.ShapeDtypeStruct((hidden // 8, width), F32),
        ),
        in_specs=[vmem] * len(sources),
        out_specs=(vmem,) * 6,
        scratch_shapes=grad_scratch(tok_rows, width),
        compiler_params=pltpu.CompilerParams(
            collective_id=1, has_side_effects=True, vmem_limit_bytes=62 * 2**20
        ),
        name="weight_grads",
    )(*sources)


HEADS = 12


norm_eps = 1e-12
floor_score = -1e30
masked_score = -1e32


def product(left, right):
    return jnp.dot(left, right, preferred_element_type=jnp.float32)


def inner_rows(left, right):
    return lax.dot_general(
        left, right, (((0,), (0,)), ((), ())), preferred_element_type=jnp.float32
    )


def against(left, right):
    return lax.dot_general(
        left, right, (((1,), (1,)), ((), ())), preferred_element_type=jnp.float32
    )


def layer_norm(value, gain, shift):
    centre = value - jnp.mean(value, -1, keepdims=True)
    spread = jnp.mean(centre * centre, -1, keepdims=True)
    inverse_dev = lax.rsqrt(spread + norm_eps)
    scaled = centre * inverse_dev
    return (scaled * gain + shift, scaled, inverse_dev)


def norm_back(grad_norm, scaled, inverse_dev, gain):
    grad_scaled = grad_norm * gain
    centred = grad_scaled - jnp.mean(grad_scaled, -1, keepdims=True)
    return inverse_dev * (centred - scaled * jnp.mean(grad_scaled * scaled, -1, keepdims=True))


def per_device(
    tokens,
    cotangent,
    token_order,
    sequence_ids,
    valid,
    teacher,
    w_query,
    b_query,
    w_key,
    w_value,
    b_value,
    w_out,
    b_out,
    norm1_gain,
    norm1_bias,
    w_up,
    b_up,
    w_down,
    b_down,
    norm2_gain,
    norm2_bias,
):
    tok_rows, model_width = tokens.shape
    peer_count = lax.axis_size(("dp", "ctx"))
    per_peer = tok_rows // peer_count
    head_count = HEADS
    head_size = model_width // head_count
    score_scale = head_size ** (-0.5)
    gelu_exact = partial(jax.nn.gelu, approximate=False)
    positions = lax.iota(jnp.int32, tok_rows)
    source = token_order // tok_rows
    slot_sort = jnp.argsort(source * tok_rows + positions)
    requests = (token_order[slot_sort] % tok_rows).reshape(peer_count, per_peer)
    wanted = lax.all_to_all(requests, ("dp", "ctx"), split_axis=0, concat_axis=0, tiled=True)
    wanted_flat = wanted.reshape(tok_rows)
    packed_x, packed_cot = (
        lax.all_to_all(
            tokens[wanted_flat].reshape(peer_count, per_peer, model_width),
            ("dp", "ctx"),
            split_axis=0,
            concat_axis=0,
            tiled=True,
        ),
        lax.all_to_all(
            cotangent[wanted_flat].reshape(peer_count, per_peer, model_width),
            ("dp", "ctx"),
            split_axis=0,
            concat_axis=0,
            tiled=True,
        ),
    )
    arrival = jnp.argsort(slot_sort)
    inputs = packed_x.reshape(tok_rows, model_width)[arrival]
    cot_rows = packed_cot.reshape(tok_rows, model_width)[arrival].astype(jnp.float32)
    valid_rows = valid.astype(jnp.float32)
    valid_count = lax.psum(jnp.sum(valid_rows), ("dp", "ctx"))
    (
        query_weight,
        query_bias,
        key_weight,
        value_weight,
        value_bias,
        out_weight,
        out_bias,
        gain_one,
        shift_one,
        up_weight,
        up_bias,
        down_weight,
        down_bias,
        gain_two,
        shift_two,
    ) = (
        lax.all_gather(w_query, "dp", axis=0, tiled=True),
        lax.all_gather(b_query, "dp", axis=0, tiled=True),
        lax.all_gather(w_key, "dp", axis=0, tiled=True),
        lax.all_gather(w_value, "dp", axis=0, tiled=True),
        lax.all_gather(b_value, "dp", axis=0, tiled=True),
        lax.all_gather(w_out, "dp", axis=0, tiled=True),
        lax.all_gather(b_out, "dp", axis=0, tiled=True),
        lax.all_gather(norm1_gain, "dp", axis=0, tiled=True),
        lax.all_gather(norm1_bias, "dp", axis=0, tiled=True),
        lax.all_gather(w_up, "dp", axis=0, tiled=True),
        lax.all_gather(b_up, "dp", axis=0, tiled=True),
        lax.all_gather(w_down, "dp", axis=0, tiled=True),
        lax.all_gather(b_down, "dp", axis=0, tiled=True),
        lax.all_gather(norm2_gain, "dp", axis=0, tiled=True),
        lax.all_gather(norm2_bias, "dp", axis=0, tiled=True),
    )
    queries = (product(inputs, query_weight) + query_bias).astype(jnp.bfloat16)
    key_rows = product(inputs, key_weight).astype(jnp.bfloat16)
    values = (product(inputs, value_weight) + value_bias).astype(jnp.bfloat16)
    group_ids = sequence_ids.reshape(-1)
    cycle_index = lax.axis_index("ctx")
    query_ids = lax.dynamic_slice_in_dim(group_ids, cycle_index * tok_rows, tok_rows)
    query_heads = queries.reshape(tok_rows, head_count, head_size)
    initial = (
        jnp.full((head_count, tok_rows), floor_score, jnp.float32),
        jnp.zeros((head_count, tok_rows), jnp.float32),
        jnp.zeros((tok_rows, head_count, head_size), jnp.float32),
    )
    folded = initial
    key_piece = lax.all_gather(key_rows, "ctx", axis=0, tiled=True)
    value_piece = lax.all_gather(values, "ctx", axis=0, tiled=True)
    length = key_piece.shape[0]
    attend_block_rows = math.gcd(length, 512)
    block_count = length // attend_block_rows

    def one_block(carried, inputs_block):
        running_max, running_sum, summed = carried
        key_block, value_block, key_start = inputs_block
        key_ids = lax.dynamic_slice_in_dim(group_ids, key_start, attend_block_rows)
        scores = (
            jnp.einsum("qhd,khd->hqk", query_heads, key_block, preferred_element_type=jnp.float32)
            * score_scale
        )
        scores = jnp.where((query_ids[:, None] == key_ids[None, :])[None], scores, masked_score)
        new_max = jnp.maximum(running_max, jnp.max(scores, -1))
        factor = jnp.exp(running_max - new_max)
        weights = jnp.exp(scores - new_max[:, :, None])
        running_sum = running_sum * factor + jnp.sum(weights, -1)
        update = jnp.einsum(
            "hqk,khd->qhd",
            weights.astype(jnp.bfloat16),
            value_block,
            preferred_element_type=jnp.float32,
        )
        summed = summed * jnp.transpose(factor)[:, :, None] + update
        return ((new_max, running_sum, summed), None)

    key_starts = attend_block_rows * lax.iota(jnp.int32, block_count)
    folded, _ = lax.scan(
        one_block,
        folded,
        (
            key_piece.reshape(block_count, attend_block_rows, head_count, head_size),
            value_piece.reshape(block_count, attend_block_rows, head_count, head_size),
            key_starts,
        ),
    )
    running_max, running_sum, summed = folded
    attended = summed / jnp.transpose(running_sum)[:, :, None]
    log_total = running_max + jnp.log(running_sum)
    context = attended.reshape(tok_rows, model_width).astype(jnp.bfloat16)
    branch = product(context, out_weight) + out_bias
    normed, scaled_one, inverse_one = layer_norm(
        inputs.astype(jnp.float32) + branch, gain_one, shift_one
    )
    normed_low = normed.astype(jnp.bfloat16)
    pre_act = product(normed_low, up_weight) + up_bias
    activated = gelu_exact(pre_act).astype(jnp.bfloat16)
    ffn_out = product(activated, down_weight) + down_bias
    result, scaled_two, inverse_two = layer_norm(normed + ffn_out, gain_two, shift_two)
    difference = result - teacher
    loss_total = lax.psum(jnp.sum(valid_rows[:, None] * difference * difference), ("dp", "ctx"))
    loss_value = loss_total / (valid_count * model_width)
    grad_out = cot_rows + 2.0 / (valid_count * model_width) * valid_rows[:, None] * difference
    grad_gain_two = jnp.sum(grad_out * scaled_two, 0)
    grad_shift_two = jnp.sum(grad_out, 0)
    grad_res_two = norm_back(grad_out, scaled_two, inverse_two, gain_two)
    grad_ffn = grad_res_two.astype(jnp.bfloat16)
    grad_down = inner_rows(activated, grad_ffn)
    grad_down_bias = jnp.sum(grad_ffn.astype(jnp.float32), 0)
    grad_act = against(grad_ffn, down_weight)
    _, gelu_pull = jax.vjp(gelu_exact, pre_act)
    grad_pre = gelu_pull(grad_act)[0].astype(jnp.bfloat16)
    grad_up = inner_rows(normed_low, grad_pre)
    grad_up_bias = jnp.sum(grad_pre.astype(jnp.float32), 0)
    grad_normed = grad_res_two + against(grad_pre, up_weight)
    ffn_shards = (
        lax.psum_scatter(
            grad_up.astype(jnp.bfloat16), "dp", scatter_dimension=0, tiled=True
        ).astype(jnp.float32),
        lax.psum_scatter(
            grad_up_bias.astype(jnp.bfloat16), "dp", scatter_dimension=0, tiled=True
        ).astype(jnp.float32),
        lax.psum_scatter(
            grad_down.astype(jnp.bfloat16), "dp", scatter_dimension=0, tiled=True
        ).astype(jnp.float32),
        lax.psum_scatter(
            grad_down_bias.astype(jnp.bfloat16), "dp", scatter_dimension=0, tiled=True
        ).astype(jnp.float32),
        lax.psum_scatter(
            grad_gain_two.astype(jnp.bfloat16), "dp", scatter_dimension=0, tiled=True
        ).astype(jnp.float32),
        lax.psum_scatter(
            grad_shift_two.astype(jnp.bfloat16), "dp", scatter_dimension=0, tiled=True
        ).astype(jnp.float32),
    )
    grad_gain_one = jnp.sum(grad_normed * scaled_one, 0)
    grad_shift_one = jnp.sum(grad_normed, 0)
    grad_res_one = norm_back(grad_normed, scaled_one, inverse_one, gain_one)
    grad_branch = grad_res_one.astype(jnp.bfloat16)
    grad_out_w = inner_rows(context, grad_branch)
    grad_out_bias = jnp.sum(grad_branch.astype(jnp.float32), 0)
    grad_context = against(grad_branch, out_weight).astype(jnp.bfloat16)
    grad_heads = grad_context.reshape(tok_rows, head_count, head_size)
    delta = jnp.transpose(jnp.sum(grad_heads.astype(jnp.float32) * attended, -1))
    all_keys, all_values = (
        lax.all_gather(key_rows, "ctx", axis=0, tiled=True),
        lax.all_gather(values, "ctx", axis=0, tiled=True),
    )
    group_len = all_keys.shape[0]
    block_rows = math.gcd(group_len, 512)
    block_count = group_len // block_rows
    key_starts = block_rows * lax.iota(jnp.int32, block_count)
    key_blocks = all_keys.reshape(block_count, block_rows, head_count, head_size)
    value_blocks = all_values.reshape(block_count, block_rows, head_count, head_size)

    def query_side(key_block, value_block, key_start):
        key_ids = lax.dynamic_slice_in_dim(group_ids, key_start, block_rows)
        scores = (
            jnp.einsum("qhd,khd->hqk", query_heads, key_block, preferred_element_type=jnp.float32)
            * score_scale
        )
        scores = jnp.where((query_ids[:, None] == key_ids[None, :])[None], scores, masked_score)
        probs = jnp.exp(scores - log_total[:, :, None])
        grad_probs = jnp.einsum(
            "qhd,khd->hqk", grad_heads, value_block, preferred_element_type=jnp.float32
        )
        grad_scores = (probs * (grad_probs - delta[:, :, None])).astype(jnp.bfloat16)
        return (probs, grad_scores)

    def back_block(grad_query, inputs_block):
        key_block, value_block, key_start = inputs_block
        probs, grad_scores = query_side(key_block, value_block, key_start)
        grad_query = (
            grad_query
            + jnp.einsum("hqk,khd->qhd", grad_scores, key_block, preferred_element_type=jnp.float32)
            * score_scale
        )
        grad_key = (
            jnp.einsum("hqk,qhd->khd", grad_scores, query_heads, preferred_element_type=jnp.float32)
            * score_scale
        )
        grad_value = jnp.einsum(
            "hqk,qhd->khd",
            probs.astype(jnp.bfloat16),
            grad_heads,
            preferred_element_type=jnp.float32,
        )
        return (grad_query, (grad_key, grad_value))

    grad_query, (key_parts, value_parts) = lax.scan(
        back_block,
        jnp.zeros((tok_rows, head_count, head_size), jnp.float32),
        (key_blocks, value_blocks, key_starts),
    )
    key_total, value_total = (
        lax.psum_scatter(
            key_parts.reshape(group_len, model_width).astype(jnp.bfloat16),
            "ctx",
            scatter_dimension=0,
            tiled=True,
        ).astype(jnp.float32),
        lax.psum_scatter(
            value_parts.reshape(group_len, model_width).astype(jnp.bfloat16),
            "ctx",
            scatter_dimension=0,
            tiled=True,
        ).astype(jnp.float32),
    )
    grad_keys = key_total.astype(jnp.bfloat16)
    grad_values = value_total.astype(jnp.bfloat16)
    grad_queries = grad_query.reshape(tok_rows, model_width).astype(jnp.bfloat16)
    grad_query_w = inner_rows(inputs, grad_queries)
    grad_query_bias = jnp.sum(grad_queries.astype(jnp.float32), 0)
    grad_key_w = inner_rows(inputs, grad_keys)
    grad_value_w = inner_rows(inputs, grad_values)
    grad_value_bias = jnp.sum(grad_values.astype(jnp.float32), 0)
    grad_inputs = (
        grad_res_one
        + against(grad_queries, query_weight)
        + against(grad_keys, key_weight)
        + against(grad_values, value_weight)
    )
    attn_shards = (
        lax.psum_scatter(
            grad_query_w.astype(jnp.bfloat16), "dp", scatter_dimension=0, tiled=True
        ).astype(jnp.float32),
        lax.psum_scatter(
            grad_query_bias.astype(jnp.bfloat16), "dp", scatter_dimension=0, tiled=True
        ).astype(jnp.float32),
        lax.psum_scatter(
            grad_key_w.astype(jnp.bfloat16), "dp", scatter_dimension=0, tiled=True
        ).astype(jnp.float32),
        lax.psum_scatter(
            grad_value_w.astype(jnp.bfloat16), "dp", scatter_dimension=0, tiled=True
        ).astype(jnp.float32),
        lax.psum_scatter(
            grad_value_bias.astype(jnp.bfloat16), "dp", scatter_dimension=0, tiled=True
        ).astype(jnp.float32),
        lax.psum_scatter(
            grad_out_w.astype(jnp.bfloat16), "dp", scatter_dimension=0, tiled=True
        ).astype(jnp.float32),
        lax.psum_scatter(
            grad_out_bias.astype(jnp.bfloat16), "dp", scatter_dimension=0, tiled=True
        ).astype(jnp.float32),
        lax.psum_scatter(
            grad_gain_one.astype(jnp.bfloat16), "dp", scatter_dimension=0, tiled=True
        ).astype(jnp.float32),
        lax.psum_scatter(
            grad_shift_one.astype(jnp.bfloat16), "dp", scatter_dimension=0, tiled=True
        ).astype(jnp.float32),
    )
    totals = (
        lax.psum(attn_shards[0].astype(jnp.bfloat16), "ctx").astype(jnp.float32),
        lax.psum(attn_shards[1].astype(jnp.bfloat16), "ctx").astype(jnp.float32),
        lax.psum(attn_shards[2].astype(jnp.bfloat16), "ctx").astype(jnp.float32),
        lax.psum(attn_shards[3].astype(jnp.bfloat16), "ctx").astype(jnp.float32),
        lax.psum(attn_shards[4].astype(jnp.bfloat16), "ctx").astype(jnp.float32),
        lax.psum(attn_shards[5].astype(jnp.bfloat16), "ctx").astype(jnp.float32),
        lax.psum(attn_shards[6].astype(jnp.bfloat16), "ctx").astype(jnp.float32),
        lax.psum(attn_shards[7].astype(jnp.bfloat16), "ctx").astype(jnp.float32),
        lax.psum(attn_shards[8].astype(jnp.bfloat16), "ctx").astype(jnp.float32),
        lax.psum(ffn_shards[0].astype(jnp.bfloat16), "ctx").astype(jnp.float32),
        lax.psum(ffn_shards[1].astype(jnp.bfloat16), "ctx").astype(jnp.float32),
        lax.psum(ffn_shards[2].astype(jnp.bfloat16), "ctx").astype(jnp.float32),
        lax.psum(ffn_shards[3].astype(jnp.bfloat16), "ctx").astype(jnp.float32),
        lax.psum(ffn_shards[4].astype(jnp.bfloat16), "ctx").astype(jnp.float32),
        lax.psum(ffn_shards[5].astype(jnp.bfloat16), "ctx").astype(jnp.float32),
    )
    back_out, back_grad = (
        lax.all_to_all(
            result[slot_sort].reshape(peer_count, per_peer, model_width).astype(jnp.bfloat16),
            ("dp", "ctx"),
            split_axis=0,
            concat_axis=0,
            tiled=True,
        ).astype(jnp.float32),
        lax.all_to_all(
            grad_inputs[slot_sort].reshape(peer_count, per_peer, model_width).astype(jnp.bfloat16),
            ("dp", "ctx"),
            split_axis=0,
            concat_axis=0,
            tiled=True,
        ).astype(jnp.float32),
    )
    homeward = jnp.argsort(wanted_flat)
    output = back_out.reshape(tok_rows, model_width)[homeward]
    input_grad = back_grad.reshape(tok_rows, model_width)[homeward]
    return (
        output,
        loss_value,
        input_grad,
        totals[0],
        totals[1],
        totals[2],
        totals[3],
        totals[4],
        totals[5],
        totals[6],
        totals[7],
        totals[8],
        totals[9],
        totals[10],
        totals[11],
        totals[12],
        totals[13],
        totals[14],
    )


def per_device_fast(
    tokens,
    cotangent,
    token_order,
    sequence_ids,
    valid,
    teacher,
    w_query,
    b_query,
    w_key,
    w_value,
    b_value,
    w_out,
    b_out,
    norm1_gain,
    norm1_bias,
    w_up,
    b_up,
    w_down,
    b_down,
    norm2_gain,
    norm2_bias,
):
    tok_rows, model_width = tokens.shape
    peer_count = lax.axis_size(("dp", "ctx"))
    per_peer = tok_rows // peer_count
    head_count = HEADS
    head_size = model_width // head_count
    score_scale = head_size ** (-0.5)
    gelu_exact = partial(jax.nn.gelu, approximate=False)
    positions = lax.iota(jnp.int32, tok_rows)
    source = token_order // tok_rows
    slot_sort = jnp.argsort(source * tok_rows + positions)
    requests = (token_order[slot_sort] % tok_rows).reshape(peer_count, per_peer)
    wanted = lax.all_to_all(requests, ("dp", "ctx"), split_axis=0, concat_axis=0, tiled=True)
    wanted_flat = wanted.reshape(tok_rows)
    packed_x, packed_cot = (
        lax.all_to_all(
            tokens[wanted_flat].reshape(peer_count, per_peer, model_width),
            ("dp", "ctx"),
            split_axis=0,
            concat_axis=0,
            tiled=True,
        ),
        lax.all_to_all(
            cotangent[wanted_flat].reshape(peer_count, per_peer, model_width),
            ("dp", "ctx"),
            split_axis=0,
            concat_axis=0,
            tiled=True,
        ),
    )
    arrival = jnp.argsort(slot_sort)
    inputs = packed_x.reshape(tok_rows, model_width)[arrival]
    cot_rows = packed_cot.reshape(tok_rows, model_width)[arrival].astype(jnp.float32)
    valid_rows = valid.astype(jnp.float32)
    valid_count = lax.psum(jnp.sum(valid_rows), ("dp", "ctx"))
    (
        query_weight,
        query_bias,
        key_weight,
        value_weight,
        value_bias,
        out_weight,
        out_bias,
        gain_one,
        shift_one,
        up_weight,
        up_bias,
        down_weight,
        down_bias,
        gain_two,
        shift_two,
    ) = (
        lax.all_gather(w_query, "dp", axis=0, tiled=True),
        lax.all_gather(b_query, "dp", axis=0, tiled=True),
        lax.all_gather(w_key, "dp", axis=0, tiled=True),
        lax.all_gather(w_value, "dp", axis=0, tiled=True),
        lax.all_gather(b_value, "dp", axis=0, tiled=True),
        lax.all_gather(w_out, "dp", axis=0, tiled=True),
        lax.all_gather(b_out, "dp", axis=0, tiled=True),
        lax.all_gather(norm1_gain, "dp", axis=0, tiled=True),
        lax.all_gather(norm1_bias, "dp", axis=0, tiled=True),
        lax.all_gather(w_up, "dp", axis=0, tiled=True),
        lax.all_gather(b_up, "dp", axis=0, tiled=True),
        lax.all_gather(w_down, "dp", axis=0, tiled=True),
        lax.all_gather(b_down, "dp", axis=0, tiled=True),
        lax.all_gather(norm2_gain, "dp", axis=0, tiled=True),
        lax.all_gather(norm2_bias, "dp", axis=0, tiled=True),
    )
    queries = (product(inputs, query_weight) + query_bias).astype(jnp.bfloat16)
    key_rows = product(inputs, key_weight).astype(jnp.bfloat16)
    values = (product(inputs, value_weight) + value_bias).astype(jnp.bfloat16)
    group_ids = sequence_ids.reshape(-1)
    cycle_index = lax.axis_index("ctx")
    query_ids = lax.dynamic_slice_in_dim(group_ids, cycle_index * tok_rows, tok_rows)
    query_heads = queries.reshape(tok_rows, head_count, head_size)
    initial = (
        jnp.full((head_count, tok_rows), floor_score, jnp.float32),
        jnp.zeros((head_count, tok_rows), jnp.float32),
        jnp.zeros((tok_rows, head_count, head_size), jnp.float32),
    )
    folded = initial
    key_piece = lax.all_gather(key_rows, "ctx", axis=0, tiled=True)
    value_piece = lax.all_gather(values, "ctx", axis=0, tiled=True)
    length = key_piece.shape[0]
    attend_block_rows = math.gcd(length, 512)
    block_count = length // attend_block_rows

    def one_block(carried, inputs_block):
        running_max, running_sum, summed = carried
        key_block, value_block, key_start = inputs_block
        key_ids = lax.dynamic_slice_in_dim(group_ids, key_start, attend_block_rows)
        scores = (
            jnp.einsum("qhd,khd->hqk", query_heads, key_block, preferred_element_type=jnp.float32)
            * score_scale
        )
        scores = jnp.where((query_ids[:, None] == key_ids[None, :])[None], scores, masked_score)
        new_max = jnp.maximum(running_max, jnp.max(scores, -1))
        factor = jnp.exp(running_max - new_max)
        weights = jnp.exp(scores - new_max[:, :, None])
        running_sum = running_sum * factor + jnp.sum(weights, -1)
        update = jnp.einsum(
            "hqk,khd->qhd",
            weights.astype(jnp.bfloat16),
            value_block,
            preferred_element_type=jnp.float32,
        )
        summed = summed * jnp.transpose(factor)[:, :, None] + update
        return ((new_max, running_sum, summed), None)

    key_starts = attend_block_rows * lax.iota(jnp.int32, block_count)
    folded, _ = lax.scan(
        one_block,
        folded,
        (
            key_piece.reshape(block_count, attend_block_rows, head_count, head_size),
            value_piece.reshape(block_count, attend_block_rows, head_count, head_size),
            key_starts,
        ),
    )
    running_max, running_sum, summed = folded
    attended = summed / jnp.transpose(running_sum)[:, :, None]
    log_total = running_max + jnp.log(running_sum)
    context = attended.reshape(tok_rows, model_width).astype(jnp.bfloat16)
    branch = product(context, out_weight) + out_bias
    normed, scaled_one, inverse_one = layer_norm(
        inputs.astype(jnp.float32) + branch, gain_one, shift_one
    )
    normed_low = normed.astype(jnp.bfloat16)
    pre_act = product(normed_low, up_weight) + up_bias
    activated = gelu_exact(pre_act).astype(jnp.bfloat16)
    ffn_out = product(activated, down_weight) + down_bias
    result, scaled_two, inverse_two = layer_norm(normed + ffn_out, gain_two, shift_two)
    difference = result - teacher
    loss_total = lax.psum(jnp.sum(valid_rows[:, None] * difference * difference), ("dp", "ctx"))
    loss_value = loss_total / (valid_count * model_width)
    grad_out = cot_rows + 2.0 / (valid_count * model_width) * valid_rows[:, None] * difference
    grad_gain_two = jnp.sum(grad_out * scaled_two, 0)
    grad_shift_two = jnp.sum(grad_out, 0)
    grad_res_two = norm_back(grad_out, scaled_two, inverse_two, gain_two)
    grad_ffn = grad_res_two.astype(jnp.bfloat16)
    grad_down_bias = jnp.sum(grad_ffn.astype(jnp.float32), 0)
    grad_act = against(grad_ffn, down_weight)
    _, gelu_pull = jax.vjp(gelu_exact, pre_act)
    grad_pre = gelu_pull(grad_act)[0].astype(jnp.bfloat16)
    grad_up_bias = jnp.sum(grad_pre.astype(jnp.float32), 0)
    grad_normed = grad_res_two + against(grad_pre, up_weight)
    grad_gain_one = jnp.sum(grad_normed * scaled_one, 0)
    grad_shift_one = jnp.sum(grad_normed, 0)
    grad_res_one = norm_back(grad_normed, scaled_one, inverse_one, gain_one)
    grad_branch = grad_res_one.astype(jnp.bfloat16)
    grad_out_bias = jnp.sum(grad_branch.astype(jnp.float32), 0)
    grad_context = against(grad_branch, out_weight).astype(jnp.bfloat16)
    grad_heads = grad_context.reshape(tok_rows, head_count, head_size)
    delta = jnp.transpose(jnp.sum(grad_heads.astype(jnp.float32) * attended, -1))
    all_keys, all_values = (
        lax.all_gather(key_rows, "ctx", axis=0, tiled=True),
        lax.all_gather(values, "ctx", axis=0, tiled=True),
    )
    group_len = all_keys.shape[0]
    block_rows = math.gcd(group_len, 512)
    block_count = group_len // block_rows
    key_starts = block_rows * lax.iota(jnp.int32, block_count)
    key_blocks = all_keys.reshape(block_count, block_rows, head_count, head_size)
    value_blocks = all_values.reshape(block_count, block_rows, head_count, head_size)

    def query_side(key_block, value_block, key_start):
        key_ids = lax.dynamic_slice_in_dim(group_ids, key_start, block_rows)
        scores = (
            jnp.einsum("qhd,khd->hqk", query_heads, key_block, preferred_element_type=jnp.float32)
            * score_scale
        )
        scores = jnp.where((query_ids[:, None] == key_ids[None, :])[None], scores, masked_score)
        probs = jnp.exp(scores - log_total[:, :, None])
        grad_probs = jnp.einsum(
            "qhd,khd->hqk", grad_heads, value_block, preferred_element_type=jnp.float32
        )
        grad_scores = (probs * (grad_probs - delta[:, :, None])).astype(jnp.bfloat16)
        return (probs, grad_scores)

    def back_block(grad_query, inputs_block):
        key_block, value_block, key_start = inputs_block
        probs, grad_scores = query_side(key_block, value_block, key_start)
        grad_query = (
            grad_query
            + jnp.einsum("hqk,khd->qhd", grad_scores, key_block, preferred_element_type=jnp.float32)
            * score_scale
        )
        grad_key = (
            jnp.einsum("hqk,qhd->khd", grad_scores, query_heads, preferred_element_type=jnp.float32)
            * score_scale
        )
        grad_value = jnp.einsum(
            "hqk,qhd->khd",
            probs.astype(jnp.bfloat16),
            grad_heads,
            preferred_element_type=jnp.float32,
        )
        return (grad_query, (grad_key, grad_value))

    grad_query, (key_parts, value_parts) = lax.scan(
        back_block,
        jnp.zeros((tok_rows, head_count, head_size), jnp.float32),
        (key_blocks, value_blocks, key_starts),
    )
    key_total, value_total = (
        lax.psum_scatter(
            key_parts.reshape(group_len, model_width).astype(jnp.bfloat16),
            "ctx",
            scatter_dimension=0,
            tiled=True,
        ).astype(jnp.float32),
        lax.psum_scatter(
            value_parts.reshape(group_len, model_width).astype(jnp.bfloat16),
            "ctx",
            scatter_dimension=0,
            tiled=True,
        ).astype(jnp.float32),
    )
    grad_keys = key_total.astype(jnp.bfloat16)
    grad_values = value_total.astype(jnp.bfloat16)
    grad_queries = grad_query.reshape(tok_rows, model_width).astype(jnp.bfloat16)
    grad_query_bias = jnp.sum(grad_queries.astype(jnp.float32), 0)
    grad_value_bias = jnp.sum(grad_values.astype(jnp.float32), 0)
    grad_inputs = (
        grad_res_one
        + against(grad_queries, query_weight)
        + against(grad_keys, key_weight)
        + against(grad_values, value_weight)
    )
    grad_query_w, grad_key_w, grad_value_w, grad_out_w, grad_up, grad_down = weight_grads(
        lax.axis_size("ctx"),
        activated.T,
        normed_low.T,
        context.T,
        inputs.T,
        grad_ffn,
        grad_pre,
        grad_branch,
        grad_queries,
        grad_keys,
        grad_values,
    )
    small = jnp.stack(
        [
            grad_query_bias,
            grad_value_bias,
            grad_out_bias,
            grad_gain_one,
            grad_shift_one,
            grad_down_bias,
            grad_gain_two,
            grad_shift_two,
        ]
        + list(grad_up_bias.reshape(4, model_width))
    )
    small = lax.psum(small, ("dp", "ctx"))
    shard = model_width // 8
    dp_index = lax.axis_index("dp")
    own = lax.dynamic_slice_in_dim(small[:8], dp_index * shard, shard, axis=1)
    own_up = lax.dynamic_slice_in_dim(small[8:].reshape(-1), dp_index * 4 * shard, 4 * shard)
    totals = (
        grad_query_w,
        own[0],
        grad_key_w,
        grad_value_w,
        own[1],
        grad_out_w,
        own[2],
        own[3],
        own[4],
        grad_up,
        own_up,
        grad_down,
        own[5],
        own[6],
        own[7],
    )
    back_out, back_grad = (
        lax.all_to_all(
            result[slot_sort].reshape(peer_count, per_peer, model_width).astype(jnp.bfloat16),
            ("dp", "ctx"),
            split_axis=0,
            concat_axis=0,
            tiled=True,
        ).astype(jnp.float32),
        lax.all_to_all(
            grad_inputs[slot_sort].reshape(peer_count, per_peer, model_width).astype(jnp.bfloat16),
            ("dp", "ctx"),
            split_axis=0,
            concat_axis=0,
            tiled=True,
        ).astype(jnp.float32),
    )
    homeward = jnp.argsort(wanted_flat)
    output = back_out.reshape(tok_rows, model_width)[homeward]
    input_grad = back_grad.reshape(tok_rows, model_width)[homeward]
    return (
        output,
        loss_value,
        input_grad,
        totals[0],
        totals[1],
        totals[2],
        totals[3],
        totals[4],
        totals[5],
        totals[6],
        totals[7],
        totals[8],
        totals[9],
        totals[10],
        totals[11],
        totals[12],
        totals[13],
        totals[14],
    )


def solution(mesh):
    in_specs = (
        P(("dp", "ctx"), None),
        P(("dp", "ctx"), None),
        P(("dp", "ctx")),
        P("dp", None),
        P(("dp", "ctx")),
        P(("dp", "ctx"), None),
        P("dp", None),
        P("dp"),
        P("dp", None),
        P("dp", None),
        P("dp"),
        P("dp", None),
        P("dp"),
        P("dp"),
        P("dp"),
        P("dp", None),
        P("dp"),
        P("dp", None),
        P("dp"),
        P("dp"),
        P("dp"),
    )
    out_specs = (
        P(("dp", "ctx"), None),
        P(),
        P(("dp", "ctx"), None),
        P("dp", None),
        P("dp"),
        P("dp", None),
        P("dp", None),
        P("dp"),
        P("dp", None),
        P("dp"),
        P("dp"),
        P("dp"),
        P("dp", None),
        P("dp"),
        P("dp", None),
        P("dp"),
        P("dp"),
        P("dp"),
    )
    fast = dict(mesh.shape) == {"dp": 8, "ctx": 4}
    return jax.shard_map(
        per_device_fast if fast else per_device, mesh=mesh, in_specs=in_specs, out_specs=out_specs, check_vma=False
    )
```

```python
import math
from functools import partial
from types import SimpleNamespace
from typing import NamedTuple

import jax
import jax.numpy as jnp
from jax import lax
from jax.experimental import pallas as pl
from jax.experimental.pallas import tpu as pltpu
from jax.sharding import PartitionSpec as P

MESH = pl.DeviceIdType.MESH
F32, BF16 = jnp.float32, jnp.bfloat16


class Place:
    def __init__(self, z_size):
        dp, z = lax.axis_index("dp"), lax.axis_index("ctx")
        self.dp, self.z, self.z_size = dp, z, z_size
        core, x, y = dp % 2, dp // 2 % 2, dp // 4
        self.core = core
        self.mate = {"dp": dp + 1 - 2 * core}
        self.across = {"dp": dp + 2 - 4 * x}
        self.along = {"dp": dp + 4 - 8 * y}
        self.j_own = y * 2 + x
        self.j_x = y * 2 + 1 - x
        self.j_y = (1 - y) * 2 + x
        self.j_d = (1 - y) * 2 + 1 - x


def remote(src, dst, send, recv, to):
    return pltpu.make_async_remote_copy(
        src_ref=src, dst_ref=dst, send_sem=send, recv_sem=recv, device_id=to, device_id_type=MESH
    )


UNITS = 12
BLOCK = 96


class Route:
    def __init__(self, z_size):
        place = Place(z_size)
        self.place = place
        dp, z, core = place.dp, place.z, place.core
        self.blocks = 8 * z_size
        self.home = dp * z_size + z
        self.group_core = z // 2
        self.quarter = 2 * (z % 2) + core
        self.block = (dp - core + self.group_core) * z_size + self.quarter
        self.mate_quarter = self.quarter + 1 - 2 * core
        self.pair_quarter = self.quarter + 2 - 4 * (z % 2)
        self.far_quarter = self.pair_quarter + 1 - 2 * core
        self.pair = {"ctx": z + 1 - 2 * (z % 2)}

    def worker(self, block):
        group, quarter = block // self.place.z_size, block % self.place.z_size
        return {"dp": group - group % 2 + quarter % 2, "ctx": 2 * (group % 2) + quarter // 2}

    def owner(self, block):
        return {"dp": block // self.place.z_size, "ctx": block % self.place.z_size}

    def greet_all(self):
        barrier = pltpu.get_barrier_semaphore()

        def signal(step, carry):
            other = (self.home + step) % self.blocks
            pl.semaphore_signal(
                barrier, inc=1, device_id=self.owner(other), device_id_type=MESH
            )
            return carry

        lax.fori_loop(1, self.blocks, signal, 0)
        pl.semaphore_wait(barrier, self.blocks - 1)


def shard_rows(unit, shard, width):
    start = width * unit + BLOCK * shard
    start = start + unit // 8 * (3 * BLOCK * shard - (width - BLOCK) * (unit - 8))
    return pl.multiple_of(start, 32)


class Weights:
    def __init__(self, place, full, send, recv):
        self.place, self.full, self.send, self.recv = place, full, send, recv
        self.width = full.shape[1]

    def at(self, unit, shard, first=0, count=BLOCK):
        start = shard_rows(unit, shard, self.width)
        return self.full.at[pl.ds(pl.multiple_of(start + first, 16), count), :]

    def copy(self, unit, kind, arriving):
        place = self.place
        own, across, along = place.dp, place.across["dp"], place.along["dp"]
        corner = across + along - own
        half = BLOCK // 2
        mate = place.mate["dp"] - own
        shard, first, count, to = (
            (own, 0, BLOCK, place.across),
            (own, 0, BLOCK, place.along),
            (own, 0, BLOCK, place.mate),
            (across, 0, half, place.along),
            (along, half, half, place.across),
            (across, 0, BLOCK, place.mate),
            (along, 0, BLOCK, place.mate),
            (corner, 0, BLOCK, place.mate),
        )[kind]
        if arriving:
            shard = (across, along, own + mate, corner, corner, across + mate, along + mate, corner + mate)[kind]
        ref = self.at(unit, shard, first, count)
        return remote(ref, ref, self.send.at[unit, kind], self.recv.at[unit, kind], to)

    def begin(self, unit):
        for kind in (0, 1, 2):
            self.copy(unit, kind, False).start()

    def pass_on(self, unit):
        self.copy(unit, 0, True).wait_recv()
        self.copy(unit, 3, False).start()
        self.copy(unit, 5, False).start()
        self.copy(unit, 1, True).wait_recv()
        self.copy(unit, 4, False).start()
        self.copy(unit, 6, False).start()

    def corner(self, unit):
        self.copy(unit, 3, True).wait_recv()
        self.copy(unit, 4, True).wait_recv()
        self.copy(unit, 7, False).start()

    def tick(self, step):
        self.begin(step)
        self.pass_on(step - 2)
        if not isinstance(step, int) or step >= 3:
            self.corner(step - 3)

    def ready(self, unit):
        for kind in (2, 5, 6, 7):
            self.copy(unit, kind, True).wait_recv()

    def drain(self):
        def one(unit, carry):
            for kind in range(8):
                self.copy(unit, kind, False).wait_send()
            return carry

        lax.fori_loop(0, UNITS, one, 0)


def iota(shape, axis):
    return lax.broadcasted_iota(jnp.int32, shape, axis)


def column(row):
    n = row.shape[1]
    return jnp.sum(jnp.where(iota((n, n), 0) == iota((n, n), 1), row, 0.0), 1, keepdims=True)


def dot(left, right):
    return jnp.dot(left, right, preferred_element_type=F32)


def dot_nt(left, right):
    return lax.dot_general(
        left, right, (((1,), (1,)), ((), ())), preferred_element_type=F32
    )


def one_hot(condition):
    return jnp.where(condition, 1.0, 0.0).astype(BF16)


FORWARD_SCRATCH = dict(
    ints=lambda t, w, b: pltpu.VMEM((b, 2, t), jnp.int32),
    order=lambda t, w, b: pltpu.VMEM((b, t), jnp.int32),
    ids=lambda t, w, b: pltpu.VMEM((2, 4, 1, t), jnp.int32),
    pieces=lambda t, w, b: pltpu.VMEM((8, 16, w // 2), BF16),
    vectors=lambda t, w, b: pltpu.VMEM((16, w), F32),
    pack_out=lambda t, w, b: pltpu.VMEM((2 * t, w), BF16),
    pack_in=lambda t, w, b: pltpu.VMEM((2 * t, w), BF16),
    teach_out=lambda t, w, b: pltpu.VMEM((t, w), BF16),
    teach_in=lambda t, w, b: pltpu.VMEM((t, w), BF16),
    full=lambda t, w, b: pltpu.VMEM((12 * w, w), BF16),
    packed=lambda t, w, b: pltpu.VMEM((t, w), BF16),
    packed_t=lambda t, w, b: pltpu.VMEM((w, t), BF16),
    cot=lambda t, w, b: pltpu.VMEM((t, w), BF16),
    query=lambda t, w, b: pltpu.VMEM((t, w), BF16),
    keys=lambda t, w, b: pltpu.VMEM((4, t, w), BF16),
    values_t=lambda t, w, b: pltpu.VMEM((4, w, t), BF16),
    mask=lambda t, w, b: pltpu.VMEM((4, t, t), F32),
    scores=lambda t, w, b: pltpu.VMEM((2, 4, t, t), F32),
    probs=lambda t, w, b: pltpu.VMEM((HEADS, 4, t, t), BF16),
    keys_t=lambda t, w, b: pltpu.VMEM((4, w, t), BF16),
    values=lambda t, w, b: pltpu.VMEM((4, t, w), BF16),
    context_t=lambda t, w, b: pltpu.VMEM((w, t), BF16),
    scaled=lambda t, w, b: pltpu.VMEM((t, w), F32),
    inverse=lambda t, w, b: pltpu.VMEM((t, 128), F32),
    normed=lambda t, w, b: pltpu.VMEM((t, w), F32),
    low=lambda t, w, b: pltpu.VMEM((t, w), BF16),
    low_t=lambda t, w, b: pltpu.VMEM((w, t), BF16),
    act=lambda t, w, b: pltpu.VMEM((t, 4 * w), BF16),
    act_t=lambda t, w, b: pltpu.VMEM((4 * w, t), BF16),
    slope=lambda t, w, b: pltpu.VMEM((t, 4 * w), BF16),
    result=lambda t, w, b: pltpu.VMEM((t, w), BF16),
    grad_res=lambda t, w, b: pltpu.VMEM((t, w), F32),
    grad_ffn=lambda t, w, b: pltpu.VMEM((t, w), BF16),
    small=lambda t, w, b: pltpu.VMEM((16, w), F32),
    routes=lambda t, w, b: pltpu.VMEM((8, t), F32),
    ints_send=lambda t, w, b: pltpu.SemaphoreType.DMA((b,)),
    ints_recv=lambda t, w, b: pltpu.SemaphoreType.DMA((b,)),
    piece_send=lambda t, w, b: pltpu.SemaphoreType.DMA((8,)),
    piece_recv=lambda t, w, b: pltpu.SemaphoreType.DMA((8,)),
    pack_send=lambda t, w, b: pltpu.SemaphoreType.DMA((b,)),
    pack_recv=lambda t, w, b: pltpu.SemaphoreType.DMA((b,)),
    misc_send=lambda t, w, b: pltpu.SemaphoreType.DMA((8,)),
    misc_recv=lambda t, w, b: pltpu.SemaphoreType.DMA((8,)),
    weight_send=lambda t, w, b: pltpu.SemaphoreType.DMA((UNITS, 8)),
    weight_recv=lambda t, w, b: pltpu.SemaphoreType.DMA((UNITS, 8)),
    own_sem=lambda t, w, b: pltpu.SemaphoreType.DMA((UNITS,)),
    store_sem=lambda t, w, b: pltpu.SemaphoreType.DMA((32,)),
)

class Kept(NamedTuple):
    full: object
    probs: object
    keys_t: object
    values: object
    packed_t: object
    query: object
    context_t: object
    scaled: object
    inverse: object
    low_t: object
    act_t: object
    slope: object
    result: object
    grad_res: object
    grad_ffn: object
    small: object
    routes: object


HEADS = 12
NORM_EPS = 1e-12


def normalize(value):
    centre = value - jnp.mean(value, -1, keepdims=True)
    spread = jnp.mean(centre * centre, -1, keepdims=True)
    inverse = lax.rsqrt(spread + NORM_EPS)
    return centre * inverse, inverse


def forward_kernel(z_size, ints, ids, tokens, cotangent, teacher, pieces, w_query, w_key, w_value, w_out, w_up, w_down, *refs):
    outs = Kept(*refs[: len(Kept._fields)])
    s = SimpleNamespace(**dict(zip(FORWARD_SCRATCH, refs[len(Kept._fields) :])))
    route = Route(z_size)
    place = route.place
    rows, width = tokens.shape
    blocks = route.blocks
    full = s.full
    weights = Weights(place, full, s.weight_send, s.weight_recv)
    stores = []

    def keep(source, target):
        copy = pltpu.make_async_copy(source, target, s.store_sem.at[len(stores)])
        copy.start()
        stores.append(copy)

    sources = (
        [w_key, w_value, w_query, w_out]
        + [w_up.at[:, width * i : width * (i + 1)] for i in range(4)]
        + [w_down.at[BLOCK * i : BLOCK * (i + 1), :] for i in range(4)]
    )
    own_copies = [
        pltpu.make_async_copy(source, weights.at(unit, place.dp), s.own_sem.at[unit])
        for unit, source in enumerate(sources)
    ]
    for copy in own_copies:
        copy.start()
    s.ints[route.home] = ints[...]
    s.teach_out[...] = teacher[...].astype(BF16)
    route.greet_all()

    def ints_copy(other):
        return remote(
            ints,
            s.ints.at[route.home],
            s.ints_send.at[other],
            s.ints_recv.at[route.home],
            route.owner(other),
        )

    def ints_arrival(other):
        ref = s.ints.at[other]
        return remote(ref, ref, s.ints_send.at[other], s.ints_recv.at[other], route.owner(other))

    def each_other(start, action):
        def one(step, carry):
            action((start + step) % blocks)
            return carry

        lax.fori_loop(1, blocks, one, 0)

    each_other(route.home, lambda other: ints_copy(other).start())
    for copy in own_copies[:2]:
        copy.wait()
    weights.begin(0)
    weights.begin(1)

    def piece_copy(step):
        other = (place.dp + step) % 8
        return remote(
            pieces,
            s.pieces.at[place.dp],
            s.piece_send.at[step],
            s.piece_recv.at[step],
            {"dp": other},
        )

    for step in range(1, 8):
        piece_copy(step).start()
    s.pieces[place.dp] = pieces[...]
    ids_copy = remote(ids, s.ids.at[1], s.misc_send.at[0], s.misc_recv.at[0], place.mate)
    ids_copy.start()
    s.ids[0] = ids[...]
    for copy in own_copies[2:]:
        copy.wait()

    each_other(route.home, lambda other: ints_arrival(other).wait_recv())
    count = jnp.zeros((1, rows), F32)
    for other in range(blocks):
        s.order[other : other + 1, :] = s.ints[other, 0:1, :]
        count = count + s.ints[other, 1:2, :].astype(F32)
    count = jnp.sum(count, 1, keepdims=True)
    order = s.order[...]
    source = lax.shift_right_logical(order, 8)
    local = (order - source * rows).astype(F32)
    mine = source == route.home
    earlier = one_hot(iota((rows, rows), 0) < iota((rows, rows), 1))
    rank = dot(one_hot(mine), earlier)
    per_block = rows // blocks
    slots = jnp.zeros((blocks, 128), F32)
    for k in range(per_block):
        picked = jnp.sum(jnp.where(mine & (rank == k), local, 0.0), 1, keepdims=True)
        slots = jnp.where(iota((blocks, 128), 1) == k, picked, slots)
    spread = one_hot(
        lax.shift_right_logical(iota((2 * rows, blocks), 0), 4) == iota((2 * rows, blocks), 1)
    )
    slot_rows = dot(spread, slots.astype(BF16))
    slot = iota((2 * rows, 128), 0)
    picked = jnp.sum(
        jnp.where(iota((2 * rows, 128), 1) == (slot & 7), slot_rows, 0.0), 1, keepdims=True
    )
    lane = iota((2 * rows, rows), 1).astype(F32)
    first = (iota((2 * rows, rows), 0) & 8) == 0
    hit = lane == picked
    s.pack_out[...] = (
        dot(one_hot(hit & first), tokens[...])
        + dot(one_hot(hit & jnp.logical_not(first)), cotangent[...])
    ).astype(BF16)
    spread8 = one_hot(
        lax.shift_right_logical(iota((rows, blocks), 0), 3) == iota((rows, blocks), 1)
    )
    slot8 = jnp.sum(
        jnp.where(
            iota((rows, 128), 1) == (iota((rows, 128), 0) & 7),
            dot(spread8, slots.astype(BF16)),
            0.0,
        ),
        1,
        keepdims=True,
    )
    diagonal = iota((rows, rows), 0) == iota((rows, rows), 1)
    s.routes[1:2, :] = jnp.sum(jnp.where(diagonal, slot8, 0.0), 0, keepdims=True)

    def span(block):
        return pl.ds(pl.multiple_of(16 * block, 16), 16)

    def pack_copy(block):
        return remote(
            s.pack_out.at[span(block), :],
            s.pack_in.at[span(route.home), :],
            s.pack_send.at[block],
            s.pack_recv.at[route.home],
            route.worker(block),
        )

    def pack_arrival(other):
        ref = s.pack_in.at[span(other), :]
        return remote(ref, ref, s.pack_send.at[other], s.pack_recv.at[other], route.owner(other))

    each_other(route.block, lambda block: pack_copy(block).start())
    s.pack_in[span(route.home), :] = s.pack_out[span(route.block), :]
    weights.tick(2)

    moved_to = route.worker(route.home)
    stays = route.block == route.home
    teach_copy = remote(
        s.teach_out, s.teach_in, s.misc_send.at[1], s.misc_recv.at[1], moved_to
    )

    for step in range(1, 8):
        piece_copy(step).wait_recv()
    wrapped = one_hot(
        iota((BLOCK, width), 0) == iota((BLOCK, width), 1) - BLOCK * (iota((BLOCK, width), 1) // BLOCK)
    )
    owner = iota((16, width), 1) // BLOCK
    vectors = jnp.zeros((16, width), F32)
    for k in range(8):
        vectors = vectors + jnp.where(owner == k, dot(s.pieces[k, :, :BLOCK], wrapped), 0.0)
    s.vectors[...] = vectors
    for k in range(8):
        part = s.pieces[k, 8:9, :].astype(F32)
        s.vectors[8 + k // 2 : 9 + k // 2, 4 * BLOCK * (k % 2) : 4 * BLOCK * (k % 2 + 1)] = part

    def vector(index):
        return s.vectors[index : index + 1, :]

    ids_copy.wait_recv()
    here = s.ints[route.block, 0:1, :]
    source_row = lax.shift_right_logical(here, 8).astype(F32)
    source_col = column(source_row)
    same = source_col == source_row
    before = iota((rows, rows), 1) < iota((rows, rows), 0)
    rank_col = jnp.sum(jnp.where(same & before, 1.0, 0.0), 1, keepdims=True)
    rank_row = jnp.sum(
        jnp.where(same & jnp.logical_not(before | diagonal), 1.0, 0.0), 0, keepdims=True
    )
    s.routes[0:1, :] = source_row * 8 + rank_row
    wide = iota((rows, 2 * rows), 1).astype(F32)
    place_col = source_col * 16 + rank_col
    each_other(route.home, lambda other: pack_arrival(other).wait_recv())
    s.packed[...] = dot(one_hot(wide == place_col), s.pack_in[...]).astype(BF16)
    s.cot[...] = dot(one_hot(wide == place_col + 8), s.pack_in[...]).astype(BF16)
    s.packed_t[...] = s.packed[...].T
    keep(s.packed_t, outs.packed_t)
    weights.tick(3)
    weights.tick(4)
    weights.tick(5)

    def kv_copy(kind):
        buffer, half = (s.keys, s.values_t)[kind // 3], kind % 3
        quarter, to = (
            (route.quarter, route.pair),
            (route.quarter, place.mate),
            (route.pair_quarter, place.mate),
        )[half]
        ref = buffer.at[quarter]
        return remote(ref, ref, s.misc_send.at[2 + kind], s.misc_recv.at[2 + kind], to)

    def kv_arrival(kind):
        buffer, half = (s.keys, s.values_t)[kind // 3], kind % 3
        quarter = (route.pair_quarter, route.mate_quarter, route.far_quarter)[half]
        ref = buffer.at[quarter]
        to = (route.pair, place.mate, place.mate)[half]
        return remote(ref, ref, s.misc_send.at[2 + kind], s.misc_recv.at[2 + kind], to)

    packed = s.packed[...]

    def whole(unit):
        return full[width * unit : width * (unit + 1), :]

    weights.ready(0)
    s.keys[route.quarter] = dot(packed, whole(0)).astype(BF16)
    weights.ready(1)
    values = (dot(packed, whole(1)) + vector(1)).astype(BF16)
    kv_copy(0).start()
    kv_copy(1).start()
    s.values_t[route.quarter] = values.T
    weights.ready(2)
    scale = (width // HEADS) ** -0.5
    s.query[...] = (
        (dot(packed, whole(2)) + vector(0)).astype(BF16).astype(F32) * scale
    ).astype(BF16)
    kv_copy(3).start()
    kv_copy(4).start()
    keep(s.query, outs.query)

    @pl.when(jnp.logical_not(stays))
    def _():
        teach_copy.start()

    @pl.when(stays)
    def _():
        s.teach_in[...] = s.teach_out[...]

    from_own = place.core == route.group_core
    query_row = jnp.where(
        from_own, s.ids[0, route.quarter], s.ids[1, route.quarter]
    ).astype(F32)
    for quarter in range(4):
        key_row = jnp.where(from_own, s.ids[0, quarter], s.ids[1, quarter]).astype(F32)
        s.mask[quarter] = jnp.where(column(key_row) == query_row, 0.0, -1e30)
    kv_arrival(0).wait_recv()
    kv_copy(2).start()
    kv_arrival(3).wait_recv()
    kv_copy(5).start()
    for kind in (1, 2, 4, 5):
        kv_arrival(kind).wait_recv()

    head = width // HEADS
    left_half = iota((rows, 2 * head), 1) < head

    def pair_of_heads(pair, carry):
        weights.tick(pair + 6)
        lanes = pl.ds(pl.multiple_of(2 * head * pair, 2 * head), 2 * head)
        both = s.query[:, lanes]
        for side in range(2):
            keep_lane = left_half if side == 0 else jnp.logical_not(left_half)
            chosen = jnp.where(keep_lane, both, jnp.zeros_like(both))
            top = jnp.full((1, rows), -3e38, F32)
            for quarter in range(4):
                part = dot_nt(s.keys[quarter, :, lanes], chosen) + s.mask[quarter]
                s.scores[side, quarter] = part
                top = jnp.maximum(top, jnp.max(part, 0, keepdims=True))
            total = jnp.zeros((1, rows), F32)
            for quarter in range(4):
                part = jnp.exp(s.scores[side, quarter] - top)
                s.scores[side, quarter] = part
                total = total + jnp.sum(part, 0, keepdims=True)
            share = 1.0 / total
            index = 2 * pair + side
            down = pl.ds(pl.multiple_of(head * index, head), head)
            summed = jnp.zeros((head, rows), F32)
            for quarter in range(4):
                part = (s.scores[side, quarter] * share).astype(BF16)
                s.probs[index, quarter] = part
                summed = summed + dot(s.values_t[quarter, down, :], part)
            s.context_t[down, :] = summed.astype(BF16)
        return carry

    lax.fori_loop(0, HEADS // 2, pair_of_heads, 0)
    keep(s.probs, outs.probs)
    keep(s.context_t, outs.context_t)
    weights.pass_on(10)
    weights.corner(9)

    weights.ready(3)
    branch = dot(s.context_t[...].T, whole(3)) + vector(2)
    scaled, inverse = normalize(s.packed[...].astype(F32) + branch)
    s.scaled[...] = scaled
    s.inverse[...] = jnp.broadcast_to(inverse, (rows, 128))
    normed = scaled * vector(3) + vector(4)
    s.normed[...] = normed
    low = normed.astype(BF16)
    s.low[...] = low
    s.low_t[...] = low.T
    keep(s.scaled, outs.scaled)
    keep(s.inverse, outs.inverse)
    keep(s.low_t, outs.low_t)
    weights.pass_on(11)
    weights.corner(10)
    weights.corner(11)

    for part in range(4):
        weights.ready(4 + part)
    root_half, norm = 2.0**-0.5, (2.0 * math.pi) ** -0.5
    piece = width // 2

    def up(step, carry):
        lanes = pl.ds(pl.multiple_of(piece * (step % 2), piece), piece)
        wide = pl.ds(pl.multiple_of(piece * step, piece), piece)
        down = pl.ds(pl.multiple_of(width * (4 + step // 2), width), width)
        bias = s.vectors[pl.ds(8 + step // 2, 1), lanes]
        pre = dot(s.low[...], full[down, lanes]) + bias
        phi = 0.5 + 0.5 * lax.erf(pre * root_half)
        act = (pre * phi).astype(BF16)
        s.act[:, wide] = act
        s.act_t[wide, :] = act.T
        s.slope[:, wide] = (phi + pre * (norm * jnp.exp(-0.5 * pre * pre))).astype(BF16)
        return carry

    lax.fori_loop(0, 8, up, 0)
    keep(s.act_t, outs.act_t)
    keep(s.slope, outs.slope)
    for quarter in range(4):
        s.keys_t[quarter] = s.keys[quarter].T
        s.values[quarter] = s.values_t[quarter].T
    keep(s.keys_t, outs.keys_t)
    keep(s.values, outs.values)
    for part in range(4):
        weights.ready(8 + part)
    keep(s.full, outs.full)
    ffn = dot(s.act[...], full[8 * width :, :]) + vector(5)

    scaled, inverse = normalize(s.normed[...] + ffn)
    result = scaled * vector(6) + vector(7)
    s.result[...] = result.astype(BF16)
    keep(s.result, outs.result)

    @pl.when(jnp.logical_not(stays))
    def _():
        teach_copy.wait_recv()

    valid = column(s.ints[route.block, 1:2, :].astype(F32))
    miss = valid * (result - s.teach_in[...].astype(F32))
    factor = 1.0 / (count * width)
    s.small[...] = jnp.zeros((16, width), F32)
    s.small[12:13, :] = jnp.sum(miss * miss, 0, keepdims=True) * factor
    grad_out = s.cot[...].astype(F32) + (2.0 * factor) * miss
    s.small[6:7, :] = jnp.sum(grad_out * scaled, 0, keepdims=True)
    s.small[7:8, :] = jnp.sum(grad_out, 0, keepdims=True)
    s.small[13:14, :] = vector(3)
    grad_scaled = grad_out * vector(6)
    grad_res = inverse * (
        grad_scaled
        - jnp.mean(grad_scaled, -1, keepdims=True)
        - scaled * jnp.mean(grad_scaled * scaled, -1, keepdims=True)
    )
    s.grad_res[...] = grad_res
    grad_ffn = grad_res.astype(BF16)
    s.grad_ffn[...] = grad_ffn
    s.small[5:6, :] = jnp.sum(grad_ffn.astype(F32), 0, keepdims=True)
    keep(s.grad_res, outs.grad_res)
    keep(s.grad_ffn, outs.grad_ffn)
    keep(s.small, outs.small)
    keep(s.routes, outs.routes)

    weights.drain()
    each_other(route.home, lambda other: ints_copy(other).wait_send())
    each_other(route.block, lambda block: pack_copy(block).wait_send())
    for step in range(1, 8):
        piece_copy(step).wait_send()
    ids_copy.wait_send()
    for kind in range(6):
        kv_copy(kind).wait_send()

    @pl.when(jnp.logical_not(stays))
    def _():
        teach_copy.wait_send()

    for copy in stores:
        copy.wait()


def encoder_forward(z_size, ints, ids, tokens, cotangent, teacher, pieces, *shards):
    rows, width = tokens.shape
    blocks = 8 * z_size
    scratch = {name: make(rows, width, blocks) for name, make in FORWARD_SCRATCH.items()}
    vmem, anywhere = pl.BlockSpec(memory_space=pltpu.VMEM), pl.BlockSpec(memory_space=pl.ANY)
    results = pl.pallas_call(
        partial(forward_kernel, z_size),
        out_shape=tuple(
            jax.ShapeDtypeStruct(scratch[name].shape, scratch[name].dtype) for name in Kept._fields
        ),
        in_specs=[vmem] * 6 + [anywhere] * 6,
        out_specs=(anywhere,) * len(Kept._fields),
        scratch_shapes=list(scratch.values()),
        compiler_params=pltpu.CompilerParams(
            collective_id=0, has_side_effects=True, vmem_limit_bytes=62 * 2**20
        ),
        name="encoder_forward",
    )(ints, ids, tokens, cotangent, teacher, pieces, *shards)
    return Kept(*results)


LEFT = (0, 1, 2, 3, 4, 4, 4, 4, 5, 6, 6, 6)
RIGHT = (0, 0, 0, 0, 1, 2, 3, 4, 5, 6, 7, 8)


class Grads:
    def __init__(self, place, s, out):
        self.place, self.s, self.out = place, s, out
        self.tok_rows = s.left.shape[2] // 2
        half = BLOCK // 2
        self.low, self.high = slice(0, half), slice(half, BLOCK)

    def source_rows(self, group, j, core):
        shard = 2 * j + core
        if group < 4:
            return pl.ds(pl.multiple_of(4 * BLOCK * shard + BLOCK * group, 32), BLOCK)
        return pl.ds(pl.multiple_of(BLOCK * shard, 32), BLOCK)

    def left_copy(self, group, j, source):
        return remote(
            source.at[self.source_rows(group, j, 1 - self.place.core), :],
            self.s.left.at[group, BLOCK * j : BLOCK * (j + 1), self.tok_rows :],
            self.s.left_send.at[group, j],
            self.s.left_recv.at[group, j],
            self.place.mate,
        )

    def left_own(self, group, j, source):
        return pltpu.make_async_copy(
            source.at[self.source_rows(group, j, self.place.core), :],
            self.s.left.at[group, BLOCK * j : BLOCK * (j + 1), : self.tok_rows],
            self.s.left_own.at[group, j],
        )

    def give_left(self, group, source):
        for j in range(4):
            self.left_copy(group, j, source).start()
            self.left_own(group, j, source).start()

    def take_left(self, group, source):
        for j in range(4):
            self.left_copy(group, j, source).wait_recv()
            self.left_own(group, j, source).wait()

    def own_right(self, index):
        return self.s.right.at[index, : self.tok_rows, :]

    def right_copy(self, index):
        return remote(
            self.own_right(index),
            self.s.right.at[index, self.tok_rows :, :],
            self.s.right_send.at[index],
            self.s.right_recv.at[index],
            self.place.mate,
        )

    def copy(self, unit, kind):
        place, low, high, s = self.place, self.low, self.high, self.s
        source, target, to = (
            (s.out_d.at[unit, low], s.in_dx.at[unit], place.across),
            (s.out_d.at[unit, high], s.in_dy.at[unit], place.along),
            (s.out_x.at[unit, low], s.in_x.at[unit, low], place.across),
            (s.out_x.at[unit, high], s.in_x.at[unit, high], place.across),
            (s.out_y.at[unit, low], s.in_y.at[unit, low], place.along),
            (s.out_y.at[unit, high], s.in_y.at[unit, high], place.along),
            (s.out_x.at[unit], s.in_z.at[0, unit], {"ctx": place.z + 1}),
            (s.out_y.at[unit], s.in_z.at[1, unit], {"ctx": place.z - 1}),
        )[kind]
        return remote(source, target, s.send.at[unit, kind], s.recv.at[unit, kind], to)

    def part(self, j):
        return pl.ds(pl.multiple_of(BLOCK * j, 32), BLOCK)

    def multiply(self, unit):
        place, low, high, s = self.place, self.low, self.high, self.s
        s.partial[...] = dot(s.left[LEFT[unit]], s.right[RIGHT[unit]])
        s.out_d[unit] = s.partial[self.part(place.j_d), :].astype(BF16)
        s.out_x[unit] = s.partial[self.part(place.j_x), :].astype(BF16)
        s.out_y[unit] = s.partial[self.part(place.j_y), :].astype(BF16)
        s.total[unit] = s.partial[self.part(place.j_own), :]
        for kind in (0, 1, 2, 5):
            self.copy(unit, kind).start()

    def pass_on(self, unit):
        low, high, s = self.low, self.high, self.s
        self.copy(unit, 0).wait_recv()
        s.out_y[unit, low] = (
            s.out_y[unit, low].astype(F32) + s.in_dx[unit].astype(F32)
        ).astype(BF16)
        self.copy(unit, 1).wait_recv()
        s.out_x[unit, high] = (
            s.out_x[unit, high].astype(F32) + s.in_dy[unit].astype(F32)
        ).astype(BF16)
        self.copy(unit, 4).start()
        self.copy(unit, 3).start()

    def gather(self, unit):
        s = self.s
        for kind in (2, 3, 4, 5):
            self.copy(unit, kind).wait_recv()
        s.total[unit] = (
            s.total[unit] + s.in_x[unit].astype(F32) + s.in_y[unit].astype(F32)
        )
        for kind in (2, 3, 4, 5):
            self.copy(unit, kind).wait_send()

    def hop(self, unit, step):
        place, s = self.place, self.s
        for way, turn in ((0, step), (1, place.z_size - 1 - step)):

            @pl.when(place.z == turn)
            def _():
                value = s.total[unit]
                if step > 0:
                    self.copy(unit, 6 + way).wait_recv()
                    value = value + s.in_z[way, unit].astype(F32)
                (s.out_x, s.out_y)[way][unit] = value.astype(BF16)
                self.copy(unit, 6 + way).start()

    def result(self, unit):
        return pltpu.make_async_copy(
            self.s.total.at[unit], self.out.at[unit], self.s.out_sem.at[unit]
        )

    def finish(self, unit):
        place, s = self.place, self.s
        last = place.z_size - 1

        @pl.when(place.z == last)
        def _():
            self.copy(unit, 6).wait_recv()

        @pl.when(place.z == 0)
        def _():
            self.copy(unit, 7).wait_recv()

        for way, present in ((0, place.z > 0), (1, place.z < last)):

            @pl.when(present)
            def _():
                s.total[unit] = s.total[unit] + s.in_z[way, unit].astype(F32)

        self.result(unit).start()

    def drain(self, lefts):
        place = self.place

        def one(unit, carry):
            self.copy(unit, 0).wait_send()
            self.copy(unit, 1).wait_send()

            @pl.when(place.z < place.z_size - 1)
            def _():
                self.copy(unit, 6).wait_send()

            @pl.when(place.z > 0)
            def _():
                self.copy(unit, 7).wait_send()

            self.result(unit).wait()
            return carry

        lax.fori_loop(0, UNITS, one, 0)
        for group in range(7):
            for j in range(4):
                self.left_copy(group, j, lefts[group]).wait_send()
        for index in range(9):
            self.right_copy(index).wait_send()


BACKWARD_SCRATCH = dict(
    left=lambda t, w, b: pltpu.VMEM((7, 4 * BLOCK, 2 * t), BF16),
    right=lambda t, w, b: pltpu.VMEM((9, 2 * t, w), BF16),
    partial=lambda t, w, b: pltpu.VMEM((4 * BLOCK, w), F32),
    out_d=lambda t, w, b: pltpu.VMEM((UNITS, BLOCK, w), BF16),
    out_x=lambda t, w, b: pltpu.VMEM((UNITS, BLOCK, w), BF16),
    out_y=lambda t, w, b: pltpu.VMEM((UNITS, BLOCK, w), BF16),
    in_dx=lambda t, w, b: pltpu.VMEM((UNITS, BLOCK // 2, w), BF16),
    in_dy=lambda t, w, b: pltpu.VMEM((UNITS, BLOCK // 2, w), BF16),
    in_x=lambda t, w, b: pltpu.VMEM((UNITS, BLOCK, w), BF16),
    in_y=lambda t, w, b: pltpu.VMEM((UNITS, BLOCK, w), BF16),
    total=lambda t, w, b: pltpu.VMEM((UNITS, BLOCK, w), F32),
    in_z=lambda t, w, b: pltpu.VMEM((2, UNITS, BLOCK, w), BF16),
    weight_a=lambda t, w, b: pltpu.VMEM((4 * w, w), BF16),
    weight_b=lambda t, w, b: pltpu.VMEM((4 * w, w), BF16),
    probs=lambda t, w, b: pltpu.VMEM((2, 2, 4, t, t), BF16),
    keys_t=lambda t, w, b: pltpu.VMEM((4, w, t), BF16),
    values=lambda t, w, b: pltpu.VMEM((4, t, w), BF16),
    query=lambda t, w, b: pltpu.VMEM((t, w), BF16),
    context_t=lambda t, w, b: pltpu.VMEM((w, t), BF16),
    scaled=lambda t, w, b: pltpu.VMEM((t, w), F32),
    inverse=lambda t, w, b: pltpu.VMEM((t, 128), F32),
    slope=lambda t, w, b: pltpu.VMEM((t, 4 * w), BF16),
    result=lambda t, w, b: pltpu.VMEM((t, w), BF16),
    grad_res=lambda t, w, b: pltpu.VMEM((t, w), F32),
    small=lambda t, w, b: pltpu.VMEM((16, w), F32),
    routes=lambda t, w, b: pltpu.VMEM((8, t), F32),
    grad_context=lambda t, w, b: pltpu.VMEM((t, w), BF16),
    grad_context_t=lambda t, w, b: pltpu.VMEM((w, t), BF16),
    grad_query_t=lambda t, w, b: pltpu.VMEM((w, t), BF16),
    kv_out=lambda t, w, b: pltpu.VMEM((HEADS // 2, 4, t, t), BF16),
    kv_mate=lambda t, w, b: pltpu.VMEM((HEADS // 2, 2, t, t), BF16),
    kv_pair=lambda t, w, b: pltpu.VMEM((HEADS // 2, t, t), BF16),
    back_out=lambda t, w, b: pltpu.VMEM((2, b, t // b, w), BF16),
    back_in=lambda t, w, b: pltpu.VMEM((2, b, t // b, w), BF16),
    homes=lambda t, w, b: pltpu.VMEM((2, t, w), BF16),
    sums=lambda t, w, b: pltpu.VMEM((3, 16, w), F32),
    got_sums=lambda t, w, b: pltpu.VMEM((3, 16, w), F32),
    got_z=lambda t, w, b: pltpu.VMEM((b // 8, 16, w), F32),
    send=lambda t, w, b: pltpu.SemaphoreType.DMA((UNITS, 8)),
    recv=lambda t, w, b: pltpu.SemaphoreType.DMA((UNITS, 8)),
    left_send=lambda t, w, b: pltpu.SemaphoreType.DMA((7, 4)),
    left_recv=lambda t, w, b: pltpu.SemaphoreType.DMA((7, 4)),
    left_own=lambda t, w, b: pltpu.SemaphoreType.DMA((7, 4)),
    right_send=lambda t, w, b: pltpu.SemaphoreType.DMA((9,)),
    right_recv=lambda t, w, b: pltpu.SemaphoreType.DMA((9,)),
    out_sem=lambda t, w, b: pltpu.SemaphoreType.DMA((UNITS,)),
    load_sem=lambda t, w, b: pltpu.SemaphoreType.DMA((20,)),
    probs_sem=lambda t, w, b: pltpu.SemaphoreType.DMA((2,)),
    kv_send=lambda t, w, b: pltpu.SemaphoreType.DMA((HEADS // 2, 3)),
    kv_recv=lambda t, w, b: pltpu.SemaphoreType.DMA((HEADS // 2, 3)),
    back_send=lambda t, w, b: pltpu.SemaphoreType.DMA((2, b)),
    back_recv=lambda t, w, b: pltpu.SemaphoreType.DMA((2, b)),
    sum_send=lambda t, w, b: pltpu.SemaphoreType.DMA((3 + b // 8,)),
    sum_recv=lambda t, w, b: pltpu.SemaphoreType.DMA((3 + b // 8,)),
)


def backward_kernel(z_size, *refs):
    count = len(Kept._fields)
    given = Kept(*refs[:count])
    out_grads, out_homes, out_small = refs[count : count + 3]
    s = SimpleNamespace(**dict(zip(BACKWARD_SCRATCH, refs[count + 3 :])))
    route = Route(z_size)
    place = route.place
    rows, width = s.query.shape
    blocks = route.blocks
    grads = Grads(place, s, out_grads)
    head = width // HEADS
    pairs = HEADS // 2

    count = [0]

    def load(source, target):
        copy = pltpu.make_async_copy(source, target, s.load_sem.at[count[0]])
        count[0] += 1
        copy.start()
        return copy

    def loaded(*copies):
        for copy in copies:
            copy.wait()

    full = given.full
    l_ffn = load(given.grad_ffn, grads.own_right(0))
    l_down = load(full.at[2 * 4 * width :, :], s.weight_a)
    l_up = load(full.at[4 * width : 8 * width, :], s.weight_b)
    l_slope = load(given.slope, s.slope)
    l_routes = load(given.routes, s.routes)
    l_result = load(given.result, s.result)
    l_small = load(given.small, s.small)
    l_grad_res = load(given.grad_res, s.grad_res)
    l_scaled = load(given.scaled, s.scaled)
    l_inverse = load(given.inverse, s.inverse)
    l_query = load(given.query, s.query)
    l_context_t = load(given.context_t, s.context_t)
    l_keys_t = load(given.keys_t, s.keys_t)
    l_values = load(given.values, s.values)

    def probs_copy(pair):
        slot = pair % 2
        return pltpu.make_async_copy(
            given.probs.at[pl.ds(2 * pair, 2)], s.probs.at[slot], s.probs_sem.at[slot]
        )

    probs_copy(0).start()
    lefts = (given.act_t,) * 4 + (given.low_t, given.context_t, given.packed_t)
    route.greet_all()

    def each_other(start, action):
        def one(step, carry):
            action((start + step) % blocks)
            return carry

        lax.fori_loop(1, blocks, one, 0)

    loaded(l_ffn)
    grads.right_copy(0).start()
    for group in range(7):
        grads.give_left(group, lefts[group])

    def back_copy(which, other):
        return remote(
            s.back_out.at[which, other],
            s.back_in.at[which, route.block],
            s.back_send.at[which, other],
            s.back_recv.at[which, route.block],
            route.owner(other),
        )

    def back_arrival(which, block):
        ref = s.back_in.at[which, block]
        return remote(
            ref, ref, s.back_send.at[which, block], s.back_recv.at[which, block], route.worker(block)
        )

    def send_back(which, value):
        ordered = one_hot(iota((rows, rows), 0).astype(F32) == s.routes[0:1, :])
        s.back_out[which] = (
            dot(ordered, value).reshape(blocks, rows // blocks, width).astype(BF16)
        )
        each_other(route.home, lambda other: back_copy(which, other).start())
        s.back_in[which, route.block] = s.back_out[which, route.home]

    def take_back(which):
        each_other(route.block, lambda block: back_arrival(which, block).wait_recv())
        placed = one_hot(iota((rows, rows), 0).astype(F32) == s.routes[1:2, :])
        flat = s.back_in[which].astype(F32).reshape(rows, width).astype(BF16)
        s.homes[which] = dot(placed, flat).astype(BF16)

    for group in range(4):
        grads.take_left(group, lefts[group])
    grads.right_copy(0).wait_recv()
    for unit in range(4):
        grads.multiply(unit)

    loaded(l_routes, l_result)
    send_back(0, s.result[...])
    loaded(l_down, l_up, l_slope, l_small, l_grad_res, l_scaled, l_inverse)
    grad_ffn = s.right[0, :rows, :]
    grad_normed = s.grad_res[...]
    for part in range(4):
        block = slice(width * part, width * (part + 1))
        grad_act = dot_nt(grad_ffn, s.weight_a[block, :])
        grad_pre = (grad_act * s.slope[:, block].astype(F32)).astype(BF16)
        s.right[1 + part, :rows, :] = grad_pre
        s.small[8 + part : 9 + part, :] = jnp.sum(grad_pre.astype(F32), 0, keepdims=True)
        grad_normed = grad_normed + dot_nt(grad_pre, s.weight_b[block, :])
        grads.right_copy(1 + part).start()
        grads.pass_on(part)
    l_rest = load(full.at[: 4 * width, :], s.weight_a)

    scaled = s.scaled[...]
    s.small[3:4, :] = jnp.sum(grad_normed * scaled, 0, keepdims=True)
    s.small[4:5, :] = jnp.sum(grad_normed, 0, keepdims=True)
    grad_scaled = grad_normed * s.small[13:14, :]
    grad_res = s.inverse[:, :1] * (
        grad_scaled
        - jnp.mean(grad_scaled, -1, keepdims=True)
        - scaled * jnp.mean(grad_scaled * scaled, -1, keepdims=True)
    )
    s.grad_res[...] = grad_res
    grad_branch = grad_res.astype(BF16)
    s.right[5, :rows, :] = grad_branch
    s.small[2:3, :] = jnp.sum(grad_branch.astype(F32), 0, keepdims=True)
    grads.right_copy(5).start()
    grads.take_left(4, lefts[4])
    for part in range(4):
        grads.right_copy(1 + part).wait_recv()
        grads.multiply(4 + part)
    loaded(l_rest)
    grad_context = dot_nt(grad_branch, s.weight_a[3 * width :, :]).astype(BF16)
    s.grad_context[...] = grad_context
    s.grad_context_t[...] = grad_context.T
    grads.take_left(5, lefts[5])
    grads.right_copy(5).wait_recv()
    grads.multiply(8)
    for unit in range(3):
        grads.gather(unit)
    grads.hop(0, 0)
    grads.hop(1, 0)
    grads.hop(0, 1)
    loaded(l_query, l_context_t, l_keys_t, l_values)

    def kv_copy(pair, kind):
        source, target, to = (
            (s.kv_out.at[pair, route.mate_quarter], s.kv_mate.at[pair, 0], place.mate),
            (s.kv_out.at[pair, route.far_quarter], s.kv_mate.at[pair, 1], place.mate),
            (s.kv_out.at[pair, route.pair_quarter], s.kv_pair.at[pair], route.pair),
        )[kind]
        return remote(source, target, s.kv_send.at[pair, kind], s.kv_recv.at[pair, kind], to)

    def kv_second(pair):
        kv_copy(pair, 1).wait_recv()
        s.kv_out[pair, route.pair_quarter] = (
            s.kv_out[pair, route.pair_quarter].astype(F32) + s.kv_mate[pair, 1].astype(F32)
        ).astype(BF16)
        kv_copy(pair, 2).start()

    def kv_third(pair):
        kv_copy(pair, 0).wait_recv()
        kv_copy(pair, 2).wait_recv()
        summed = (
            s.kv_out[pair, route.quarter].astype(F32)
            + s.kv_mate[pair, 0].astype(F32)
            + s.kv_pair[pair].astype(F32)
        ).astype(BF16)
        lanes = pl.ds(pl.multiple_of(2 * head * pair, 2 * head), 2 * head)
        s.right[7, :rows, lanes] = summed[:, : 2 * head]
        s.right[8, :rows, lanes] = summed[:, 2 * head :]

    left_half = iota((rows, 2 * head), 1) < head
    scale = head**-0.5

    def pair_of_heads(pair, carry):
        @pl.when(pair < pairs - 1)
        def _():
            probs_copy(pair + 1).start()
            grads.pass_on(pair + 4)

        grads.gather(pair + 3)
        for step in range(3):
            grads.hop(pair + 2 - step, step)

        @pl.when(pair > 0)
        def _():
            grads.finish(pair - 1)
            kv_second(pair - 1)

        @pl.when(pair > 1)
        def _():
            kv_third(pair - 2)

        probs_copy(pair).wait()
        slot = pair % 2
        lanes = pl.ds(pl.multiple_of(2 * head * pair, 2 * head), 2 * head)
        both_c = s.grad_context[:, lanes]
        both_q = s.query[:, lanes]
        chosen_c, chosen_q, delta, grad_q = [], [], [], []
        for side in range(2):
            keep_lane = left_half if side == 0 else jnp.logical_not(left_half)
            chosen_c.append(jnp.where(keep_lane, both_c, jnp.zeros_like(both_c)))
            chosen_q.append(jnp.where(keep_lane, both_q, jnp.zeros_like(both_q)))
            down = pl.ds(pl.multiple_of(head * (2 * pair + side), head), head)
            delta.append(
                jnp.sum(
                    s.grad_context_t[down, :].astype(F32) * s.context_t[down, :].astype(F32),
                    0,
                    keepdims=True,
                )
            )
            grad_q.append(jnp.zeros((head, rows), F32))
        for quarter in range(4):
            value = s.values[quarter, :, lanes]
            grad_k = jnp.zeros((rows, 2 * head), F32)
            grad_v = jnp.zeros((rows, 2 * head), F32)
            for side in range(2):
                down = pl.ds(pl.multiple_of(head * (2 * pair + side), head), head)
                probs = s.probs[slot, side, quarter]
                grad_probs = dot_nt(value, chosen_c[side])
                grad_scores = (probs.astype(F32) * (grad_probs - delta[side])).astype(BF16)
                grad_v = grad_v + dot(probs, chosen_c[side])
                grad_k = grad_k + dot(grad_scores, chosen_q[side])
                grad_q[side] = grad_q[side] + dot(s.keys_t[quarter, down, :], grad_scores)
            s.kv_out[pair, quarter, :, : 2 * head] = grad_k.astype(BF16)
            s.kv_out[pair, quarter, :, 2 * head :] = grad_v.astype(BF16)
        kv_copy(pair, 0).start()
        kv_copy(pair, 1).start()
        for side in range(2):
            down = pl.ds(pl.multiple_of(head * (2 * pair + side), head), head)
            s.grad_query_t[down, :] = (grad_q[side] * scale).astype(BF16)
        return carry

    lax.fori_loop(0, pairs, pair_of_heads, 0)
    grad_query = s.grad_query_t[...].T
    s.right[6, :rows, :] = grad_query
    s.small[0:1, :] = jnp.sum(grad_query.astype(F32), 0, keepdims=True)
    grads.right_copy(6).start()
    kv_second(pairs - 1)
    kv_third(pairs - 2)
    grads.finish(5)
    grads.hop(8, 0)
    grads.hop(7, 1)
    grads.hop(6, 2)
    grads.take_left(6, lefts[6])
    grads.right_copy(6).wait_recv()
    grads.multiply(9)
    kv_third(pairs - 1)
    grads.right_copy(7).start()
    grads.right_copy(8).start()
    grad_value = s.right[8, :rows, :]
    s.small[1:2, :] = jnp.sum(grad_value.astype(F32), 0, keepdims=True)

    def sum_copy(stage, to):
        return remote(
            s.small if stage == 0 else s.sums.at[stage - 1],
            s.got_sums.at[stage],
            s.sum_send.at[stage],
            s.sum_recv.at[stage],
            to,
        )

    sum_copies = [
        sum_copy(stage, to) for stage, to in enumerate((place.mate, place.across, place.along))
    ]
    sum_copies[0].start()
    for unit in (10, 11):
        grads.right_copy(unit - 3).wait_recv()
        grads.multiply(unit)
    sum_copies[0].wait_recv()
    s.sums[0] = s.small[...] + s.got_sums[0]
    sum_copies[1].start()
    grads.pass_on(9)
    grad_input = (
        s.grad_res[...]
        + dot_nt(s.right[6, :rows, :], s.weight_a[2 * width : 3 * width, :])
        + dot_nt(s.right[7, :rows, :], s.weight_a[:width, :])
        + dot_nt(grad_value, s.weight_a[width : 2 * width, :])
    )
    send_back(1, grad_input.astype(BF16))
    grads.pass_on(10)
    grads.pass_on(11)
    sum_copies[1].wait_recv()
    s.sums[1] = s.sums[0] + s.got_sums[1]
    sum_copies[2].start()
    grads.gather(9)
    grads.hop(9, 0)
    grads.hop(8, 1)
    grads.hop(7, 2)
    grads.finish(6)
    grads.gather(10)
    sum_copies[2].wait_recv()
    s.sums[2] = s.sums[1] + s.got_sums[2]

    def z_copy(step):
        other = (place.z + step) % z_size
        return remote(
            s.sums.at[2],
            s.got_z.at[place.z],
            s.sum_send.at[2 + step],
            s.sum_recv.at[2 + step],
            {"ctx": other},
        )

    for step in range(1, z_size):
        z_copy(step).start()
    s.got_z[place.z] = s.sums[2]
    take_back(0)
    grads.hop(10, 0)
    grads.hop(9, 1)
    grads.hop(8, 2)
    grads.finish(7)
    grads.gather(11)
    grads.hop(11, 0)
    grads.hop(10, 1)
    grads.hop(9, 2)
    grads.finish(8)
    take_back(1)
    home_copy = pltpu.make_async_copy(s.homes, out_homes, s.probs_sem.at[0])
    home_copy.start()
    grads.hop(11, 1)
    grads.hop(10, 2)
    grads.finish(9)
    for step in range(1, z_size):
        z_copy(step).wait_recv()
    total = s.got_z[0]
    for z in range(1, z_size):
        total = total + s.got_z[z]
    out_small[...] = total
    grads.hop(11, 2)
    grads.finish(10)
    grads.finish(11)

    grads.drain(lefts)
    for pair in range(pairs):
        for kind in range(3):
            kv_copy(pair, kind).wait_send()
    for which in range(2):
        each_other(route.home, lambda other: back_copy(which, other).wait_send())
    for copy in sum_copies:
        copy.wait_send()
    for step in range(1, z_size):
        z_copy(step).wait_send()
    home_copy.wait()


def encoder_backward(z_size, kept):
    rows, width = kept.query.shape
    blocks = 8 * z_size
    scratch = {name: make(rows, width, blocks) for name, make in BACKWARD_SCRATCH.items()}
    vmem, anywhere = pl.BlockSpec(memory_space=pltpu.VMEM), pl.BlockSpec(memory_space=pl.ANY)
    return pl.pallas_call(
        partial(backward_kernel, z_size),
        out_shape=(
            jax.ShapeDtypeStruct((UNITS, BLOCK, width), F32),
            jax.ShapeDtypeStruct((2, rows, width), BF16),
            jax.ShapeDtypeStruct((16, width), F32),
        ),
        in_specs=[anywhere] * len(Kept._fields),
        out_specs=(anywhere, anywhere, vmem),
        scratch_shapes=list(scratch.values()),
        compiler_params=pltpu.CompilerParams(
            collective_id=1, has_side_effects=True, vmem_limit_bytes=62 * 2**20
        ),
        name="encoder_backward",
    )(*kept)


norm_eps = 1e-12
floor_score = -1e30
masked_score = -1e32


def product(left, right):
    return jnp.dot(left, right, preferred_element_type=jnp.float32)


def inner_rows(left, right):
    return lax.dot_general(
        left, right, (((0,), (0,)), ((), ())), preferred_element_type=jnp.float32
    )


def against(left, right):
    return lax.dot_general(
        left, right, (((1,), (1,)), ((), ())), preferred_element_type=jnp.float32
    )


def layer_norm(value, gain, shift):
    centre = value - jnp.mean(value, -1, keepdims=True)
    spread = jnp.mean(centre * centre, -1, keepdims=True)
    inverse_dev = lax.rsqrt(spread + norm_eps)
    scaled = centre * inverse_dev
    return (scaled * gain + shift, scaled, inverse_dev)


def norm_back(grad_norm, scaled, inverse_dev, gain):
    grad_scaled = grad_norm * gain
    centred = grad_scaled - jnp.mean(grad_scaled, -1, keepdims=True)
    return inverse_dev * (centred - scaled * jnp.mean(grad_scaled * scaled, -1, keepdims=True))


def per_device(
    tokens,
    cotangent,
    token_order,
    sequence_ids,
    valid,
    teacher,
    w_query,
    b_query,
    w_key,
    w_value,
    b_value,
    w_out,
    b_out,
    norm1_gain,
    norm1_bias,
    w_up,
    b_up,
    w_down,
    b_down,
    norm2_gain,
    norm2_bias,
):
    tok_rows, model_width = tokens.shape
    peer_count = lax.axis_size(("dp", "ctx"))
    per_peer = tok_rows // peer_count
    head_count = HEADS
    head_size = model_width // head_count
    score_scale = head_size ** (-0.5)
    gelu_exact = partial(jax.nn.gelu, approximate=False)
    positions = lax.iota(jnp.int32, tok_rows)
    source = token_order // tok_rows
    slot_sort = jnp.argsort(source * tok_rows + positions)
    requests = (token_order[slot_sort] % tok_rows).reshape(peer_count, per_peer)
    wanted = lax.all_to_all(requests, ("dp", "ctx"), split_axis=0, concat_axis=0, tiled=True)
    wanted_flat = wanted.reshape(tok_rows)
    packed_x, packed_cot = (
        lax.all_to_all(
            tokens[wanted_flat].reshape(peer_count, per_peer, model_width),
            ("dp", "ctx"),
            split_axis=0,
            concat_axis=0,
            tiled=True,
        ),
        lax.all_to_all(
            cotangent[wanted_flat].reshape(peer_count, per_peer, model_width),
            ("dp", "ctx"),
            split_axis=0,
            concat_axis=0,
            tiled=True,
        ),
    )
    arrival = jnp.argsort(slot_sort)
    inputs = packed_x.reshape(tok_rows, model_width)[arrival]
    cot_rows = packed_cot.reshape(tok_rows, model_width)[arrival].astype(jnp.float32)
    valid_rows = valid.astype(jnp.float32)
    valid_count = lax.psum(jnp.sum(valid_rows), ("dp", "ctx"))
    (
        query_weight,
        query_bias,
        key_weight,
        value_weight,
        value_bias,
        out_weight,
        out_bias,
        gain_one,
        shift_one,
        up_weight,
        up_bias,
        down_weight,
        down_bias,
        gain_two,
        shift_two,
    ) = (
        lax.all_gather(w_query, "dp", axis=0, tiled=True),
        lax.all_gather(b_query, "dp", axis=0, tiled=True),
        lax.all_gather(w_key, "dp", axis=0, tiled=True),
        lax.all_gather(w_value, "dp", axis=0, tiled=True),
        lax.all_gather(b_value, "dp", axis=0, tiled=True),
        lax.all_gather(w_out, "dp", axis=0, tiled=True),
        lax.all_gather(b_out, "dp", axis=0, tiled=True),
        lax.all_gather(norm1_gain, "dp", axis=0, tiled=True),
        lax.all_gather(norm1_bias, "dp", axis=0, tiled=True),
        lax.all_gather(w_up, "dp", axis=0, tiled=True),
        lax.all_gather(b_up, "dp", axis=0, tiled=True),
        lax.all_gather(w_down, "dp", axis=0, tiled=True),
        lax.all_gather(b_down, "dp", axis=0, tiled=True),
        lax.all_gather(norm2_gain, "dp", axis=0, tiled=True),
        lax.all_gather(norm2_bias, "dp", axis=0, tiled=True),
    )
    queries = (product(inputs, query_weight) + query_bias).astype(jnp.bfloat16)
    key_rows = product(inputs, key_weight).astype(jnp.bfloat16)
    values = (product(inputs, value_weight) + value_bias).astype(jnp.bfloat16)
    group_ids = sequence_ids.reshape(-1)
    cycle_index = lax.axis_index("ctx")
    query_ids = lax.dynamic_slice_in_dim(group_ids, cycle_index * tok_rows, tok_rows)
    query_heads = queries.reshape(tok_rows, head_count, head_size)
    initial = (
        jnp.full((head_count, tok_rows), floor_score, jnp.float32),
        jnp.zeros((head_count, tok_rows), jnp.float32),
        jnp.zeros((tok_rows, head_count, head_size), jnp.float32),
    )
    folded = initial
    key_piece = lax.all_gather(key_rows, "ctx", axis=0, tiled=True)
    value_piece = lax.all_gather(values, "ctx", axis=0, tiled=True)
    length = key_piece.shape[0]
    attend_block_rows = math.gcd(length, 512)
    block_count = length // attend_block_rows

    def one_block(carried, inputs_block):
        running_max, running_sum, summed = carried
        key_block, value_block, key_start = inputs_block
        key_ids = lax.dynamic_slice_in_dim(group_ids, key_start, attend_block_rows)
        scores = (
            jnp.einsum("qhd,khd->hqk", query_heads, key_block, preferred_element_type=jnp.float32)
            * score_scale
        )
        scores = jnp.where((query_ids[:, None] == key_ids[None, :])[None], scores, masked_score)
        new_max = jnp.maximum(running_max, jnp.max(scores, -1))
        factor = jnp.exp(running_max - new_max)
        weights = jnp.exp(scores - new_max[:, :, None])
        running_sum = running_sum * factor + jnp.sum(weights, -1)
        update = jnp.einsum(
            "hqk,khd->qhd",
            weights.astype(jnp.bfloat16),
            value_block,
            preferred_element_type=jnp.float32,
        )
        summed = summed * jnp.transpose(factor)[:, :, None] + update
        return ((new_max, running_sum, summed), None)

    key_starts = attend_block_rows * lax.iota(jnp.int32, block_count)
    folded, _ = lax.scan(
        one_block,
        folded,
        (
            key_piece.reshape(block_count, attend_block_rows, head_count, head_size),
            value_piece.reshape(block_count, attend_block_rows, head_count, head_size),
            key_starts,
        ),
    )
    running_max, running_sum, summed = folded
    attended = summed / jnp.transpose(running_sum)[:, :, None]
    log_total = running_max + jnp.log(running_sum)
    context = attended.reshape(tok_rows, model_width).astype(jnp.bfloat16)
    branch = product(context, out_weight) + out_bias
    normed, scaled_one, inverse_one = layer_norm(
        inputs.astype(jnp.float32) + branch, gain_one, shift_one
    )
    normed_low = normed.astype(jnp.bfloat16)
    pre_act = product(normed_low, up_weight) + up_bias
    activated = gelu_exact(pre_act).astype(jnp.bfloat16)
    ffn_out = product(activated, down_weight) + down_bias
    result, scaled_two, inverse_two = layer_norm(normed + ffn_out, gain_two, shift_two)
    difference = result - teacher
    loss_total = lax.psum(jnp.sum(valid_rows[:, None] * difference * difference), ("dp", "ctx"))
    loss_value = loss_total / (valid_count * model_width)
    grad_out = cot_rows + 2.0 / (valid_count * model_width) * valid_rows[:, None] * difference
    grad_gain_two = jnp.sum(grad_out * scaled_two, 0)
    grad_shift_two = jnp.sum(grad_out, 0)
    grad_res_two = norm_back(grad_out, scaled_two, inverse_two, gain_two)
    grad_ffn = grad_res_two.astype(jnp.bfloat16)
    grad_down = inner_rows(activated, grad_ffn)
    grad_down_bias = jnp.sum(grad_ffn.astype(jnp.float32), 0)
    grad_act = against(grad_ffn, down_weight)
    _, gelu_pull = jax.vjp(gelu_exact, pre_act)
    grad_pre = gelu_pull(grad_act)[0].astype(jnp.bfloat16)
    grad_up = inner_rows(normed_low, grad_pre)
    grad_up_bias = jnp.sum(grad_pre.astype(jnp.float32), 0)
    grad_normed = grad_res_two + against(grad_pre, up_weight)
    ffn_shards = (
        lax.psum_scatter(
            grad_up.astype(jnp.bfloat16), "dp", scatter_dimension=0, tiled=True
        ).astype(jnp.float32),
        lax.psum_scatter(
            grad_up_bias.astype(jnp.bfloat16), "dp", scatter_dimension=0, tiled=True
        ).astype(jnp.float32),
        lax.psum_scatter(
            grad_down.astype(jnp.bfloat16), "dp", scatter_dimension=0, tiled=True
        ).astype(jnp.float32),
        lax.psum_scatter(
            grad_down_bias.astype(jnp.bfloat16), "dp", scatter_dimension=0, tiled=True
        ).astype(jnp.float32),
        lax.psum_scatter(
            grad_gain_two.astype(jnp.bfloat16), "dp", scatter_dimension=0, tiled=True
        ).astype(jnp.float32),
        lax.psum_scatter(
            grad_shift_two.astype(jnp.bfloat16), "dp", scatter_dimension=0, tiled=True
        ).astype(jnp.float32),
    )
    grad_gain_one = jnp.sum(grad_normed * scaled_one, 0)
    grad_shift_one = jnp.sum(grad_normed, 0)
    grad_res_one = norm_back(grad_normed, scaled_one, inverse_one, gain_one)
    grad_branch = grad_res_one.astype(jnp.bfloat16)
    grad_out_w = inner_rows(context, grad_branch)
    grad_out_bias = jnp.sum(grad_branch.astype(jnp.float32), 0)
    grad_context = against(grad_branch, out_weight).astype(jnp.bfloat16)
    grad_heads = grad_context.reshape(tok_rows, head_count, head_size)
    delta = jnp.transpose(jnp.sum(grad_heads.astype(jnp.float32) * attended, -1))
    all_keys, all_values = (
        lax.all_gather(key_rows, "ctx", axis=0, tiled=True),
        lax.all_gather(values, "ctx", axis=0, tiled=True),
    )
    group_len = all_keys.shape[0]
    block_rows = math.gcd(group_len, 512)
    block_count = group_len // block_rows
    key_starts = block_rows * lax.iota(jnp.int32, block_count)
    key_blocks = all_keys.reshape(block_count, block_rows, head_count, head_size)
    value_blocks = all_values.reshape(block_count, block_rows, head_count, head_size)

    def query_side(key_block, value_block, key_start):
        key_ids = lax.dynamic_slice_in_dim(group_ids, key_start, block_rows)
        scores = (
            jnp.einsum("qhd,khd->hqk", query_heads, key_block, preferred_element_type=jnp.float32)
            * score_scale
        )
        scores = jnp.where((query_ids[:, None] == key_ids[None, :])[None], scores, masked_score)
        probs = jnp.exp(scores - log_total[:, :, None])
        grad_probs = jnp.einsum(
            "qhd,khd->hqk", grad_heads, value_block, preferred_element_type=jnp.float32
        )
        grad_scores = (probs * (grad_probs - delta[:, :, None])).astype(jnp.bfloat16)
        return (probs, grad_scores)

    def back_block(grad_query, inputs_block):
        key_block, value_block, key_start = inputs_block
        probs, grad_scores = query_side(key_block, value_block, key_start)
        grad_query = (
            grad_query
            + jnp.einsum("hqk,khd->qhd", grad_scores, key_block, preferred_element_type=jnp.float32)
            * score_scale
        )
        grad_key = (
            jnp.einsum("hqk,qhd->khd", grad_scores, query_heads, preferred_element_type=jnp.float32)
            * score_scale
        )
        grad_value = jnp.einsum(
            "hqk,qhd->khd",
            probs.astype(jnp.bfloat16),
            grad_heads,
            preferred_element_type=jnp.float32,
        )
        return (grad_query, (grad_key, grad_value))

    grad_query, (key_parts, value_parts) = lax.scan(
        back_block,
        jnp.zeros((tok_rows, head_count, head_size), jnp.float32),
        (key_blocks, value_blocks, key_starts),
    )
    key_total, value_total = (
        lax.psum_scatter(
            key_parts.reshape(group_len, model_width).astype(jnp.bfloat16),
            "ctx",
            scatter_dimension=0,
            tiled=True,
        ).astype(jnp.float32),
        lax.psum_scatter(
            value_parts.reshape(group_len, model_width).astype(jnp.bfloat16),
            "ctx",
            scatter_dimension=0,
            tiled=True,
        ).astype(jnp.float32),
    )
    grad_keys = key_total.astype(jnp.bfloat16)
    grad_values = value_total.astype(jnp.bfloat16)
    grad_queries = grad_query.reshape(tok_rows, model_width).astype(jnp.bfloat16)
    grad_query_w = inner_rows(inputs, grad_queries)
    grad_query_bias = jnp.sum(grad_queries.astype(jnp.float32), 0)
    grad_key_w = inner_rows(inputs, grad_keys)
    grad_value_w = inner_rows(inputs, grad_values)
    grad_value_bias = jnp.sum(grad_values.astype(jnp.float32), 0)
    grad_inputs = (
        grad_res_one
        + against(grad_queries, query_weight)
        + against(grad_keys, key_weight)
        + against(grad_values, value_weight)
    )
    attn_shards = (
        lax.psum_scatter(
            grad_query_w.astype(jnp.bfloat16), "dp", scatter_dimension=0, tiled=True
        ).astype(jnp.float32),
        lax.psum_scatter(
            grad_query_bias.astype(jnp.bfloat16), "dp", scatter_dimension=0, tiled=True
        ).astype(jnp.float32),
        lax.psum_scatter(
            grad_key_w.astype(jnp.bfloat16), "dp", scatter_dimension=0, tiled=True
        ).astype(jnp.float32),
        lax.psum_scatter(
            grad_value_w.astype(jnp.bfloat16), "dp", scatter_dimension=0, tiled=True
        ).astype(jnp.float32),
        lax.psum_scatter(
            grad_value_bias.astype(jnp.bfloat16), "dp", scatter_dimension=0, tiled=True
        ).astype(jnp.float32),
        lax.psum_scatter(
            grad_out_w.astype(jnp.bfloat16), "dp", scatter_dimension=0, tiled=True
        ).astype(jnp.float32),
        lax.psum_scatter(
            grad_out_bias.astype(jnp.bfloat16), "dp", scatter_dimension=0, tiled=True
        ).astype(jnp.float32),
        lax.psum_scatter(
            grad_gain_one.astype(jnp.bfloat16), "dp", scatter_dimension=0, tiled=True
        ).astype(jnp.float32),
        lax.psum_scatter(
            grad_shift_one.astype(jnp.bfloat16), "dp", scatter_dimension=0, tiled=True
        ).astype(jnp.float32),
    )
    totals = (
        lax.psum(attn_shards[0].astype(jnp.bfloat16), "ctx").astype(jnp.float32),
        lax.psum(attn_shards[1].astype(jnp.bfloat16), "ctx").astype(jnp.float32),
        lax.psum(attn_shards[2].astype(jnp.bfloat16), "ctx").astype(jnp.float32),
        lax.psum(attn_shards[3].astype(jnp.bfloat16), "ctx").astype(jnp.float32),
        lax.psum(attn_shards[4].astype(jnp.bfloat16), "ctx").astype(jnp.float32),
        lax.psum(attn_shards[5].astype(jnp.bfloat16), "ctx").astype(jnp.float32),
        lax.psum(attn_shards[6].astype(jnp.bfloat16), "ctx").astype(jnp.float32),
        lax.psum(attn_shards[7].astype(jnp.bfloat16), "ctx").astype(jnp.float32),
        lax.psum(attn_shards[8].astype(jnp.bfloat16), "ctx").astype(jnp.float32),
        lax.psum(ffn_shards[0].astype(jnp.bfloat16), "ctx").astype(jnp.float32),
        lax.psum(ffn_shards[1].astype(jnp.bfloat16), "ctx").astype(jnp.float32),
        lax.psum(ffn_shards[2].astype(jnp.bfloat16), "ctx").astype(jnp.float32),
        lax.psum(ffn_shards[3].astype(jnp.bfloat16), "ctx").astype(jnp.float32),
        lax.psum(ffn_shards[4].astype(jnp.bfloat16), "ctx").astype(jnp.float32),
        lax.psum(ffn_shards[5].astype(jnp.bfloat16), "ctx").astype(jnp.float32),
    )
    back_out, back_grad = (
        lax.all_to_all(
            result[slot_sort].reshape(peer_count, per_peer, model_width).astype(jnp.bfloat16),
            ("dp", "ctx"),
            split_axis=0,
            concat_axis=0,
            tiled=True,
        ).astype(jnp.float32),
        lax.all_to_all(
            grad_inputs[slot_sort].reshape(peer_count, per_peer, model_width).astype(jnp.bfloat16),
            ("dp", "ctx"),
            split_axis=0,
            concat_axis=0,
            tiled=True,
        ).astype(jnp.float32),
    )
    homeward = jnp.argsort(wanted_flat)
    output = back_out.reshape(tok_rows, model_width)[homeward]
    input_grad = back_grad.reshape(tok_rows, model_width)[homeward]
    return (
        output,
        loss_value,
        input_grad,
        totals[0],
        totals[1],
        totals[2],
        totals[3],
        totals[4],
        totals[5],
        totals[6],
        totals[7],
        totals[8],
        totals[9],
        totals[10],
        totals[11],
        totals[12],
        totals[13],
        totals[14],
    )


def per_device_fast(
    tokens,
    cotangent,
    token_order,
    sequence_ids,
    valid,
    teacher,
    w_query,
    b_query,
    w_key,
    w_value,
    b_value,
    w_out,
    b_out,
    norm1_gain,
    norm1_bias,
    w_up,
    b_up,
    w_down,
    b_down,
    norm2_gain,
    norm2_bias,
):
    rows, width = tokens.shape
    z_size = lax.axis_size("ctx")
    ints = jnp.stack([token_order, valid])
    ids = sequence_ids.reshape(z_size, 1, rows)
    narrow = jnp.stack(
        [b_query, b_value, b_out, norm1_gain, norm1_bias, b_down, norm2_gain, norm2_bias]
    )
    pieces = jnp.concatenate(
        [
            jnp.pad(narrow, ((0, 0), (0, 3 * BLOCK))),
            b_up[None],
            jnp.zeros((7, 4 * BLOCK), BF16),
        ]
    )
    kept = encoder_forward(
        z_size,
        ints,
        ids,
        tokens,
        cotangent,
        teacher,
        pieces,
        w_query,
        w_key,
        w_value,
        w_out,
        w_up,
        w_down,
    )
    grads, homes, small = encoder_backward(z_size, kept)
    dp_index = lax.axis_index("dp")
    own = lax.dynamic_slice_in_dim(small[:8], dp_index * BLOCK, BLOCK, axis=1)
    own_up = lax.dynamic_slice_in_dim(
        small[8:12].reshape(-1), dp_index * 4 * BLOCK, 4 * BLOCK
    )
    homes = homes.astype(F32)
    return (
        homes[0],
        jnp.sum(small[12]),
        homes[1],
        grads[9],
        own[0],
        grads[10],
        grads[11],
        own[1],
        grads[8],
        own[2],
        own[3],
        own[4],
        jnp.concatenate(list(grads[4:8]), axis=1),
        own_up,
        grads[:4].reshape(4 * BLOCK, width),
        own[5],
        own[6],
        own[7],
    )


def solution(mesh):
    in_specs = (
        P(("dp", "ctx"), None),
        P(("dp", "ctx"), None),
        P(("dp", "ctx")),
        P("dp", None),
        P(("dp", "ctx")),
        P(("dp", "ctx"), None),
        P("dp", None),
        P("dp"),
        P("dp", None),
        P("dp", None),
        P("dp"),
        P("dp", None),
        P("dp"),
        P("dp"),
        P("dp"),
        P("dp", None),
        P("dp"),
        P("dp", None),
        P("dp"),
        P("dp"),
        P("dp"),
    )
    out_specs = (
        P(("dp", "ctx"), None),
        P(),
        P(("dp", "ctx"), None),
        P("dp", None),
        P("dp"),
        P("dp", None),
        P("dp", None),
        P("dp"),
        P("dp", None),
        P("dp"),
        P("dp"),
        P("dp"),
        P("dp", None),
        P("dp"),
        P("dp", None),
        P("dp"),
        P("dp"),
        P("dp"),
    )
    fast = dict(mesh.shape) == {"dp": 8, "ctx": 4}
    return jax.shard_map(
        per_device_fast if fast else per_device, mesh=mesh, in_specs=in_specs, out_specs=out_specs, check_vma=False
    )
```

```python
import math
from functools import partial
from types import SimpleNamespace
from typing import NamedTuple

import jax
import jax.numpy as jnp
from jax import lax
from jax.experimental import pallas as pl
from jax.experimental.pallas import tpu as pltpu
from jax.sharding import PartitionSpec as P

MESH = pl.DeviceIdType.MESH
F32, BF16 = jnp.float32, jnp.bfloat16


class Place:
    def __init__(self, z_size):
        dp, z = lax.axis_index("dp"), lax.axis_index("ctx")
        self.dp, self.z, self.z_size = dp, z, z_size
        core, x, y = dp % 2, dp // 2 % 2, dp // 4
        self.core = core
        self.mate = {"dp": dp + 1 - 2 * core}
        self.across = {"dp": dp + 2 - 4 * x}
        self.along = {"dp": dp + 4 - 8 * y}
        self.j_own = y * 2 + x
        self.j_x = y * 2 + 1 - x
        self.j_y = (1 - y) * 2 + x
        self.j_d = (1 - y) * 2 + 1 - x


def remote(src, dst, send, recv, to):
    return pltpu.make_async_remote_copy(
        src_ref=src, dst_ref=dst, send_sem=send, recv_sem=recv, device_id=to, device_id_type=MESH
    )


UNITS = 12
BLOCK = 96


class Route:
    def __init__(self, z_size):
        place = Place(z_size)
        self.place = place
        dp, z, core = place.dp, place.z, place.core
        self.blocks = 8 * z_size
        self.home = dp * z_size + z
        self.group_core = z // 2
        self.quarter = 2 * (z % 2) + core
        self.block = (dp - core + self.group_core) * z_size + self.quarter
        self.mate_quarter = self.quarter + 1 - 2 * core
        self.pair_quarter = self.quarter + 2 - 4 * (z % 2)
        self.far_quarter = self.pair_quarter + 1 - 2 * core
        self.pair = {"ctx": z + 1 - 2 * (z % 2)}

    def worker(self, block):
        group, quarter = block // self.place.z_size, block % self.place.z_size
        return {"dp": group - group % 2 + quarter % 2, "ctx": 2 * (group % 2) + quarter // 2}

    def owner(self, block):
        return {"dp": block // self.place.z_size, "ctx": block % self.place.z_size}

    def greet_all(self):
        barrier = pltpu.get_barrier_semaphore()

        def signal(step, carry):
            other = (self.home + step) % self.blocks
            pl.semaphore_signal(
                barrier, inc=1, device_id=self.owner(other), device_id_type=MESH
            )
            return carry

        lax.fori_loop(1, self.blocks, signal, 0)
        pl.semaphore_wait(barrier, self.blocks - 1)


def shard_rows(unit, shard, width):
    start = width * unit + BLOCK * shard
    start = start + unit // 8 * (3 * BLOCK * shard - (width - BLOCK) * (unit - 8))
    return pl.multiple_of(start, 32)


class Weights:
    def __init__(self, place, full, send, recv):
        self.place, self.full, self.send, self.recv = place, full, send, recv
        self.width = full.shape[1]

    def at(self, unit, shard, first=0, count=BLOCK):
        start = shard_rows(unit, shard, self.width)
        return self.full.at[pl.ds(pl.multiple_of(start + first, 16), count), :]

    def copy(self, unit, kind, arriving):
        place = self.place
        own, across, along = place.dp, place.across["dp"], place.along["dp"]
        corner = across + along - own
        half = BLOCK // 2
        mate = place.mate["dp"] - own
        shard, first, count, to = (
            (own, 0, BLOCK, place.across),
            (own, 0, BLOCK, place.along),
            (own, 0, BLOCK, place.mate),
            (across, 0, half, place.along),
            (along, half, half, place.across),
            (across, 0, BLOCK, place.mate),
            (along, 0, BLOCK, place.mate),
            (corner, 0, BLOCK, place.mate),
        )[kind]
        if arriving:
            shard = (across, along, own + mate, corner, corner, across + mate, along + mate, corner + mate)[kind]
        ref = self.at(unit, shard, first, count)
        return remote(ref, ref, self.send.at[unit, kind], self.recv.at[unit, kind], to)

    def begin(self, unit):
        for kind in (0, 1, 2):
            self.copy(unit, kind, False).start()

    def pass_on(self, unit):
        self.copy(unit, 0, True).wait_recv()
        self.copy(unit, 3, False).start()
        self.copy(unit, 5, False).start()
        self.copy(unit, 1, True).wait_recv()
        self.copy(unit, 4, False).start()
        self.copy(unit, 6, False).start()

    def corner(self, unit):
        self.copy(unit, 3, True).wait_recv()
        self.copy(unit, 4, True).wait_recv()
        self.copy(unit, 7, False).start()

    def tick(self, step):
        self.begin(step)
        self.pass_on(step - 2)
        if not isinstance(step, int) or step >= 3:
            self.corner(step - 3)

    def ready(self, unit):
        for kind in (2, 5, 6, 7):
            self.copy(unit, kind, True).wait_recv()

    def drain(self):
        def one(unit, carry):
            for kind in range(8):
                self.copy(unit, kind, False).wait_send()
            return carry

        lax.fori_loop(0, UNITS, one, 0)


def iota(shape, axis):
    return lax.broadcasted_iota(jnp.int32, shape, axis)


def column(row):
    n = row.shape[1]
    return jnp.sum(jnp.where(iota((n, n), 0) == iota((n, n), 1), row, 0.0), 1, keepdims=True)


def dot(left, right):
    return jnp.dot(left, right, preferred_element_type=F32)


def dot_nt(left, right):
    return lax.dot_general(
        left, right, (((1,), (1,)), ((), ())), preferred_element_type=F32
    )


def one_hot(condition):
    return jnp.where(condition, 1.0, 0.0).astype(BF16)


FORWARD_SCRATCH = dict(
    ints=lambda t, w, b: pltpu.VMEM((b, 2, t), jnp.int32),
    order=lambda t, w, b: pltpu.VMEM((b, t), jnp.int32),
    ids=lambda t, w, b: pltpu.VMEM((2, 4, 1, t), jnp.int32),
    pieces=lambda t, w, b: pltpu.VMEM((8, 16, w // 2), BF16),
    vectors=lambda t, w, b: pltpu.VMEM((16, w), F32),
    pack_out=lambda t, w, b: pltpu.VMEM((2, b, t // b, w), BF16),
    pack_in=lambda t, w, b: pltpu.VMEM((2, b, t // b, w), BF16),
    teach_out=lambda t, w, b: pltpu.VMEM((t, w), BF16),
    teach_in=lambda t, w, b: pltpu.VMEM((t, w), BF16),
    full=lambda t, w, b: pltpu.VMEM((12 * w, w), BF16),
    packed=lambda t, w, b: pltpu.VMEM((4, t, w), BF16),
    packed_t=lambda t, w, b: pltpu.VMEM((2, w, t), BF16),
    query=lambda t, w, b: pltpu.VMEM((t, w), BF16),
    keys=lambda t, w, b: pltpu.VMEM((4, t, w), BF16),
    values_t=lambda t, w, b: pltpu.VMEM((4, w, t), BF16),
    mask=lambda t, w, b: pltpu.VMEM((4, t, t), F32),
    scores=lambda t, w, b: pltpu.VMEM((2, 4, t, t), F32),
    probs=lambda t, w, b: pltpu.VMEM((HEADS, 4, t, t), BF16),
    keys_t=lambda t, w, b: pltpu.VMEM((4, w, t), BF16),
    values=lambda t, w, b: pltpu.VMEM((4, t, w), BF16),
    context_t=lambda t, w, b: pltpu.VMEM((w, t), BF16),
    scaled=lambda t, w, b: pltpu.VMEM((t, w), F32),
    inverse=lambda t, w, b: pltpu.VMEM((t, 128), F32),
    normed=lambda t, w, b: pltpu.VMEM((t, w), F32),
    low=lambda t, w, b: pltpu.VMEM((t, w), BF16),
    low_t=lambda t, w, b: pltpu.VMEM((w, t), BF16),
    act=lambda t, w, b: pltpu.VMEM((t, 4 * w), BF16),
    act_t=lambda t, w, b: pltpu.VMEM((4 * w, t), BF16),
    slope=lambda t, w, b: pltpu.VMEM((t, 4 * w), BF16),
    result=lambda t, w, b: pltpu.VMEM((t, w), BF16),
    grad_res=lambda t, w, b: pltpu.VMEM((t, w), F32),
    grad_ffn=lambda t, w, b: pltpu.VMEM((t, w), BF16),
    small=lambda t, w, b: pltpu.VMEM((16, w), F32),
    routes=lambda t, w, b: pltpu.VMEM((8, t), F32),
    ints_send=lambda t, w, b: pltpu.SemaphoreType.DMA((b,)),
    ints_recv=lambda t, w, b: pltpu.SemaphoreType.DMA((b,)),
    piece_send=lambda t, w, b: pltpu.SemaphoreType.DMA((8,)),
    piece_recv=lambda t, w, b: pltpu.SemaphoreType.DMA((8,)),
    pack_send=lambda t, w, b: pltpu.SemaphoreType.DMA((2, b)),
    pack_recv=lambda t, w, b: pltpu.SemaphoreType.DMA((2, b)),
    misc_send=lambda t, w, b: pltpu.SemaphoreType.DMA((8,)),
    misc_recv=lambda t, w, b: pltpu.SemaphoreType.DMA((8,)),
    weight_send=lambda t, w, b: pltpu.SemaphoreType.DMA((UNITS, 8)),
    weight_recv=lambda t, w, b: pltpu.SemaphoreType.DMA((UNITS, 8)),
    own_sem=lambda t, w, b: pltpu.SemaphoreType.DMA((UNITS,)),
    store_sem=lambda t, w, b: pltpu.SemaphoreType.DMA((32,)),
)

class Kept(NamedTuple):
    full: object
    probs: object
    keys_t: object
    values: object
    packed_t: object
    query: object
    context_t: object
    scaled: object
    inverse: object
    low_t: object
    act_t: object
    slope: object
    result: object
    grad_res: object
    grad_ffn: object
    small: object
    routes: object


HEADS = 12
NORM_EPS = 1e-12


def normalize(value):
    centre = value - jnp.mean(value, -1, keepdims=True)
    spread = jnp.mean(centre * centre, -1, keepdims=True)
    inverse = lax.rsqrt(spread + NORM_EPS)
    return centre * inverse, inverse


def forward_kernel(z_size, ints, ids, tokens, cotangent, teacher, pieces, w_query, w_key, w_value, w_out, w_up, w_down, *refs):
    outs = Kept(*refs[: len(Kept._fields)])
    s = SimpleNamespace(**dict(zip(FORWARD_SCRATCH, refs[len(Kept._fields) :])))
    route = Route(z_size)
    place = route.place
    rows, width = tokens.shape
    blocks = route.blocks
    full = s.full
    weights = Weights(place, full, s.weight_send, s.weight_recv)
    stores = []

    def keep(source, target):
        copy = pltpu.make_async_copy(source, target, s.store_sem.at[len(stores)])
        copy.start()
        stores.append(copy)

    sources = (
        [w_key, w_value, w_query, w_out]
        + [w_up.at[:, width * i : width * (i + 1)] for i in range(4)]
        + [w_down.at[BLOCK * i : BLOCK * (i + 1), :] for i in range(4)]
    )
    own_copies = [
        pltpu.make_async_copy(source, weights.at(unit, place.dp), s.own_sem.at[unit])
        for unit, source in enumerate(sources)
    ]
    for copy in own_copies:
        copy.start()
    s.ints[route.home] = ints[...]
    s.teach_out[...] = teacher[...].astype(BF16)
    route.greet_all()

    def ints_copy(other):
        return remote(
            ints,
            s.ints.at[route.home],
            s.ints_send.at[other],
            s.ints_recv.at[route.home],
            route.owner(other),
        )

    def ints_arrival(other):
        ref = s.ints.at[other]
        return remote(ref, ref, s.ints_send.at[other], s.ints_recv.at[other], route.owner(other))

    def each_other(start, action):
        def one(step, carry):
            action((start + step) % blocks)
            return carry

        lax.fori_loop(1, blocks, one, 0)

    each_other(route.home, lambda other: ints_copy(other).start())
    def piece_copy(step):
        other = (place.dp + step) % 8
        return remote(
            pieces,
            s.pieces.at[place.dp],
            s.piece_send.at[step],
            s.piece_recv.at[step],
            {"dp": other},
        )

    for step in range(1, 8):
        piece_copy(step).start()
    s.pieces[place.dp] = pieces[...]
    ids_copy = remote(ids, s.ids.at[1], s.misc_send.at[0], s.misc_recv.at[0], place.mate)
    ids_copy.start()
    s.ids[0] = ids[...]
    for copy in own_copies[:2]:
        copy.wait()
    weights.begin(0)
    weights.begin(1)
    for copy in own_copies[2:]:
        copy.wait()

    each_other(route.home, lambda other: ints_arrival(other).wait_recv())
    count = jnp.zeros((1, rows), F32)
    for other in range(blocks):
        s.order[other : other + 1, :] = s.ints[other, 0:1, :]
        count = count + s.ints[other, 1:2, :].astype(F32)
    count = jnp.sum(count, 1, keepdims=True)
    order = s.order[...]
    source = lax.shift_right_logical(order, 8)
    local = (order - source * rows).astype(F32)
    mine = source == route.home
    earlier = one_hot(iota((rows, rows), 0) < iota((rows, rows), 1))
    rank = dot(one_hot(mine), earlier)
    per_block = rows // blocks
    slots = jnp.zeros((blocks, 128), F32)
    for k in range(per_block):
        picked = jnp.sum(jnp.where(mine & (rank == k), local, 0.0), 1, keepdims=True)
        slots = jnp.where(iota((blocks, 128), 1) == k, picked, slots)
    spread = one_hot(
        lax.shift_right_logical(iota((rows, blocks), 0), 3) == iota((rows, blocks), 1)
    )
    picked = jnp.sum(
        jnp.where(
            iota((rows, 128), 1) == (iota((rows, 128), 0) & 7),
            dot(spread, slots.astype(BF16)),
            0.0,
        ),
        1,
        keepdims=True,
    )
    lane = iota((rows, rows), 1)
    diagonal = iota((rows, rows), 0) == lane
    ordered = one_hot(lane.astype(F32) == picked)

    def pack_copy(which, block):
        return remote(
            s.pack_out.at[which, block],
            s.pack_in.at[which, route.home],
            s.pack_send.at[which, block],
            s.pack_recv.at[which, route.home],
            route.worker(block),
        )

    def pack_arrival(which, other):
        ref = s.pack_in.at[which, other]
        return remote(
            ref, ref, s.pack_send.at[which, other], s.pack_recv.at[which, other], route.owner(other)
        )

    def pack(which, value):
        s.pack_out[which] = (
            dot(ordered, value).reshape(blocks, per_block, width).astype(BF16)
        )

    def send_pack(which):
        each_other(route.block, lambda block: pack_copy(which, block).start())
        s.pack_in[which, route.home] = s.pack_out[which, route.block]

    def take_pack(which):
        each_other(route.home, lambda other: pack_arrival(which, other).wait_recv())
        flat = s.pack_in[which].astype(F32).reshape(rows, width).astype(BF16)
        return dot(one_hot(lane.astype(F32) == place_col), flat).astype(BF16)

    pack(0, tokens[...])
    send_pack(0)
    weights.tick(2)
    pack(1, cotangent[...])
    s.routes[1:2, :] = jnp.sum(jnp.where(diagonal, picked, 0.0), 0, keepdims=True)

    moved_to = route.worker(route.home)
    stays = route.block == route.home
    teach_copy = remote(s.teach_out, s.teach_in, s.misc_send.at[1], s.misc_recv.at[1], moved_to)

    for step in range(1, 8):
        piece_copy(step).wait_recv()
    wrapped = one_hot(
        iota((BLOCK, width), 0) == iota((BLOCK, width), 1) - BLOCK * (iota((BLOCK, width), 1) // BLOCK)
    )
    owner = iota((16, width), 1) // BLOCK
    vectors = jnp.zeros((16, width), F32)
    for k in range(8):
        vectors = vectors + jnp.where(owner == k, dot(s.pieces[k, :, :BLOCK], wrapped), 0.0)
    s.vectors[...] = vectors
    for k in range(8):
        part = s.pieces[k, 8:9, :].astype(F32)
        s.vectors[8 + k // 2 : 9 + k // 2, 4 * BLOCK * (k % 2) : 4 * BLOCK * (k % 2 + 1)] = part

    def vector(index):
        return s.vectors[index : index + 1, :]

    ids_copy.wait_recv()
    here = s.ints[route.block, 0:1, :]
    source_row = lax.shift_right_logical(here, 8).astype(F32)
    source_col = column(source_row)
    same = source_col == source_row
    before = iota((rows, rows), 1) < iota((rows, rows), 0)
    rank_col = jnp.sum(jnp.where(same & before, 1.0, 0.0), 1, keepdims=True)
    rank_row = jnp.sum(
        jnp.where(same & jnp.logical_not(before | diagonal), 1.0, 0.0), 0, keepdims=True
    )
    s.routes[0:1, :] = source_row * 8 + rank_row
    place_col = source_col * 8 + rank_col
    from_own = place.core == route.group_core
    query_row = jnp.where(from_own, s.ids[0, route.quarter], s.ids[1, route.quarter]).astype(F32)
    for quarter in range(4):
        key_row = jnp.where(from_own, s.ids[0, quarter], s.ids[1, quarter]).astype(F32)
        s.mask[quarter] = jnp.where(column(key_row) == query_row, 0.0, -1e30)

    def rows_copy(kind, arriving):
        quarter, to = (
            (route.quarter, route.pair),
            (route.quarter, place.mate),
            (route.pair_quarter, place.mate),
        )[kind]
        if arriving:
            quarter = (route.pair_quarter, route.mate_quarter, route.far_quarter)[kind]
        ref = s.packed.at[quarter]
        return remote(ref, ref, s.misc_send.at[2 + kind], s.misc_recv.at[2 + kind], to)

    packed = take_pack(0)
    s.packed[route.quarter] = packed
    s.packed_t[0] = packed.T
    rows_copy(0, False).start()
    rows_copy(1, False).start()
    weights.tick(3)
    send_pack(1)

    @pl.when(jnp.logical_not(stays))
    def _():
        teach_copy.start()

    @pl.when(stays)
    def _():
        s.teach_in[...] = s.teach_out[...]

    weights.tick(4)
    weights.tick(5)

    def whole(unit):
        return full[width * unit : width * (unit + 1), :]

    def keys_values(quarter):
        value = s.packed[quarter]
        keys = dot(value, whole(0)).astype(BF16)
        s.keys[quarter] = keys
        s.keys_t[quarter] = keys.T
        values = (dot(value, whole(1)) + vector(1)).astype(BF16)
        s.values[quarter] = values
        s.values_t[quarter] = values.T

    rows_copy(0, True).wait_recv()
    rows_copy(2, False).start()
    weights.ready(0)
    weights.ready(1)
    keys_values(route.quarter)
    rows_copy(1, True).wait_recv()
    keys_values(route.mate_quarter)
    weights.tick(6)
    s.packed_t[1] = s.packed[route.pair_quarter].T
    keep(s.packed_t, outs.packed_t)
    keys_values(route.pair_quarter)
    rows_copy(2, True).wait_recv()
    keys_values(route.far_quarter)
    weights.ready(2)
    scale = (width // HEADS) ** -0.5
    s.query[...] = (
        (dot(packed, whole(2)) + vector(0)).astype(BF16).astype(F32) * scale
    ).astype(BF16)
    keep(s.query, outs.query)
    keep(s.keys_t, outs.keys_t)
    keep(s.values, outs.values)
    weights.tick(7)

    head = width // HEADS
    left_half = iota((rows, 2 * head), 1) < head

    def pair_of_heads(pair, carry):
        @pl.when(pair % 2 == 0)
        def _():
            weights.tick(pair // 2 + 8)

        lanes = pl.ds(pl.multiple_of(2 * head * pair, 2 * head), 2 * head)
        both = s.query[:, lanes]
        for side in range(2):
            keep_lane = left_half if side == 0 else jnp.logical_not(left_half)
            chosen = jnp.where(keep_lane, both, jnp.zeros_like(both))
            top = jnp.full((1, rows), -3e38, F32)
            for quarter in range(4):
                part = dot_nt(s.keys[quarter, :, lanes], chosen) + s.mask[quarter]
                s.scores[side, quarter] = part
                top = jnp.maximum(top, jnp.max(part, 0, keepdims=True))
            total = jnp.zeros((1, rows), F32)
            for quarter in range(4):
                part = jnp.exp(s.scores[side, quarter] - top)
                s.scores[side, quarter] = part
                total = total + jnp.sum(part, 0, keepdims=True)
            share = 1.0 / total
            index = 2 * pair + side
            down = pl.ds(pl.multiple_of(head * index, head), head)
            summed = jnp.zeros((head, rows), F32)
            for quarter in range(4):
                part = (s.scores[side, quarter] * share).astype(BF16)
                s.probs[index, quarter] = part
                summed = summed + dot(s.values_t[quarter, down, :], part)
            s.context_t[down, :] = summed.astype(BF16)
        return carry

    lax.fori_loop(0, HEADS // 2, pair_of_heads, 0)
    keep(s.probs, outs.probs)
    keep(s.context_t, outs.context_t)
    weights.tick(11)

    weights.ready(3)
    branch = dot(s.context_t[...].T, whole(3)) + vector(2)
    scaled, inverse = normalize(packed.astype(F32) + branch)
    s.scaled[...] = scaled
    s.inverse[...] = jnp.broadcast_to(inverse, (rows, 128))
    normed = scaled * vector(3) + vector(4)
    s.normed[...] = normed
    low = normed.astype(BF16)
    s.low[...] = low
    s.low_t[...] = low.T
    keep(s.scaled, outs.scaled)
    keep(s.inverse, outs.inverse)
    keep(s.low_t, outs.low_t)

    root_half, norm = 2.0**-0.5, (2.0 * math.pi) ** -0.5
    piece = width // 2

    def up(step, carry):
        lanes = pl.ds(pl.multiple_of(piece * (step % 2), piece), piece)
        wide = pl.ds(pl.multiple_of(piece * step, piece), piece)
        down = pl.ds(pl.multiple_of(width * (4 + step // 2), width), width)
        bias = s.vectors[pl.ds(8 + step // 2, 1), lanes]
        pre = dot(s.low[...], full[down, lanes]) + bias
        phi = 0.5 + 0.5 * lax.erf(pre * root_half)
        act = (pre * phi).astype(BF16)
        s.act[:, wide] = act
        s.act_t[wide, :] = act.T
        s.slope[:, wide] = (phi + pre * (norm * jnp.exp(-0.5 * pre * pre))).astype(BF16)
        return carry

    for part in range(4):
        weights.ready(4 + part)
        lax.fori_loop(2 * part, 2 * part + 2, up, 0)
        if part % 2 == 1:
            weights.pass_on(10 + part // 2)
            weights.corner(9 + part // 2)
    keep(full.at[: 8 * width, :], outs.full.at[: 8 * width, :])
    weights.corner(11)
    keep(s.act_t, outs.act_t)
    keep(s.slope, outs.slope)
    for part in range(4):
        weights.ready(8 + part)
    keep(full.at[8 * width :, :], outs.full.at[8 * width :, :])
    ffn = dot(s.act[...], full[8 * width :, :]) + vector(5)

    scaled, inverse = normalize(s.normed[...] + ffn)
    result = scaled * vector(6) + vector(7)
    s.result[...] = result.astype(BF16)
    keep(s.result, outs.result)

    @pl.when(jnp.logical_not(stays))
    def _():
        teach_copy.wait_recv()

    valid = column(s.ints[route.block, 1:2, :].astype(F32))
    miss = valid * (result - s.teach_in[...].astype(F32))
    factor = 1.0 / (count * width)
    s.small[...] = jnp.zeros((16, width), F32)
    s.small[12:13, :] = jnp.sum(miss * miss, 0, keepdims=True) * factor
    grad_out = take_pack(1).astype(F32) + (2.0 * factor) * miss
    s.small[6:7, :] = jnp.sum(grad_out * scaled, 0, keepdims=True)
    s.small[7:8, :] = jnp.sum(grad_out, 0, keepdims=True)
    s.small[13:14, :] = vector(3)
    grad_scaled = grad_out * vector(6)
    grad_res = inverse * (
        grad_scaled
        - jnp.mean(grad_scaled, -1, keepdims=True)
        - scaled * jnp.mean(grad_scaled * scaled, -1, keepdims=True)
    )
    s.grad_res[...] = grad_res
    grad_ffn = grad_res.astype(BF16)
    s.grad_ffn[...] = grad_ffn
    s.small[5:6, :] = jnp.sum(grad_ffn.astype(F32), 0, keepdims=True)
    keep(s.grad_res, outs.grad_res)
    keep(s.grad_ffn, outs.grad_ffn)
    keep(s.small, outs.small)
    keep(s.routes, outs.routes)

    weights.drain()
    each_other(route.home, lambda other: ints_copy(other).wait_send())
    for which in range(2):
        each_other(route.block, lambda block: pack_copy(which, block).wait_send())
    for step in range(1, 8):
        piece_copy(step).wait_send()
    ids_copy.wait_send()
    for kind in range(3):
        rows_copy(kind, False).wait_send()

    @pl.when(jnp.logical_not(stays))
    def _():
        teach_copy.wait_send()

    for copy in stores:
        copy.wait()


def encoder_forward(z_size, ints, ids, tokens, cotangent, teacher, pieces, *shards):
    rows, width = tokens.shape
    blocks = 8 * z_size
    scratch = {name: make(rows, width, blocks) for name, make in FORWARD_SCRATCH.items()}
    vmem, anywhere = pl.BlockSpec(memory_space=pltpu.VMEM), pl.BlockSpec(memory_space=pl.ANY)
    results = pl.pallas_call(
        partial(forward_kernel, z_size),
        out_shape=tuple(
            jax.ShapeDtypeStruct(scratch[name].shape, scratch[name].dtype) for name in Kept._fields
        ),
        in_specs=[vmem] * 6 + [anywhere] * 6,
        out_specs=(anywhere,) * len(Kept._fields),
        scratch_shapes=list(scratch.values()),
        compiler_params=pltpu.CompilerParams(
            collective_id=0, has_side_effects=True, vmem_limit_bytes=62 * 2**20
        ),
        name="encoder_forward",
    )(ints, ids, tokens, cotangent, teacher, pieces, *shards)
    return Kept(*results)


LEFT = (0, 1, 2, 3, 4, 4, 4, 4, 5, 6, 6, 6)
RIGHT = (0, 0, 0, 0, 1, 2, 3, 4, 5, 6, 7, 8)


class Grads:
    def __init__(self, place, s, out):
        self.place, self.s, self.out = place, s, out
        self.tok_rows = s.left.shape[2] // 2
        half = BLOCK // 2
        self.low, self.high = slice(0, half), slice(half, BLOCK)

    def source_rows(self, group, j, core):
        shard = 2 * j + core
        if group < 4:
            return pl.ds(pl.multiple_of(4 * BLOCK * shard + BLOCK * group, 32), BLOCK)
        return pl.ds(pl.multiple_of(BLOCK * shard, 32), BLOCK)

    def left_copy(self, group, j, source):
        return remote(
            source.at[self.source_rows(group, j, 1 - self.place.core), :],
            self.s.left.at[group, BLOCK * j : BLOCK * (j + 1), self.tok_rows :],
            self.s.left_send.at[group, j],
            self.s.left_recv.at[group, j],
            self.place.mate,
        )

    def left_own(self, group, j, source):
        return pltpu.make_async_copy(
            source.at[self.source_rows(group, j, self.place.core), :],
            self.s.left.at[group, BLOCK * j : BLOCK * (j + 1), : self.tok_rows],
            self.s.left_own.at[group, j],
        )

    def give_left(self, group, source):
        for j in range(4):
            self.left_copy(group, j, source).start()
            self.left_own(group, j, source).start()

    def take_left(self, group, source):
        for j in range(4):
            self.left_copy(group, j, source).wait_recv()
            self.left_own(group, j, source).wait()

    def own_right(self, index):
        return self.s.right.at[index, : self.tok_rows, :]

    def right_copy(self, index):
        return remote(
            self.own_right(index),
            self.s.right.at[index, self.tok_rows :, :],
            self.s.right_send.at[index],
            self.s.right_recv.at[index],
            self.place.mate,
        )

    def copy(self, unit, kind):
        place, low, high, s = self.place, self.low, self.high, self.s
        source, target, to = (
            (s.out_d.at[unit, low], s.in_dx.at[unit], place.across),
            (s.out_d.at[unit, high], s.in_dy.at[unit], place.along),
            (s.out_x.at[unit, low], s.in_x.at[unit, low], place.across),
            (s.out_x.at[unit, high], s.in_x.at[unit, high], place.across),
            (s.out_y.at[unit, low], s.in_y.at[unit, low], place.along),
            (s.out_y.at[unit, high], s.in_y.at[unit, high], place.along),
            (s.out_x.at[unit], s.in_z.at[0, unit], {"ctx": place.z + 1}),
            (s.out_y.at[unit], s.in_z.at[1, unit], {"ctx": place.z - 1}),
        )[kind]
        return remote(source, target, s.send.at[unit, kind], s.recv.at[unit, kind], to)

    def part(self, j):
        return pl.ds(pl.multiple_of(BLOCK * j, 32), BLOCK)

    def multiply(self, unit):
        place, s = self.place, self.s
        s.partial[...] = dot(s.left[LEFT[unit]], s.right[RIGHT[unit]])
        s.out_d[unit] = s.partial[self.part(place.j_d), :].astype(BF16)
        s.out_x[unit] = s.partial[self.part(place.j_x), :].astype(BF16)
        s.out_y[unit] = s.partial[self.part(place.j_y), :].astype(BF16)
        s.total[unit] = s.partial[self.part(place.j_own), :]

    def begin(self, unit):
        for kind in (0, 1, 2, 5):
            self.copy(unit, kind).start()

    def pass_on(self, unit):
        low, high, s = self.low, self.high, self.s
        self.copy(unit, 0).wait_recv()
        s.out_y[unit, low] = (
            s.out_y[unit, low].astype(F32) + s.in_dx[unit].astype(F32)
        ).astype(BF16)
        self.copy(unit, 1).wait_recv()
        s.out_x[unit, high] = (
            s.out_x[unit, high].astype(F32) + s.in_dy[unit].astype(F32)
        ).astype(BF16)
        self.copy(unit, 4).start()
        self.copy(unit, 3).start()

    def gather(self, unit):
        s = self.s
        for kind in (2, 3, 4, 5):
            self.copy(unit, kind).wait_recv()
        s.total[unit] = (
            s.total[unit] + s.in_x[unit].astype(F32) + s.in_y[unit].astype(F32)
        )
        for kind in (2, 3, 4, 5):
            self.copy(unit, kind).wait_send()

    def hop(self, unit, step):
        place, s = self.place, self.s
        for way, turn in ((0, step), (1, place.z_size - 1 - step)):

            @pl.when(place.z == turn)
            def _():
                value = s.total[unit]
                if step > 0:
                    self.copy(unit, 6 + way).wait_recv()
                    value = value + s.in_z[way, unit].astype(F32)
                (s.out_x, s.out_y)[way][unit] = value.astype(BF16)
                self.copy(unit, 6 + way).start()

    def result(self, unit):
        return pltpu.make_async_copy(
            self.s.total.at[unit], self.out.at[unit], self.s.out_sem.at[unit]
        )

    def finish(self, unit):
        place, s = self.place, self.s
        last = place.z_size - 1

        @pl.when(place.z == last)
        def _():
            self.copy(unit, 6).wait_recv()

        @pl.when(place.z == 0)
        def _():
            self.copy(unit, 7).wait_recv()

        for way, present in ((0, place.z > 0), (1, place.z < last)):

            @pl.when(present)
            def _():
                s.total[unit] = s.total[unit] + s.in_z[way, unit].astype(F32)

        self.result(unit).start()

    def tick(self, step):
        def stage(lag, action):
            if not isinstance(step, int) or 0 <= step - lag < UNITS:
                action(step - lag)

        stage(0, self.begin)
        stage(1, self.pass_on)
        stage(2, self.gather)
        for hop in range(self.place.z_size - 1):
            stage(2 + hop, lambda unit: self.hop(unit, hop))
        stage(1 + self.place.z_size, self.finish)

    def drain(self, lefts):
        place = self.place

        def one(unit, carry):
            self.copy(unit, 0).wait_send()
            self.copy(unit, 1).wait_send()

            @pl.when(place.z < place.z_size - 1)
            def _():
                self.copy(unit, 6).wait_send()

            @pl.when(place.z > 0)
            def _():
                self.copy(unit, 7).wait_send()

            self.result(unit).wait()
            return carry

        lax.fori_loop(0, UNITS, one, 0)
        for group in range(7):
            for j in range(4):
                self.left_copy(group, j, lefts[group]).wait_send()
        for index in range(9):
            self.right_copy(index).wait_send()


BACKWARD_SCRATCH = dict(
    left=lambda t, w, b: pltpu.VMEM((7, 4 * BLOCK, 2 * t), BF16),
    right=lambda t, w, b: pltpu.VMEM((9, 2 * t, w), BF16),
    partial=lambda t, w, b: pltpu.VMEM((4 * BLOCK, w), F32),
    out_d=lambda t, w, b: pltpu.VMEM((UNITS, BLOCK, w), BF16),
    out_x=lambda t, w, b: pltpu.VMEM((UNITS, BLOCK, w), BF16),
    out_y=lambda t, w, b: pltpu.VMEM((UNITS, BLOCK, w), BF16),
    in_dx=lambda t, w, b: pltpu.VMEM((UNITS, BLOCK // 2, w), BF16),
    in_dy=lambda t, w, b: pltpu.VMEM((UNITS, BLOCK // 2, w), BF16),
    in_x=lambda t, w, b: pltpu.VMEM((UNITS, BLOCK, w), BF16),
    in_y=lambda t, w, b: pltpu.VMEM((UNITS, BLOCK, w), BF16),
    total=lambda t, w, b: pltpu.VMEM((UNITS, BLOCK, w), F32),
    in_z=lambda t, w, b: pltpu.VMEM((2, UNITS, BLOCK, w), BF16),
    weight_a=lambda t, w, b: pltpu.VMEM((4 * w, w), BF16),
    weight_b=lambda t, w, b: pltpu.VMEM((4 * w, w), BF16),
    probs=lambda t, w, b: pltpu.VMEM((2, 2, 4, t, t), BF16),
    keys_t=lambda t, w, b: pltpu.VMEM((4, w, t), BF16),
    values=lambda t, w, b: pltpu.VMEM((4, t, w), BF16),
    query=lambda t, w, b: pltpu.VMEM((t, w), BF16),
    context_t=lambda t, w, b: pltpu.VMEM((w, t), BF16),
    scaled=lambda t, w, b: pltpu.VMEM((t, w), F32),
    inverse=lambda t, w, b: pltpu.VMEM((t, 128), F32),
    slope=lambda t, w, b: pltpu.VMEM((t, 4 * w), BF16),
    result=lambda t, w, b: pltpu.VMEM((t, w), BF16),
    grad_res=lambda t, w, b: pltpu.VMEM((t, w), F32),
    small=lambda t, w, b: pltpu.VMEM((16, w), F32),
    routes=lambda t, w, b: pltpu.VMEM((8, t), F32),
    grad_context=lambda t, w, b: pltpu.VMEM((t, w), BF16),
    grad_context_t=lambda t, w, b: pltpu.VMEM((w, t), BF16),
    grad_query_t=lambda t, w, b: pltpu.VMEM((w, t), BF16),
    kv_out=lambda t, w, b: pltpu.VMEM((HEADS // 2, 4, t, t), BF16),
    kv_mate=lambda t, w, b: pltpu.VMEM((HEADS // 2, 2, t, t), BF16),
    kv_pair=lambda t, w, b: pltpu.VMEM((HEADS // 2, t, t), BF16),
    back_out=lambda t, w, b: pltpu.VMEM((2, b, t // b, w), BF16),
    back_in=lambda t, w, b: pltpu.VMEM((2, b, t // b, w), BF16),
    homes=lambda t, w, b: pltpu.VMEM((2, t, w), BF16),
    sums=lambda t, w, b: pltpu.VMEM((3, 16, w), F32),
    got_sums=lambda t, w, b: pltpu.VMEM((3, 16, w), F32),
    got_z=lambda t, w, b: pltpu.VMEM((b // 8, 16, w), F32),
    send=lambda t, w, b: pltpu.SemaphoreType.DMA((UNITS, 8)),
    recv=lambda t, w, b: pltpu.SemaphoreType.DMA((UNITS, 8)),
    left_send=lambda t, w, b: pltpu.SemaphoreType.DMA((7, 4)),
    left_recv=lambda t, w, b: pltpu.SemaphoreType.DMA((7, 4)),
    left_own=lambda t, w, b: pltpu.SemaphoreType.DMA((7, 4)),
    right_send=lambda t, w, b: pltpu.SemaphoreType.DMA((9,)),
    right_recv=lambda t, w, b: pltpu.SemaphoreType.DMA((9,)),
    out_sem=lambda t, w, b: pltpu.SemaphoreType.DMA((UNITS,)),
    load_sem=lambda t, w, b: pltpu.SemaphoreType.DMA((20,)),
    probs_sem=lambda t, w, b: pltpu.SemaphoreType.DMA((2,)),
    kv_send=lambda t, w, b: pltpu.SemaphoreType.DMA((HEADS // 2, 3)),
    kv_recv=lambda t, w, b: pltpu.SemaphoreType.DMA((HEADS // 2, 3)),
    back_send=lambda t, w, b: pltpu.SemaphoreType.DMA((2, b)),
    back_recv=lambda t, w, b: pltpu.SemaphoreType.DMA((2, b)),
    sum_send=lambda t, w, b: pltpu.SemaphoreType.DMA((3 + b // 8,)),
    sum_recv=lambda t, w, b: pltpu.SemaphoreType.DMA((3 + b // 8,)),
)


def backward_kernel(z_size, *refs):
    count = len(Kept._fields)
    given = Kept(*refs[:count])
    out_grads, out_homes, out_small = refs[count : count + 3]
    s = SimpleNamespace(**dict(zip(BACKWARD_SCRATCH, refs[count + 3 :])))
    route = Route(z_size)
    place = route.place
    rows, width = s.query.shape
    blocks = route.blocks
    grads = Grads(place, s, out_grads)
    head = width // HEADS
    pairs = HEADS // 2

    count = [0]

    def load(source, target):
        copy = pltpu.make_async_copy(source, target, s.load_sem.at[count[0]])
        count[0] += 1
        copy.start()
        return copy

    def loaded(*copies):
        for copy in copies:
            copy.wait()

    full = given.full
    l_ffn = load(given.grad_ffn, grads.own_right(0))
    l_down = load(full.at[2 * 4 * width :, :], s.weight_a)
    l_up = load(full.at[4 * width : 8 * width, :], s.weight_b)
    l_slope = load(given.slope, s.slope)
    l_routes = load(given.routes, s.routes)
    l_result = load(given.result, s.result)
    l_small = load(given.small, s.small)
    l_grad_res = load(given.grad_res, s.grad_res)
    l_scaled = load(given.scaled, s.scaled)
    l_inverse = load(given.inverse, s.inverse)
    l_query = load(given.query, s.query)
    l_context_t = load(given.context_t, s.context_t)
    l_keys_t = load(given.keys_t, s.keys_t)
    l_values = load(given.values, s.values)

    def probs_copy(pair):
        slot = pair % 2
        return pltpu.make_async_copy(
            given.probs.at[pl.ds(2 * pair, 2)], s.probs.at[slot], s.probs_sem.at[slot]
        )

    probs_copy(0).start()
    lefts = (given.act_t,) * 4 + (given.low_t, given.context_t, given.packed_t.at[0])
    route.greet_all()

    def each_other(start, action):
        def one(step, carry):
            action((start + step) % blocks)
            return carry

        lax.fori_loop(1, blocks, one, 0)

    loaded(l_ffn)
    grads.right_copy(0).start()
    for group in range(7):
        grads.give_left(group, lefts[group])

    def back_copy(which, other):
        return remote(
            s.back_out.at[which, other],
            s.back_in.at[which, route.block],
            s.back_send.at[which, other],
            s.back_recv.at[which, route.block],
            route.owner(other),
        )

    def back_arrival(which, block):
        ref = s.back_in.at[which, block]
        return remote(
            ref, ref, s.back_send.at[which, block], s.back_recv.at[which, block], route.worker(block)
        )

    def send_back(which, value):
        ordered = one_hot(iota((rows, rows), 0).astype(F32) == s.routes[0:1, :])
        s.back_out[which] = (
            dot(ordered, value).reshape(blocks, rows // blocks, width).astype(BF16)
        )
        each_other(route.home, lambda other: back_copy(which, other).start())
        s.back_in[which, route.block] = s.back_out[which, route.home]

    def take_back(which):
        each_other(route.block, lambda block: back_arrival(which, block).wait_recv())
        placed = one_hot(iota((rows, rows), 0).astype(F32) == s.routes[1:2, :])
        flat = s.back_in[which].astype(F32).reshape(rows, width).astype(BF16)
        s.homes[which] = dot(placed, flat).astype(BF16)

    grads.right_copy(0).wait_recv()
    for unit in range(4):
        grads.take_left(unit, lefts[unit])
        grads.multiply(unit)
        if unit in (0, 3):
            grads.tick(unit // 3)

    loaded(l_routes, l_result)
    send_back(0, s.result[...])
    loaded(l_down, l_up, l_slope, l_small, l_grad_res, l_scaled, l_inverse)
    grad_ffn = s.right[0, :rows, :]
    grad_normed = s.grad_res[...]
    for part in range(4):
        block = slice(width * part, width * (part + 1))
        grad_act = dot_nt(grad_ffn, s.weight_a[block, :])
        grad_pre = (grad_act * s.slope[:, block].astype(F32)).astype(BF16)
        s.right[1 + part, :rows, :] = grad_pre
        s.small[8 + part : 9 + part, :] = jnp.sum(grad_pre.astype(F32), 0, keepdims=True)
        grad_normed = grad_normed + dot_nt(grad_pre, s.weight_b[block, :])
        grads.right_copy(1 + part).start()
        if part % 2 == 1:
            grads.tick(2 + part // 2)
    l_rest = load(full.at[: 4 * width, :], s.weight_a)

    scaled = s.scaled[...]
    s.small[3:4, :] = jnp.sum(grad_normed * scaled, 0, keepdims=True)
    s.small[4:5, :] = jnp.sum(grad_normed, 0, keepdims=True)
    grad_scaled = grad_normed * s.small[13:14, :]
    grad_res = s.inverse[:, :1] * (
        grad_scaled
        - jnp.mean(grad_scaled, -1, keepdims=True)
        - scaled * jnp.mean(grad_scaled * scaled, -1, keepdims=True)
    )
    s.grad_res[...] = grad_res
    grad_branch = grad_res.astype(BF16)
    s.right[5, :rows, :] = grad_branch
    s.small[2:3, :] = jnp.sum(grad_branch.astype(F32), 0, keepdims=True)
    grads.right_copy(5).start()
    grads.take_left(4, lefts[4])
    for part in range(4):
        grads.right_copy(1 + part).wait_recv()
        grads.multiply(4 + part)
        if part == 1:
            grads.tick(4)
    loaded(l_rest)
    grad_context = dot_nt(grad_branch, s.weight_a[3 * width :, :]).astype(BF16)
    s.grad_context[...] = grad_context
    s.grad_context_t[...] = grad_context.T
    grads.take_left(5, lefts[5])
    grads.right_copy(5).wait_recv()
    grads.multiply(8)
    grads.tick(5)
    loaded(l_query, l_context_t, l_keys_t, l_values)

    def kv_copy(pair, kind):
        source, target, to = (
            (s.kv_out.at[pair, route.mate_quarter], s.kv_mate.at[pair, 0], place.mate),
            (s.kv_out.at[pair, route.far_quarter], s.kv_mate.at[pair, 1], place.mate),
            (s.kv_out.at[pair, route.pair_quarter], s.kv_pair.at[pair], route.pair),
        )[kind]
        return remote(source, target, s.kv_send.at[pair, kind], s.kv_recv.at[pair, kind], to)

    def kv_second(pair):
        kv_copy(pair, 1).wait_recv()
        s.kv_out[pair, route.pair_quarter] = (
            s.kv_out[pair, route.pair_quarter].astype(F32) + s.kv_mate[pair, 1].astype(F32)
        ).astype(BF16)
        kv_copy(pair, 2).start()

    def kv_third(pair):
        kv_copy(pair, 0).wait_recv()
        kv_copy(pair, 2).wait_recv()
        summed = (
            s.kv_out[pair, route.quarter].astype(F32)
            + s.kv_mate[pair, 0].astype(F32)
            + s.kv_pair[pair].astype(F32)
        ).astype(BF16)
        lanes = pl.ds(pl.multiple_of(2 * head * pair, 2 * head), 2 * head)
        s.right[7, :rows, lanes] = summed[:, : 2 * head]
        s.right[8, :rows, lanes] = summed[:, 2 * head :]

    left_half = iota((rows, 2 * head), 1) < head
    scale = head**-0.5

    def pair_of_heads(pair, carry):
        @pl.when(pair < pairs - 1)
        def _():
            probs_copy(pair + 1).start()

        @pl.when(pair % 2 == 1)
        def _():
            grads.tick(pair // 2 + 6)

        @pl.when(pair > 1)
        def _():
            kv_second(pair - 2)

        @pl.when(pair > 3)
        def _():
            kv_third(pair - 4)

        probs_copy(pair).wait()
        slot = pair % 2
        lanes = pl.ds(pl.multiple_of(2 * head * pair, 2 * head), 2 * head)
        both_c = s.grad_context[:, lanes]
        both_q = s.query[:, lanes]
        chosen_c, chosen_q, delta, grad_q = [], [], [], []
        for side in range(2):
            keep_lane = left_half if side == 0 else jnp.logical_not(left_half)
            chosen_c.append(jnp.where(keep_lane, both_c, jnp.zeros_like(both_c)))
            chosen_q.append(jnp.where(keep_lane, both_q, jnp.zeros_like(both_q)))
            down = pl.ds(pl.multiple_of(head * (2 * pair + side), head), head)
            delta.append(
                jnp.sum(
                    s.grad_context_t[down, :].astype(F32) * s.context_t[down, :].astype(F32),
                    0,
                    keepdims=True,
                )
            )
            grad_q.append(jnp.zeros((head, rows), F32))
        for quarter in range(4):
            value = s.values[quarter, :, lanes]
            grad_k = jnp.zeros((rows, 2 * head), F32)
            grad_v = jnp.zeros((rows, 2 * head), F32)
            for side in range(2):
                down = pl.ds(pl.multiple_of(head * (2 * pair + side), head), head)
                probs = s.probs[slot, side, quarter]
                grad_probs = dot_nt(value, chosen_c[side])
                grad_scores = (probs.astype(F32) * (grad_probs - delta[side])).astype(BF16)
                grad_v = grad_v + dot(probs, chosen_c[side])
                grad_k = grad_k + dot(grad_scores, chosen_q[side])
                grad_q[side] = grad_q[side] + dot(s.keys_t[quarter, down, :], grad_scores)
            s.kv_out[pair, quarter, :, : 2 * head] = grad_k.astype(BF16)
            s.kv_out[pair, quarter, :, 2 * head :] = grad_v.astype(BF16)
        kv_copy(pair, 0).start()
        kv_copy(pair, 1).start()
        for side in range(2):
            down = pl.ds(pl.multiple_of(head * (2 * pair + side), head), head)
            s.grad_query_t[down, :] = (grad_q[side] * scale).astype(BF16)
        return carry

    lax.fori_loop(0, pairs, pair_of_heads, 0)
    grad_query = s.grad_query_t[...].T
    s.right[6, :rows, :] = grad_query
    s.small[0:1, :] = jnp.sum(grad_query.astype(F32), 0, keepdims=True)
    grads.right_copy(6).start()
    grads.take_left(6, lefts[6])
    grads.right_copy(6).wait_recv()
    grads.multiply(9)
    kv_second(pairs - 2)
    kv_second(pairs - 1)
    kv_third(pairs - 4)
    kv_third(pairs - 3)
    grads.tick(9)
    kv_third(pairs - 2)
    kv_third(pairs - 1)
    grads.right_copy(7).start()
    grads.right_copy(8).start()
    grad_value = s.right[8, :rows, :]
    s.small[1:2, :] = jnp.sum(grad_value.astype(F32), 0, keepdims=True)

    def sum_copy(stage, to):
        return remote(
            s.small if stage == 0 else s.sums.at[stage - 1],
            s.got_sums.at[stage],
            s.sum_send.at[stage],
            s.sum_recv.at[stage],
            to,
        )

    sum_copies = [
        sum_copy(stage, to) for stage, to in enumerate((place.mate, place.across, place.along))
    ]
    sum_copies[0].start()
    for unit in (10, 11):
        grads.right_copy(unit - 3).wait_recv()
        grads.multiply(unit)
    grads.tick(10)
    sum_copies[0].wait_recv()
    s.sums[0] = s.small[...] + s.got_sums[0]
    sum_copies[1].start()
    grad_input = (
        s.grad_res[...]
        + dot_nt(s.right[6, :rows, :], s.weight_a[2 * width : 3 * width, :])
        + dot_nt(s.right[7, :rows, :], s.weight_a[:width, :])
        + dot_nt(grad_value, s.weight_a[width : 2 * width, :])
    )
    send_back(1, grad_input.astype(BF16))
    grads.tick(11)
    take_back(0)
    sum_copies[1].wait_recv()
    s.sums[1] = s.sums[0] + s.got_sums[1]
    sum_copies[2].start()
    grads.tick(12)
    sum_copies[2].wait_recv()
    s.sums[2] = s.sums[1] + s.got_sums[2]

    def z_copy(step):
        other = (place.z + step) % z_size
        return remote(
            s.sums.at[2],
            s.got_z.at[place.z],
            s.sum_send.at[2 + step],
            s.sum_recv.at[2 + step],
            {"ctx": other},
        )

    for step in range(1, z_size):
        z_copy(step).start()
    s.got_z[place.z] = s.sums[2]
    grads.tick(13)
    take_back(1)
    home_copy = pltpu.make_async_copy(s.homes, out_homes, s.probs_sem.at[0])
    home_copy.start()
    grads.tick(14)
    for step in range(1, z_size):
        z_copy(step).wait_recv()
    total = s.got_z[0]
    for z in range(1, z_size):
        total = total + s.got_z[z]
    out_small[...] = total
    grads.tick(15)
    grads.tick(16)

    grads.drain(lefts)
    for pair in range(pairs):
        for kind in range(3):
            kv_copy(pair, kind).wait_send()
    for which in range(2):
        each_other(route.home, lambda other: back_copy(which, other).wait_send())
    for copy in sum_copies:
        copy.wait_send()
    for step in range(1, z_size):
        z_copy(step).wait_send()
    home_copy.wait()


def encoder_backward(z_size, kept):
    rows, width = kept.query.shape
    blocks = 8 * z_size
    scratch = {name: make(rows, width, blocks) for name, make in BACKWARD_SCRATCH.items()}
    vmem, anywhere = pl.BlockSpec(memory_space=pltpu.VMEM), pl.BlockSpec(memory_space=pl.ANY)
    return pl.pallas_call(
        partial(backward_kernel, z_size),
        out_shape=(
            jax.ShapeDtypeStruct((UNITS, BLOCK, width), F32),
            jax.ShapeDtypeStruct((2, rows, width), BF16),
            jax.ShapeDtypeStruct((16, width), F32),
        ),
        in_specs=[anywhere] * len(Kept._fields),
        out_specs=(anywhere, anywhere, vmem),
        scratch_shapes=list(scratch.values()),
        compiler_params=pltpu.CompilerParams(
            collective_id=1, has_side_effects=True, vmem_limit_bytes=62 * 2**20
        ),
        name="encoder_backward",
    )(*kept)


norm_eps = 1e-12
floor_score = -1e30
masked_score = -1e32


def product(left, right):
    return jnp.dot(left, right, preferred_element_type=jnp.float32)


def inner_rows(left, right):
    return lax.dot_general(
        left, right, (((0,), (0,)), ((), ())), preferred_element_type=jnp.float32
    )


def against(left, right):
    return lax.dot_general(
        left, right, (((1,), (1,)), ((), ())), preferred_element_type=jnp.float32
    )


def layer_norm(value, gain, shift):
    centre = value - jnp.mean(value, -1, keepdims=True)
    spread = jnp.mean(centre * centre, -1, keepdims=True)
    inverse_dev = lax.rsqrt(spread + norm_eps)
    scaled = centre * inverse_dev
    return (scaled * gain + shift, scaled, inverse_dev)


def norm_back(grad_norm, scaled, inverse_dev, gain):
    grad_scaled = grad_norm * gain
    centred = grad_scaled - jnp.mean(grad_scaled, -1, keepdims=True)
    return inverse_dev * (centred - scaled * jnp.mean(grad_scaled * scaled, -1, keepdims=True))


def per_device(
    tokens,
    cotangent,
    token_order,
    sequence_ids,
    valid,
    teacher,
    w_query,
    b_query,
    w_key,
    w_value,
    b_value,
    w_out,
    b_out,
    norm1_gain,
    norm1_bias,
    w_up,
    b_up,
    w_down,
    b_down,
    norm2_gain,
    norm2_bias,
):
    tok_rows, model_width = tokens.shape
    peer_count = lax.axis_size(("dp", "ctx"))
    per_peer = tok_rows // peer_count
    head_count = HEADS
    head_size = model_width // head_count
    score_scale = head_size ** (-0.5)
    gelu_exact = partial(jax.nn.gelu, approximate=False)
    positions = lax.iota(jnp.int32, tok_rows)
    source = token_order // tok_rows
    slot_sort = jnp.argsort(source * tok_rows + positions)
    requests = (token_order[slot_sort] % tok_rows).reshape(peer_count, per_peer)
    wanted = lax.all_to_all(requests, ("dp", "ctx"), split_axis=0, concat_axis=0, tiled=True)
    wanted_flat = wanted.reshape(tok_rows)
    packed_x, packed_cot = (
        lax.all_to_all(
            tokens[wanted_flat].reshape(peer_count, per_peer, model_width),
            ("dp", "ctx"),
            split_axis=0,
            concat_axis=0,
            tiled=True,
        ),
        lax.all_to_all(
            cotangent[wanted_flat].reshape(peer_count, per_peer, model_width),
            ("dp", "ctx"),
            split_axis=0,
            concat_axis=0,
            tiled=True,
        ),
    )
    arrival = jnp.argsort(slot_sort)
    inputs = packed_x.reshape(tok_rows, model_width)[arrival]
    cot_rows = packed_cot.reshape(tok_rows, model_width)[arrival].astype(jnp.float32)
    valid_rows = valid.astype(jnp.float32)
    valid_count = lax.psum(jnp.sum(valid_rows), ("dp", "ctx"))
    (
        query_weight,
        query_bias,
        key_weight,
        value_weight,
        value_bias,
        out_weight,
        out_bias,
        gain_one,
        shift_one,
        up_weight,
        up_bias,
        down_weight,
        down_bias,
        gain_two,
        shift_two,
    ) = (
        lax.all_gather(w_query, "dp", axis=0, tiled=True),
        lax.all_gather(b_query, "dp", axis=0, tiled=True),
        lax.all_gather(w_key, "dp", axis=0, tiled=True),
        lax.all_gather(w_value, "dp", axis=0, tiled=True),
        lax.all_gather(b_value, "dp", axis=0, tiled=True),
        lax.all_gather(w_out, "dp", axis=0, tiled=True),
        lax.all_gather(b_out, "dp", axis=0, tiled=True),
        lax.all_gather(norm1_gain, "dp", axis=0, tiled=True),
        lax.all_gather(norm1_bias, "dp", axis=0, tiled=True),
        lax.all_gather(w_up, "dp", axis=0, tiled=True),
        lax.all_gather(b_up, "dp", axis=0, tiled=True),
        lax.all_gather(w_down, "dp", axis=0, tiled=True),
        lax.all_gather(b_down, "dp", axis=0, tiled=True),
        lax.all_gather(norm2_gain, "dp", axis=0, tiled=True),
        lax.all_gather(norm2_bias, "dp", axis=0, tiled=True),
    )
    queries = (product(inputs, query_weight) + query_bias).astype(jnp.bfloat16)
    key_rows = product(inputs, key_weight).astype(jnp.bfloat16)
    values = (product(inputs, value_weight) + value_bias).astype(jnp.bfloat16)
    group_ids = sequence_ids.reshape(-1)
    cycle_index = lax.axis_index("ctx")
    query_ids = lax.dynamic_slice_in_dim(group_ids, cycle_index * tok_rows, tok_rows)
    query_heads = queries.reshape(tok_rows, head_count, head_size)
    initial = (
        jnp.full((head_count, tok_rows), floor_score, jnp.float32),
        jnp.zeros((head_count, tok_rows), jnp.float32),
        jnp.zeros((tok_rows, head_count, head_size), jnp.float32),
    )
    folded = initial
    key_piece = lax.all_gather(key_rows, "ctx", axis=0, tiled=True)
    value_piece = lax.all_gather(values, "ctx", axis=0, tiled=True)
    length = key_piece.shape[0]
    attend_block_rows = math.gcd(length, 512)
    block_count = length // attend_block_rows

    def one_block(carried, inputs_block):
        running_max, running_sum, summed = carried
        key_block, value_block, key_start = inputs_block
        key_ids = lax.dynamic_slice_in_dim(group_ids, key_start, attend_block_rows)
        scores = (
            jnp.einsum("qhd,khd->hqk", query_heads, key_block, preferred_element_type=jnp.float32)
            * score_scale
        )
        scores = jnp.where((query_ids[:, None] == key_ids[None, :])[None], scores, masked_score)
        new_max = jnp.maximum(running_max, jnp.max(scores, -1))
        factor = jnp.exp(running_max - new_max)
        weights = jnp.exp(scores - new_max[:, :, None])
        running_sum = running_sum * factor + jnp.sum(weights, -1)
        update = jnp.einsum(
            "hqk,khd->qhd",
            weights.astype(jnp.bfloat16),
            value_block,
            preferred_element_type=jnp.float32,
        )
        summed = summed * jnp.transpose(factor)[:, :, None] + update
        return ((new_max, running_sum, summed), None)

    key_starts = attend_block_rows * lax.iota(jnp.int32, block_count)
    folded, _ = lax.scan(
        one_block,
        folded,
        (
            key_piece.reshape(block_count, attend_block_rows, head_count, head_size),
            value_piece.reshape(block_count, attend_block_rows, head_count, head_size),
            key_starts,
        ),
    )
    running_max, running_sum, summed = folded
    attended = summed / jnp.transpose(running_sum)[:, :, None]
    log_total = running_max + jnp.log(running_sum)
    context = attended.reshape(tok_rows, model_width).astype(jnp.bfloat16)
    branch = product(context, out_weight) + out_bias
    normed, scaled_one, inverse_one = layer_norm(
        inputs.astype(jnp.float32) + branch, gain_one, shift_one
    )
    normed_low = normed.astype(jnp.bfloat16)
    pre_act = product(normed_low, up_weight) + up_bias
    activated = gelu_exact(pre_act).astype(jnp.bfloat16)
    ffn_out = product(activated, down_weight) + down_bias
    result, scaled_two, inverse_two = layer_norm(normed + ffn_out, gain_two, shift_two)
    difference = result - teacher
    loss_total = lax.psum(jnp.sum(valid_rows[:, None] * difference * difference), ("dp", "ctx"))
    loss_value = loss_total / (valid_count * model_width)
    grad_out = cot_rows + 2.0 / (valid_count * model_width) * valid_rows[:, None] * difference
    grad_gain_two = jnp.sum(grad_out * scaled_two, 0)
    grad_shift_two = jnp.sum(grad_out, 0)
    grad_res_two = norm_back(grad_out, scaled_two, inverse_two, gain_two)
    grad_ffn = grad_res_two.astype(jnp.bfloat16)
    grad_down = inner_rows(activated, grad_ffn)
    grad_down_bias = jnp.sum(grad_ffn.astype(jnp.float32), 0)
    grad_act = against(grad_ffn, down_weight)
    _, gelu_pull = jax.vjp(gelu_exact, pre_act)
    grad_pre = gelu_pull(grad_act)[0].astype(jnp.bfloat16)
    grad_up = inner_rows(normed_low, grad_pre)
    grad_up_bias = jnp.sum(grad_pre.astype(jnp.float32), 0)
    grad_normed = grad_res_two + against(grad_pre, up_weight)
    ffn_shards = (
        lax.psum_scatter(
            grad_up.astype(jnp.bfloat16), "dp", scatter_dimension=0, tiled=True
        ).astype(jnp.float32),
        lax.psum_scatter(
            grad_up_bias.astype(jnp.bfloat16), "dp", scatter_dimension=0, tiled=True
        ).astype(jnp.float32),
        lax.psum_scatter(
            grad_down.astype(jnp.bfloat16), "dp", scatter_dimension=0, tiled=True
        ).astype(jnp.float32),
        lax.psum_scatter(
            grad_down_bias.astype(jnp.bfloat16), "dp", scatter_dimension=0, tiled=True
        ).astype(jnp.float32),
        lax.psum_scatter(
            grad_gain_two.astype(jnp.bfloat16), "dp", scatter_dimension=0, tiled=True
        ).astype(jnp.float32),
        lax.psum_scatter(
            grad_shift_two.astype(jnp.bfloat16), "dp", scatter_dimension=0, tiled=True
        ).astype(jnp.float32),
    )
    grad_gain_one = jnp.sum(grad_normed * scaled_one, 0)
    grad_shift_one = jnp.sum(grad_normed, 0)
    grad_res_one = norm_back(grad_normed, scaled_one, inverse_one, gain_one)
    grad_branch = grad_res_one.astype(jnp.bfloat16)
    grad_out_w = inner_rows(context, grad_branch)
    grad_out_bias = jnp.sum(grad_branch.astype(jnp.float32), 0)
    grad_context = against(grad_branch, out_weight).astype(jnp.bfloat16)
    grad_heads = grad_context.reshape(tok_rows, head_count, head_size)
    delta = jnp.transpose(jnp.sum(grad_heads.astype(jnp.float32) * attended, -1))
    all_keys, all_values = (
        lax.all_gather(key_rows, "ctx", axis=0, tiled=True),
        lax.all_gather(values, "ctx", axis=0, tiled=True),
    )
    group_len = all_keys.shape[0]
    block_rows = math.gcd(group_len, 512)
    block_count = group_len // block_rows
    key_starts = block_rows * lax.iota(jnp.int32, block_count)
    key_blocks = all_keys.reshape(block_count, block_rows, head_count, head_size)
    value_blocks = all_values.reshape(block_count, block_rows, head_count, head_size)

    def query_side(key_block, value_block, key_start):
        key_ids = lax.dynamic_slice_in_dim(group_ids, key_start, block_rows)
        scores = (
            jnp.einsum("qhd,khd->hqk", query_heads, key_block, preferred_element_type=jnp.float32)
            * score_scale
        )
        scores = jnp.where((query_ids[:, None] == key_ids[None, :])[None], scores, masked_score)
        probs = jnp.exp(scores - log_total[:, :, None])
        grad_probs = jnp.einsum(
            "qhd,khd->hqk", grad_heads, value_block, preferred_element_type=jnp.float32
        )
        grad_scores = (probs * (grad_probs - delta[:, :, None])).astype(jnp.bfloat16)
        return (probs, grad_scores)

    def back_block(grad_query, inputs_block):
        key_block, value_block, key_start = inputs_block
        probs, grad_scores = query_side(key_block, value_block, key_start)
        grad_query = (
            grad_query
            + jnp.einsum("hqk,khd->qhd", grad_scores, key_block, preferred_element_type=jnp.float32)
            * score_scale
        )
        grad_key = (
            jnp.einsum("hqk,qhd->khd", grad_scores, query_heads, preferred_element_type=jnp.float32)
            * score_scale
        )
        grad_value = jnp.einsum(
            "hqk,qhd->khd",
            probs.astype(jnp.bfloat16),
            grad_heads,
            preferred_element_type=jnp.float32,
        )
        return (grad_query, (grad_key, grad_value))

    grad_query, (key_parts, value_parts) = lax.scan(
        back_block,
        jnp.zeros((tok_rows, head_count, head_size), jnp.float32),
        (key_blocks, value_blocks, key_starts),
    )
    key_total, value_total = (
        lax.psum_scatter(
            key_parts.reshape(group_len, model_width).astype(jnp.bfloat16),
            "ctx",
            scatter_dimension=0,
            tiled=True,
        ).astype(jnp.float32),
        lax.psum_scatter(
            value_parts.reshape(group_len, model_width).astype(jnp.bfloat16),
            "ctx",
            scatter_dimension=0,
            tiled=True,
        ).astype(jnp.float32),
    )
    grad_keys = key_total.astype(jnp.bfloat16)
    grad_values = value_total.astype(jnp.bfloat16)
    grad_queries = grad_query.reshape(tok_rows, model_width).astype(jnp.bfloat16)
    grad_query_w = inner_rows(inputs, grad_queries)
    grad_query_bias = jnp.sum(grad_queries.astype(jnp.float32), 0)
    grad_key_w = inner_rows(inputs, grad_keys)
    grad_value_w = inner_rows(inputs, grad_values)
    grad_value_bias = jnp.sum(grad_values.astype(jnp.float32), 0)
    grad_inputs = (
        grad_res_one
        + against(grad_queries, query_weight)
        + against(grad_keys, key_weight)
        + against(grad_values, value_weight)
    )
    attn_shards = (
        lax.psum_scatter(
            grad_query_w.astype(jnp.bfloat16), "dp", scatter_dimension=0, tiled=True
        ).astype(jnp.float32),
        lax.psum_scatter(
            grad_query_bias.astype(jnp.bfloat16), "dp", scatter_dimension=0, tiled=True
        ).astype(jnp.float32),
        lax.psum_scatter(
            grad_key_w.astype(jnp.bfloat16), "dp", scatter_dimension=0, tiled=True
        ).astype(jnp.float32),
        lax.psum_scatter(
            grad_value_w.astype(jnp.bfloat16), "dp", scatter_dimension=0, tiled=True
        ).astype(jnp.float32),
        lax.psum_scatter(
            grad_value_bias.astype(jnp.bfloat16), "dp", scatter_dimension=0, tiled=True
        ).astype(jnp.float32),
        lax.psum_scatter(
            grad_out_w.astype(jnp.bfloat16), "dp", scatter_dimension=0, tiled=True
        ).astype(jnp.float32),
        lax.psum_scatter(
            grad_out_bias.astype(jnp.bfloat16), "dp", scatter_dimension=0, tiled=True
        ).astype(jnp.float32),
        lax.psum_scatter(
            grad_gain_one.astype(jnp.bfloat16), "dp", scatter_dimension=0, tiled=True
        ).astype(jnp.float32),
        lax.psum_scatter(
            grad_shift_one.astype(jnp.bfloat16), "dp", scatter_dimension=0, tiled=True
        ).astype(jnp.float32),
    )
    totals = (
        lax.psum(attn_shards[0].astype(jnp.bfloat16), "ctx").astype(jnp.float32),
        lax.psum(attn_shards[1].astype(jnp.bfloat16), "ctx").astype(jnp.float32),
        lax.psum(attn_shards[2].astype(jnp.bfloat16), "ctx").astype(jnp.float32),
        lax.psum(attn_shards[3].astype(jnp.bfloat16), "ctx").astype(jnp.float32),
        lax.psum(attn_shards[4].astype(jnp.bfloat16), "ctx").astype(jnp.float32),
        lax.psum(attn_shards[5].astype(jnp.bfloat16), "ctx").astype(jnp.float32),
        lax.psum(attn_shards[6].astype(jnp.bfloat16), "ctx").astype(jnp.float32),
        lax.psum(attn_shards[7].astype(jnp.bfloat16), "ctx").astype(jnp.float32),
        lax.psum(attn_shards[8].astype(jnp.bfloat16), "ctx").astype(jnp.float32),
        lax.psum(ffn_shards[0].astype(jnp.bfloat16), "ctx").astype(jnp.float32),
        lax.psum(ffn_shards[1].astype(jnp.bfloat16), "ctx").astype(jnp.float32),
        lax.psum(ffn_shards[2].astype(jnp.bfloat16), "ctx").astype(jnp.float32),
        lax.psum(ffn_shards[3].astype(jnp.bfloat16), "ctx").astype(jnp.float32),
        lax.psum(ffn_shards[4].astype(jnp.bfloat16), "ctx").astype(jnp.float32),
        lax.psum(ffn_shards[5].astype(jnp.bfloat16), "ctx").astype(jnp.float32),
    )
    back_out, back_grad = (
        lax.all_to_all(
            result[slot_sort].reshape(peer_count, per_peer, model_width).astype(jnp.bfloat16),
            ("dp", "ctx"),
            split_axis=0,
            concat_axis=0,
            tiled=True,
        ).astype(jnp.float32),
        lax.all_to_all(
            grad_inputs[slot_sort].reshape(peer_count, per_peer, model_width).astype(jnp.bfloat16),
            ("dp", "ctx"),
            split_axis=0,
            concat_axis=0,
            tiled=True,
        ).astype(jnp.float32),
    )
    homeward = jnp.argsort(wanted_flat)
    output = back_out.reshape(tok_rows, model_width)[homeward]
    input_grad = back_grad.reshape(tok_rows, model_width)[homeward]
    return (
        output,
        loss_value,
        input_grad,
        totals[0],
        totals[1],
        totals[2],
        totals[3],
        totals[4],
        totals[5],
        totals[6],
        totals[7],
        totals[8],
        totals[9],
        totals[10],
        totals[11],
        totals[12],
        totals[13],
        totals[14],
    )


def per_device_fast(
    tokens,
    cotangent,
    token_order,
    sequence_ids,
    valid,
    teacher,
    w_query,
    b_query,
    w_key,
    w_value,
    b_value,
    w_out,
    b_out,
    norm1_gain,
    norm1_bias,
    w_up,
    b_up,
    w_down,
    b_down,
    norm2_gain,
    norm2_bias,
):
    rows, width = tokens.shape
    z_size = lax.axis_size("ctx")
    ints = jnp.stack([token_order, valid])
    ids = sequence_ids.reshape(z_size, 1, rows)
    narrow = jnp.stack(
        [b_query, b_value, b_out, norm1_gain, norm1_bias, b_down, norm2_gain, norm2_bias]
    )
    pieces = jnp.concatenate(
        [
            jnp.pad(narrow, ((0, 0), (0, 3 * BLOCK))),
            b_up[None],
            jnp.zeros((7, 4 * BLOCK), BF16),
        ]
    )
    kept = encoder_forward(
        z_size,
        ints,
        ids,
        tokens,
        cotangent,
        teacher,
        pieces,
        w_query,
        w_key,
        w_value,
        w_out,
        w_up,
        w_down,
    )
    grads, homes, small = encoder_backward(z_size, kept)
    dp_index = lax.axis_index("dp")
    own = lax.dynamic_slice_in_dim(small[:8], dp_index * BLOCK, BLOCK, axis=1)
    own_up = lax.dynamic_slice_in_dim(
        small[8:12].reshape(-1), dp_index * 4 * BLOCK, 4 * BLOCK
    )
    homes = homes.astype(F32)
    return (
        homes[0],
        jnp.sum(small[12]),
        homes[1],
        grads[9],
        own[0],
        grads[10],
        grads[11],
        own[1],
        grads[8],
        own[2],
        own[3],
        own[4],
        jnp.concatenate(list(grads[4:8]), axis=1),
        own_up,
        grads[:4].reshape(4 * BLOCK, width),
        own[5],
        own[6],
        own[7],
    )


def solution(mesh):
    in_specs = (
        P(("dp", "ctx"), None),
        P(("dp", "ctx"), None),
        P(("dp", "ctx")),
        P("dp", None),
        P(("dp", "ctx")),
        P(("dp", "ctx"), None),
        P("dp", None),
        P("dp"),
        P("dp", None),
        P("dp", None),
        P("dp"),
        P("dp", None),
        P("dp"),
        P("dp"),
        P("dp"),
        P("dp", None),
        P("dp"),
        P("dp", None),
        P("dp"),
        P("dp"),
        P("dp"),
    )
    out_specs = (
        P(("dp", "ctx"), None),
        P(),
        P(("dp", "ctx"), None),
        P("dp", None),
        P("dp"),
        P("dp", None),
        P("dp", None),
        P("dp"),
        P("dp", None),
        P("dp"),
        P("dp"),
        P("dp"),
        P("dp", None),
        P("dp"),
        P("dp", None),
        P("dp"),
        P("dp"),
        P("dp"),
    )
    fast = dict(mesh.shape) == {"dp": 8, "ctx": 4}
    return jax.shard_map(
        per_device_fast if fast else per_device, mesh=mesh, in_specs=in_specs, out_specs=out_specs, check_vma=False
    )
```

```python
import math
from functools import partial
from types import SimpleNamespace
from typing import NamedTuple

import jax
import jax.numpy as jnp
from jax import lax
from jax.experimental import pallas as pl
from jax.experimental.pallas import tpu as pltpu
from jax.sharding import PartitionSpec as P

MESH = pl.DeviceIdType.MESH
F32, BF16 = jnp.float32, jnp.bfloat16


class Place:
    def __init__(self, z_size):
        dp, z = lax.axis_index("dp"), lax.axis_index("ctx")
        self.dp, self.z, self.z_size = dp, z, z_size
        core, x, y = dp % 2, dp // 2 % 2, dp // 4
        self.core = core
        self.mate = {"dp": dp + 1 - 2 * core}
        self.across = {"dp": dp + 2 - 4 * x}
        self.along = {"dp": dp + 4 - 8 * y}
        self.j_own = y * 2 + x
        self.j_x = y * 2 + 1 - x
        self.j_y = (1 - y) * 2 + x
        self.j_d = (1 - y) * 2 + 1 - x


def remote(src, dst, send, recv, to):
    return pltpu.make_async_remote_copy(
        src_ref=src, dst_ref=dst, send_sem=send, recv_sem=recv, device_id=to, device_id_type=MESH
    )


UNITS = 12
BLOCK = 96


class Route:
    def __init__(self, z_size):
        place = Place(z_size)
        self.place = place
        dp, z, core = place.dp, place.z, place.core
        self.blocks = 8 * z_size
        self.home = dp * z_size + z
        self.group_core = z // 2
        self.quarter = 2 * (z % 2) + core
        self.block = (dp - core + self.group_core) * z_size + self.quarter
        self.mate_quarter = self.quarter + 1 - 2 * core
        self.pair_quarter = self.quarter + 2 - 4 * (z % 2)
        self.far_quarter = self.pair_quarter + 1 - 2 * core
        self.pair = {"ctx": z + 1 - 2 * (z % 2)}

    def worker(self, block):
        group, quarter = block // self.place.z_size, block % self.place.z_size
        return {"dp": group - group % 2 + quarter % 2, "ctx": 2 * (group % 2) + quarter // 2}

    def owner(self, block):
        return {"dp": block // self.place.z_size, "ctx": block % self.place.z_size}

    def greet_all(self):
        barrier = pltpu.get_barrier_semaphore()

        def signal(step, carry):
            other = (self.home + step) % self.blocks
            pl.semaphore_signal(
                barrier, inc=1, device_id=self.owner(other), device_id_type=MESH
            )
            return carry

        lax.fori_loop(1, self.blocks, signal, 0)
        pl.semaphore_wait(barrier, self.blocks - 1)


def shard_rows(unit, shard, width):
    start = width * unit + BLOCK * shard
    start = start + unit // 8 * (3 * BLOCK * shard - (width - BLOCK) * (unit - 8))
    return pl.multiple_of(start, 32)


class Weights:
    def __init__(self, place, full, send, recv):
        self.place, self.full, self.send, self.recv = place, full, send, recv
        self.width = full.shape[1]

    def at(self, unit, shard, first=0, count=BLOCK):
        start = shard_rows(unit, shard, self.width)
        return self.full.at[pl.ds(pl.multiple_of(start + first, 16), count), :]

    def copy(self, unit, kind, arriving):
        place = self.place
        own, across, along = place.dp, place.across["dp"], place.along["dp"]
        corner = across + along - own
        half = BLOCK // 2
        mate = place.mate["dp"] - own
        shard, first, count, to = (
            (own, 0, BLOCK, place.across),
            (own, 0, BLOCK, place.along),
            (own, 0, BLOCK, place.mate),
            (across, 0, half, place.along),
            (along, half, half, place.across),
            (across, 0, BLOCK, place.mate),
            (along, 0, BLOCK, place.mate),
            (corner, 0, BLOCK, place.mate),
        )[kind]
        if arriving:
            shard = (across, along, own + mate, corner, corner, across + mate, along + mate, corner + mate)[kind]
        ref = self.at(unit, shard, first, count)
        return remote(ref, ref, self.send.at[unit, kind], self.recv.at[unit, kind], to)

    def begin(self, unit):
        for kind in (0, 1, 2):
            self.copy(unit, kind, False).start()

    def pass_on(self, unit):
        self.copy(unit, 0, True).wait_recv()
        self.copy(unit, 3, False).start()
        self.copy(unit, 5, False).start()
        self.copy(unit, 1, True).wait_recv()
        self.copy(unit, 4, False).start()
        self.copy(unit, 6, False).start()

    def corner(self, unit):
        self.copy(unit, 3, True).wait_recv()
        self.copy(unit, 4, True).wait_recv()
        self.copy(unit, 7, False).start()

    def tick(self, step):
        self.begin(step)
        self.pass_on(step - 2)
        if not isinstance(step, int) or step >= 3:
            self.corner(step - 3)

    def ready(self, unit):
        for kind in (2, 5, 6, 7):
            self.copy(unit, kind, True).wait_recv()

    def drain(self):
        def one(unit, carry):
            for kind in range(8):
                self.copy(unit, kind, False).wait_send()
            return carry

        lax.fori_loop(0, UNITS, one, 0)


def iota(shape, axis):
    return lax.broadcasted_iota(jnp.int32, shape, axis)


def column(row):
    n = row.shape[1]
    return jnp.sum(jnp.where(iota((n, n), 0) == iota((n, n), 1), row, 0.0), 1, keepdims=True)


def dot(left, right):
    return jnp.dot(left, right, preferred_element_type=F32)


def dot_nt(left, right):
    return lax.dot_general(
        left, right, (((1,), (1,)), ((), ())), preferred_element_type=F32
    )


def one_hot(condition):
    return jnp.where(condition, 1.0, 0.0).astype(BF16)


FORWARD_SCRATCH = dict(
    ints=lambda t, w, b: pltpu.VMEM((b, 2, t), jnp.int32),
    order=lambda t, w, b: pltpu.VMEM((b, t), jnp.int32),
    ids=lambda t, w, b: pltpu.VMEM((2, 4, 1, t), jnp.int32),
    pieces=lambda t, w, b: pltpu.VMEM((8, 16, w // 2), BF16),
    vectors=lambda t, w, b: pltpu.VMEM((16, w), F32),
    pack_out=lambda t, w, b: pltpu.VMEM((2, b, t // b, w), BF16),
    pack_in=lambda t, w, b: pltpu.VMEM((2, b, t // b, w), BF16),
    teach_out=lambda t, w, b: pltpu.VMEM((t, w), BF16),
    teach_in=lambda t, w, b: pltpu.VMEM((t, w), BF16),
    full=lambda t, w, b: pltpu.VMEM((12 * w, w), BF16),
    packed=lambda t, w, b: pltpu.VMEM((4, t, w), BF16),
    packed_t=lambda t, w, b: pltpu.VMEM((2, w, t), BF16),
    query=lambda t, w, b: pltpu.VMEM((t, w), BF16),
    keys=lambda t, w, b: pltpu.VMEM((4, t, w), BF16),
    values_t=lambda t, w, b: pltpu.VMEM((4, w, t), BF16),
    mask=lambda t, w, b: pltpu.VMEM((4, t, t), F32),
    scores=lambda t, w, b: pltpu.VMEM((2, 4, t, t), F32),
    probs=lambda t, w, b: pltpu.VMEM((HEADS, 4, t, t), BF16),
    keys_t=lambda t, w, b: pltpu.VMEM((4, w, t), BF16),
    values=lambda t, w, b: pltpu.VMEM((4, t, w), BF16),
    context_t=lambda t, w, b: pltpu.VMEM((w, t), BF16),
    scaled=lambda t, w, b: pltpu.VMEM((t, w), F32),
    inverse=lambda t, w, b: pltpu.VMEM((t, 128), F32),
    normed=lambda t, w, b: pltpu.VMEM((t, w), F32),
    low=lambda t, w, b: pltpu.VMEM((t, w), BF16),
    low_t=lambda t, w, b: pltpu.VMEM((w, t), BF16),
    act=lambda t, w, b: pltpu.VMEM((t, 4 * w), BF16),
    act_t=lambda t, w, b: pltpu.VMEM((4 * w, t), BF16),
    slope=lambda t, w, b: pltpu.VMEM((t, 4 * w), BF16),
    result=lambda t, w, b: pltpu.VMEM((t, w), BF16),
    grad_res=lambda t, w, b: pltpu.VMEM((t, w), F32),
    grad_ffn=lambda t, w, b: pltpu.VMEM((t, w), BF16),
    small=lambda t, w, b: pltpu.VMEM((16, w), F32),
    routes=lambda t, w, b: pltpu.VMEM((8, t), F32),
    ints_send=lambda t, w, b: pltpu.SemaphoreType.DMA((b,)),
    ints_recv=lambda t, w, b: pltpu.SemaphoreType.DMA((b,)),
    piece_send=lambda t, w, b: pltpu.SemaphoreType.DMA((8,)),
    piece_recv=lambda t, w, b: pltpu.SemaphoreType.DMA((8,)),
    pack_send=lambda t, w, b: pltpu.SemaphoreType.DMA((2, b)),
    pack_recv=lambda t, w, b: pltpu.SemaphoreType.DMA((2, b)),
    misc_send=lambda t, w, b: pltpu.SemaphoreType.DMA((8,)),
    misc_recv=lambda t, w, b: pltpu.SemaphoreType.DMA((8,)),
    weight_send=lambda t, w, b: pltpu.SemaphoreType.DMA((UNITS, 8)),
    weight_recv=lambda t, w, b: pltpu.SemaphoreType.DMA((UNITS, 8)),
    own_sem=lambda t, w, b: pltpu.SemaphoreType.DMA((UNITS,)),
    store_sem=lambda t, w, b: pltpu.SemaphoreType.DMA((32,)),
)

class Kept(NamedTuple):
    full: object
    probs: object
    keys_t: object
    values: object
    packed_t: object
    query: object
    context_t: object
    scaled: object
    inverse: object
    low_t: object
    act_t: object
    slope: object
    result: object
    grad_res: object
    grad_ffn: object
    small: object
    routes: object


HEADS = 12
NORM_EPS = 1e-12


def normalize(value):
    centre = value - jnp.mean(value, -1, keepdims=True)
    spread = jnp.mean(centre * centre, -1, keepdims=True)
    inverse = lax.rsqrt(spread + NORM_EPS)
    return centre * inverse, inverse


def forward_kernel(z_size, ints, ids, tokens, cotangent, teacher, pieces, w_query, w_key, w_value, w_out, w_up, w_down, *refs):
    outs = Kept(*refs[: len(Kept._fields)])
    s = SimpleNamespace(**dict(zip(FORWARD_SCRATCH, refs[len(Kept._fields) :])))
    route = Route(z_size)
    place = route.place
    rows, width = tokens.shape
    blocks = route.blocks
    full = s.full
    weights = Weights(place, full, s.weight_send, s.weight_recv)
    stores = []

    def keep(source, target):
        copy = pltpu.make_async_copy(source, target, s.store_sem.at[len(stores)])
        copy.start()
        stores.append(copy)

    sources = (
        [w_key, w_value, w_query, w_out]
        + [w_up.at[:, width * i : width * (i + 1)] for i in range(4)]
        + [w_down.at[BLOCK * i : BLOCK * (i + 1), :] for i in range(4)]
    )
    own_copies = [
        pltpu.make_async_copy(source, weights.at(unit, place.dp), s.own_sem.at[unit])
        for unit, source in enumerate(sources)
    ]
    for copy in own_copies:
        copy.start()
    s.ints[route.home] = ints[...]
    s.teach_out[...] = teacher[...].astype(BF16)
    route.greet_all()

    def ints_copy(other):
        return remote(
            ints,
            s.ints.at[route.home],
            s.ints_send.at[other],
            s.ints_recv.at[route.home],
            route.owner(other),
        )

    def ints_arrival(other):
        ref = s.ints.at[other]
        return remote(ref, ref, s.ints_send.at[other], s.ints_recv.at[other], route.owner(other))

    def each_other(start, action):
        def one(step, carry):
            action((start + step) % blocks)
            return carry

        lax.fori_loop(1, blocks, one, 0)

    each_other(route.home, lambda other: ints_copy(other).start())
    def piece_copy(step):
        other = (place.dp + step) % 8
        return remote(
            pieces,
            s.pieces.at[place.dp],
            s.piece_send.at[step],
            s.piece_recv.at[step],
            {"dp": other},
        )

    for step in range(1, 8):
        piece_copy(step).start()
    s.pieces[place.dp] = pieces[...]
    ids_copy = remote(ids, s.ids.at[1], s.misc_send.at[0], s.misc_recv.at[0], place.mate)
    ids_copy.start()
    s.ids[0] = ids[...]
    for copy in own_copies[:2]:
        copy.wait()
    weights.begin(0)
    weights.begin(1)
    for copy in own_copies[2:]:
        copy.wait()

    each_other(route.home, lambda other: ints_arrival(other).wait_recv())
    count = jnp.zeros((1, rows), F32)
    for other in range(blocks):
        s.order[other : other + 1, :] = s.ints[other, 0:1, :]
        count = count + s.ints[other, 1:2, :].astype(F32)
    count = jnp.sum(count, 1, keepdims=True)
    order = s.order[...]
    source = lax.shift_right_logical(order, 8)
    local = (order - source * rows).astype(F32)
    mine = source == route.home
    earlier = one_hot(iota((rows, rows), 0) < iota((rows, rows), 1))
    rank = dot(one_hot(mine), earlier)
    per_block = rows // blocks
    slots = jnp.zeros((blocks, 128), F32)
    for k in range(per_block):
        picked = jnp.sum(jnp.where(mine & (rank == k), local, 0.0), 1, keepdims=True)
        slots = jnp.where(iota((blocks, 128), 1) == k, picked, slots)
    spread = one_hot(
        lax.shift_right_logical(iota((rows, blocks), 0), 3) == iota((rows, blocks), 1)
    )
    picked = jnp.sum(
        jnp.where(
            iota((rows, 128), 1) == (iota((rows, 128), 0) & 7),
            dot(spread, slots.astype(BF16)),
            0.0,
        ),
        1,
        keepdims=True,
    )
    lane = iota((rows, rows), 1)
    diagonal = iota((rows, rows), 0) == lane
    ordered = one_hot(lane.astype(F32) == picked)

    def pack_copy(which, block):
        return remote(
            s.pack_out.at[which, block],
            s.pack_in.at[which, route.home],
            s.pack_send.at[which, block],
            s.pack_recv.at[which, route.home],
            route.worker(block),
        )

    def pack_arrival(which, other):
        ref = s.pack_in.at[which, other]
        return remote(
            ref, ref, s.pack_send.at[which, other], s.pack_recv.at[which, other], route.owner(other)
        )

    def pack(which, value):
        s.pack_out[which] = (
            dot(ordered, value).reshape(blocks, per_block, width).astype(BF16)
        )

    def send_pack(which):
        each_other(route.block, lambda block: pack_copy(which, block).start())
        s.pack_in[which, route.home] = s.pack_out[which, route.block]

    def take_pack(which):
        each_other(route.home, lambda other: pack_arrival(which, other).wait_recv())
        flat = s.pack_in[which].astype(F32).reshape(rows, width).astype(BF16)
        return dot(one_hot(lane.astype(F32) == place_col), flat).astype(BF16)

    pack(0, tokens[...])
    send_pack(0)
    weights.tick(2)
    pack(1, cotangent[...])
    s.routes[1:2, :] = jnp.sum(jnp.where(diagonal, picked, 0.0), 0, keepdims=True)

    moved_to = route.worker(route.home)
    stays = route.block == route.home
    teach_copy = remote(s.teach_out, s.teach_in, s.misc_send.at[1], s.misc_recv.at[1], moved_to)

    for step in range(1, 8):
        piece_copy(step).wait_recv()
    wrapped = one_hot(
        iota((BLOCK, width), 0) == iota((BLOCK, width), 1) - BLOCK * (iota((BLOCK, width), 1) // BLOCK)
    )
    owner = iota((16, width), 1) // BLOCK
    vectors = jnp.zeros((16, width), F32)
    for k in range(8):
        vectors = vectors + jnp.where(owner == k, dot(s.pieces[k, :, :BLOCK], wrapped), 0.0)
    s.vectors[...] = vectors
    for k in range(8):
        part = s.pieces[k, 8:9, :].astype(F32)
        s.vectors[8 + k // 2 : 9 + k // 2, 4 * BLOCK * (k % 2) : 4 * BLOCK * (k % 2 + 1)] = part

    def vector(index):
        return s.vectors[index : index + 1, :]

    ids_copy.wait_recv()
    here = s.ints[route.block, 0:1, :]
    source_row = lax.shift_right_logical(here, 8).astype(F32)
    source_col = column(source_row)
    same = source_col == source_row
    before = iota((rows, rows), 1) < iota((rows, rows), 0)
    rank_col = jnp.sum(jnp.where(same & before, 1.0, 0.0), 1, keepdims=True)
    rank_row = jnp.sum(
        jnp.where(same & jnp.logical_not(before | diagonal), 1.0, 0.0), 0, keepdims=True
    )
    s.routes[0:1, :] = source_row * 8 + rank_row
    place_col = source_col * 8 + rank_col
    from_own = place.core == route.group_core
    query_row = jnp.where(from_own, s.ids[0, route.quarter], s.ids[1, route.quarter]).astype(F32)
    for quarter in range(4):
        key_row = jnp.where(from_own, s.ids[0, quarter], s.ids[1, quarter]).astype(F32)
        s.mask[quarter] = jnp.where(column(key_row) == query_row, 0.0, -1e30)

    def rows_copy(kind, arriving):
        quarter, to = (
            (route.quarter, route.pair),
            (route.quarter, place.mate),
            (route.pair_quarter, place.mate),
        )[kind]
        if arriving:
            quarter = (route.pair_quarter, route.mate_quarter, route.far_quarter)[kind]
        ref = s.packed.at[quarter]
        return remote(ref, ref, s.misc_send.at[2 + kind], s.misc_recv.at[2 + kind], to)

    packed = take_pack(0)
    s.packed[route.quarter] = packed
    s.packed_t[0] = packed.T
    rows_copy(0, False).start()
    rows_copy(1, False).start()
    weights.tick(3)
    send_pack(1)

    @pl.when(jnp.logical_not(stays))
    def _():
        teach_copy.start()

    @pl.when(stays)
    def _():
        s.teach_in[...] = s.teach_out[...]

    weights.tick(4)
    weights.tick(5)

    def whole(unit):
        return full[width * unit : width * (unit + 1), :]

    def keys_values(quarter):
        value = s.packed[quarter]
        keys = dot(value, whole(0)).astype(BF16)
        s.keys[quarter] = keys
        s.keys_t[quarter] = keys.T
        values = (dot(value, whole(1)) + vector(1)).astype(BF16)
        s.values[quarter] = values
        s.values_t[quarter] = values.T

    rows_copy(0, True).wait_recv()
    rows_copy(2, False).start()
    weights.ready(0)
    weights.ready(1)
    keys_values(route.quarter)
    rows_copy(1, True).wait_recv()
    keys_values(route.mate_quarter)
    weights.tick(6)
    s.packed_t[1] = s.packed[route.pair_quarter].T
    keep(s.packed_t, outs.packed_t)
    keys_values(route.pair_quarter)
    rows_copy(2, True).wait_recv()
    keys_values(route.far_quarter)
    weights.ready(2)
    scale = (width // HEADS) ** -0.5
    s.query[...] = (
        (dot(packed, whole(2)) + vector(0)).astype(BF16).astype(F32) * scale
    ).astype(BF16)
    keep(s.query, outs.query)
    keep(s.keys_t, outs.keys_t)
    keep(s.values, outs.values)
    weights.tick(7)

    head = width // HEADS
    left_half = iota((rows, 2 * head), 1) < head

    def pair_of_heads(pair, carry):
        @pl.when(pair % 2 == 0)
        def _():
            weights.tick(pair // 2 + 8)

        lanes = pl.ds(pl.multiple_of(2 * head * pair, 2 * head), 2 * head)
        both = s.query[:, lanes]
        for side in range(2):
            keep_lane = left_half if side == 0 else jnp.logical_not(left_half)
            chosen = jnp.where(keep_lane, both, jnp.zeros_like(both))
            top = jnp.full((1, rows), -3e38, F32)
            for quarter in range(4):
                part = dot_nt(s.keys[quarter, :, lanes], chosen) + s.mask[quarter]
                s.scores[side, quarter] = part
                top = jnp.maximum(top, jnp.max(part, 0, keepdims=True))
            total = jnp.zeros((1, rows), F32)
            for quarter in range(4):
                part = jnp.exp(s.scores[side, quarter] - top)
                s.scores[side, quarter] = part
                total = total + jnp.sum(part, 0, keepdims=True)
            share = 1.0 / total
            index = 2 * pair + side
            down = pl.ds(pl.multiple_of(head * index, head), head)
            summed = jnp.zeros((head, rows), F32)
            for quarter in range(4):
                part = (s.scores[side, quarter] * share).astype(BF16)
                s.probs[index, quarter] = part
                summed = summed + dot(s.values_t[quarter, down, :], part)
            s.context_t[down, :] = summed.astype(BF16)
        return carry

    lax.fori_loop(0, HEADS // 2, pair_of_heads, 0)
    keep(s.probs, outs.probs)
    keep(s.context_t, outs.context_t)
    weights.tick(11)

    weights.ready(3)
    branch = dot(s.context_t[...].T, whole(3)) + vector(2)
    scaled, inverse = normalize(packed.astype(F32) + branch)
    s.scaled[...] = scaled
    s.inverse[...] = jnp.broadcast_to(inverse, (rows, 128))
    normed = scaled * vector(3) + vector(4)
    s.normed[...] = normed
    low = normed.astype(BF16)
    s.low[...] = low
    s.low_t[...] = low.T
    keep(s.scaled, outs.scaled)
    keep(s.inverse, outs.inverse)
    keep(s.low_t, outs.low_t)

    root_half, norm = 2.0**-0.5, (2.0 * math.pi) ** -0.5
    piece = width // 2

    def up(step, carry):
        lanes = pl.ds(pl.multiple_of(piece * (step % 2), piece), piece)
        wide = pl.ds(pl.multiple_of(piece * step, piece), piece)
        down = pl.ds(pl.multiple_of(width * (4 + step // 2), width), width)
        bias = s.vectors[pl.ds(8 + step // 2, 1), lanes]
        pre = dot(s.low[...], full[down, lanes]) + bias
        phi = 0.5 + 0.5 * lax.erf(pre * root_half)
        act = (pre * phi).astype(BF16)
        s.act[:, wide] = act
        s.act_t[wide, :] = act.T
        s.slope[:, wide] = (phi + pre * (norm * jnp.exp(-0.5 * pre * pre))).astype(BF16)
        return carry

    for part in range(4):
        weights.ready(4 + part)
        lax.fori_loop(2 * part, 2 * part + 2, up, 0)
        if part % 2 == 1:
            weights.pass_on(10 + part // 2)
            weights.corner(9 + part // 2)
    keep(full.at[: 8 * width, :], outs.full.at[: 8 * width, :])
    weights.corner(11)
    keep(s.act_t, outs.act_t)
    keep(s.slope, outs.slope)
    for part in range(4):
        weights.ready(8 + part)
    keep(full.at[8 * width :, :], outs.full.at[8 * width :, :])
    ffn = dot(s.act[...], full[8 * width :, :]) + vector(5)

    scaled, inverse = normalize(s.normed[...] + ffn)
    result = scaled * vector(6) + vector(7)
    s.result[...] = result.astype(BF16)
    keep(s.result, outs.result)

    @pl.when(jnp.logical_not(stays))
    def _():
        teach_copy.wait_recv()

    valid = column(s.ints[route.block, 1:2, :].astype(F32))
    miss = valid * (result - s.teach_in[...].astype(F32))
    factor = 1.0 / (count * width)
    s.small[...] = jnp.zeros((16, width), F32)
    s.small[12:13, :] = jnp.sum(miss * miss, 0, keepdims=True) * factor
    grad_out = take_pack(1).astype(F32) + (2.0 * factor) * miss
    s.small[6:7, :] = jnp.sum(grad_out * scaled, 0, keepdims=True)
    s.small[7:8, :] = jnp.sum(grad_out, 0, keepdims=True)
    s.small[13:14, :] = vector(3)
    grad_scaled = grad_out * vector(6)
    grad_res = inverse * (
        grad_scaled
        - jnp.mean(grad_scaled, -1, keepdims=True)
        - scaled * jnp.mean(grad_scaled * scaled, -1, keepdims=True)
    )
    s.grad_res[...] = grad_res
    grad_ffn = grad_res.astype(BF16)
    s.grad_ffn[...] = grad_ffn
    s.small[5:6, :] = jnp.sum(grad_ffn.astype(F32), 0, keepdims=True)
    keep(s.grad_res, outs.grad_res)
    keep(s.grad_ffn, outs.grad_ffn)
    keep(s.small, outs.small)
    keep(s.routes, outs.routes)

    weights.drain()
    each_other(route.home, lambda other: ints_copy(other).wait_send())
    for which in range(2):
        each_other(route.block, lambda block: pack_copy(which, block).wait_send())
    for step in range(1, 8):
        piece_copy(step).wait_send()
    ids_copy.wait_send()
    for kind in range(3):
        rows_copy(kind, False).wait_send()

    @pl.when(jnp.logical_not(stays))
    def _():
        teach_copy.wait_send()

    for copy in stores:
        copy.wait()


def encoder_forward(z_size, ints, ids, tokens, cotangent, teacher, pieces, *shards):
    rows, width = tokens.shape
    blocks = 8 * z_size
    scratch = {name: make(rows, width, blocks) for name, make in FORWARD_SCRATCH.items()}
    vmem, anywhere = pl.BlockSpec(memory_space=pltpu.VMEM), pl.BlockSpec(memory_space=pl.ANY)
    results = pl.pallas_call(
        partial(forward_kernel, z_size),
        out_shape=tuple(
            jax.ShapeDtypeStruct(scratch[name].shape, scratch[name].dtype) for name in Kept._fields
        ),
        in_specs=[vmem] * 6 + [anywhere] * 6,
        out_specs=(anywhere,) * len(Kept._fields),
        scratch_shapes=list(scratch.values()),
        compiler_params=pltpu.CompilerParams(
            collective_id=0, has_side_effects=True, vmem_limit_bytes=62 * 2**20
        ),
        name="encoder_forward",
    )(ints, ids, tokens, cotangent, teacher, pieces, *shards)
    return Kept(*results)


LEFT = (0, 1, 2, 3, 4, 4, 4, 4, 5)
RIGHT = (0, 0, 0, 0, 1, 2, 3, 4, 5, 6)


class Grads:
    def __init__(self, place, s, out):
        self.place, self.s, self.out = place, s, out
        self.tok_rows = s.left.shape[2] // 2
        half = BLOCK // 2
        self.low, self.high = slice(0, half), slice(half, BLOCK)

    def source_rows(self, group, j, core):
        shard = 2 * j + core
        if group < 4:
            return pl.ds(pl.multiple_of(4 * BLOCK * shard + BLOCK * group, 32), BLOCK)
        return pl.ds(pl.multiple_of(BLOCK * shard, 32), BLOCK)

    def left_copy(self, group, j, source):
        if group < 6:
            target = self.s.left.at[group, BLOCK * j : BLOCK * (j + 1), self.tok_rows :]
        else:
            first = self.tok_rows * (group - 4)
            target = self.s.left_x.at[BLOCK * j : BLOCK * (j + 1), first : first + self.tok_rows]
        return remote(
            source.at[self.source_rows(group, j, 1 - self.place.core), :],
            target,
            self.s.left_send.at[group, j],
            self.s.left_recv.at[group, j],
            self.place.mate,
        )

    def left_own(self, group, j, source):
        if group < 6:
            target = self.s.left.at[group, BLOCK * j : BLOCK * (j + 1), : self.tok_rows]
        else:
            first = self.tok_rows * (group - 6)
            target = self.s.left_x.at[BLOCK * j : BLOCK * (j + 1), first : first + self.tok_rows]
        return pltpu.make_async_copy(
            source.at[self.source_rows(group, j, self.place.core), :],
            target,
            self.s.left_own.at[group, j],
        )

    def give_left(self, group, source):
        for j in range(4):
            self.left_copy(group, j, source).start()
            self.left_own(group, j, source).start()

    def take_left(self, group, source):
        for j in range(4):
            self.left_copy(group, j, source).wait_recv()
            self.left_own(group, j, source).wait()

    def own_right(self, index):
        return self.s.right.at[index, : self.tok_rows, :]

    def right_copy(self, index):
        if index < 7:
            source, target = self.own_right(index), self.s.right.at[index, self.tok_rows :, :]
        else:
            half = 2 * self.tok_rows
            source = self.s.right_kv.at[index - 7, :half, :]
            target = self.s.right_kv.at[index - 7, half:, :]
        return remote(
            source,
            target,
            self.s.right_send.at[index],
            self.s.right_recv.at[index],
            self.place.mate,
        )

    def copy(self, unit, kind):
        place, low, high, s = self.place, self.low, self.high, self.s
        source, target, to = (
            (s.out_d.at[unit, low], s.in_dx.at[unit], place.across),
            (s.out_d.at[unit, high], s.in_dy.at[unit], place.along),
            (s.out_x.at[unit, low], s.in_x.at[unit, low], place.across),
            (s.out_x.at[unit, high], s.in_x.at[unit, high], place.across),
            (s.out_y.at[unit, low], s.in_y.at[unit, low], place.along),
            (s.out_y.at[unit, high], s.in_y.at[unit, high], place.along),
            (s.out_x.at[unit], s.in_z.at[0, unit], {"ctx": place.z + 1}),
            (s.out_y.at[unit], s.in_z.at[1, unit], {"ctx": place.z - 1}),
        )[kind]
        return remote(source, target, s.send.at[unit, kind], s.recv.at[unit, kind], to)

    def part(self, j):
        return pl.ds(pl.multiple_of(BLOCK * j, 32), BLOCK)

    def multiply(self, unit):
        place, s = self.place, self.s
        if unit < 9:
            s.partial[...] = dot(s.left[LEFT[unit]], s.right[RIGHT[unit]])
        elif unit == 9:
            n = self.tok_rows
            s.partial[...] = dot(s.left_x[:, :n], s.right[6, :n, :]) + dot(
                s.left_x[:, 2 * n : 3 * n], s.right[6, n:, :]
            )
        else:
            s.partial[...] = dot(s.left_x[...], s.right_kv[unit - 10])
        s.out_d[unit] = s.partial[self.part(place.j_d), :].astype(BF16)
        s.out_x[unit] = s.partial[self.part(place.j_x), :].astype(BF16)
        s.out_y[unit] = s.partial[self.part(place.j_y), :].astype(BF16)
        s.total[unit] = s.partial[self.part(place.j_own), :]

    def begin(self, unit):
        for kind in (0, 1, 2, 5):
            self.copy(unit, kind).start()

    def pass_on(self, unit):
        low, high, s = self.low, self.high, self.s
        self.copy(unit, 0).wait_recv()
        s.out_y[unit, low] = (
            s.out_y[unit, low].astype(F32) + s.in_dx[unit].astype(F32)
        ).astype(BF16)
        self.copy(unit, 1).wait_recv()
        s.out_x[unit, high] = (
            s.out_x[unit, high].astype(F32) + s.in_dy[unit].astype(F32)
        ).astype(BF16)
        self.copy(unit, 4).start()
        self.copy(unit, 3).start()

    def gather(self, unit):
        s = self.s
        for kind in (2, 3, 4, 5):
            self.copy(unit, kind).wait_recv()
        s.total[unit] = (
            s.total[unit] + s.in_x[unit].astype(F32) + s.in_y[unit].astype(F32)
        )
        for kind in (2, 3, 4, 5):
            self.copy(unit, kind).wait_send()

    def hop(self, unit, step):
        place, s = self.place, self.s
        for way, turn in ((0, step), (1, place.z_size - 1 - step)):

            @pl.when(place.z == turn)
            def _():
                value = s.total[unit]
                if step > 0:
                    self.copy(unit, 6 + way).wait_recv()
                    value = value + s.in_z[way, unit].astype(F32)
                (s.out_x, s.out_y)[way][unit] = value.astype(BF16)
                self.copy(unit, 6 + way).start()

    def result(self, unit):
        return pltpu.make_async_copy(
            self.s.total.at[unit], self.out.at[unit], self.s.out_sem.at[unit]
        )

    def finish(self, unit):
        place, s = self.place, self.s
        last = place.z_size - 1

        @pl.when(place.z == last)
        def _():
            self.copy(unit, 6).wait_recv()

        @pl.when(place.z == 0)
        def _():
            self.copy(unit, 7).wait_recv()

        for way, present in ((0, place.z > 0), (1, place.z < last)):

            @pl.when(present)
            def _():
                s.total[unit] = s.total[unit] + s.in_z[way, unit].astype(F32)

        self.result(unit).start()

    def line(self, *work):
        for unit, stage in work:
            if stage == 0:
                self.gather(unit)
            if stage < self.place.z_size - 1:
                self.hop(unit, stage)
            else:
                self.finish(unit)

    def drain(self, lefts):
        place = self.place

        def one(unit, carry):
            self.copy(unit, 0).wait_send()
            self.copy(unit, 1).wait_send()

            @pl.when(place.z < place.z_size - 1)
            def _():
                self.copy(unit, 6).wait_send()

            @pl.when(place.z > 0)
            def _():
                self.copy(unit, 7).wait_send()

            self.result(unit).wait()
            return carry

        lax.fori_loop(0, UNITS, one, 0)
        for group in range(8):
            for j in range(4):
                self.left_copy(group, j, lefts[group]).wait_send()
        for index in range(9):
            self.right_copy(index).wait_send()


BACKWARD_SCRATCH = dict(
    left=lambda t, w, b: pltpu.VMEM((6, 4 * BLOCK, 2 * t), BF16),
    left_x=lambda t, w, b: pltpu.VMEM((4 * BLOCK, 4 * t), BF16),
    right=lambda t, w, b: pltpu.VMEM((7, 2 * t, w), BF16),
    right_kv=lambda t, w, b: pltpu.VMEM((2, 4 * t, w), BF16),
    partial=lambda t, w, b: pltpu.VMEM((4 * BLOCK, w), F32),
    out_d=lambda t, w, b: pltpu.VMEM((UNITS, BLOCK, w), BF16),
    out_x=lambda t, w, b: pltpu.VMEM((UNITS, BLOCK, w), BF16),
    out_y=lambda t, w, b: pltpu.VMEM((UNITS, BLOCK, w), BF16),
    in_dx=lambda t, w, b: pltpu.VMEM((UNITS, BLOCK // 2, w), BF16),
    in_dy=lambda t, w, b: pltpu.VMEM((UNITS, BLOCK // 2, w), BF16),
    in_x=lambda t, w, b: pltpu.VMEM((UNITS, BLOCK, w), BF16),
    in_y=lambda t, w, b: pltpu.VMEM((UNITS, BLOCK, w), BF16),
    total=lambda t, w, b: pltpu.VMEM((UNITS, BLOCK, w), F32),
    in_z=lambda t, w, b: pltpu.VMEM((2, UNITS, BLOCK, w), BF16),
    weight_a=lambda t, w, b: pltpu.VMEM((4 * w, w), BF16),
    weight_b=lambda t, w, b: pltpu.VMEM((4 * w, w), BF16),
    probs=lambda t, w, b: pltpu.VMEM((2, 2, 4, t, t), BF16),
    keys_t=lambda t, w, b: pltpu.VMEM((4, w, t), BF16),
    values=lambda t, w, b: pltpu.VMEM((4, t, w), BF16),
    query=lambda t, w, b: pltpu.VMEM((t, w), BF16),
    context_t=lambda t, w, b: pltpu.VMEM((w, t), BF16),
    scaled=lambda t, w, b: pltpu.VMEM((t, w), F32),
    inverse=lambda t, w, b: pltpu.VMEM((t, 128), F32),
    slope=lambda t, w, b: pltpu.VMEM((t, 4 * w), BF16),
    result=lambda t, w, b: pltpu.VMEM((t, w), BF16),
    grad_res=lambda t, w, b: pltpu.VMEM((t, w), F32),
    small=lambda t, w, b: pltpu.VMEM((16, w), F32),
    routes=lambda t, w, b: pltpu.VMEM((8, t), F32),
    grad_context=lambda t, w, b: pltpu.VMEM((t, w), BF16),
    grad_context_t=lambda t, w, b: pltpu.VMEM((w, t), BF16),
    grad_query_t=lambda t, w, b: pltpu.VMEM((w, t), BF16),
    kv_out=lambda t, w, b: pltpu.VMEM((HEADS // 2, 4, t, t), BF16),
    kv_mate=lambda t, w, b: pltpu.VMEM((HEADS // 2, 2, t, t), BF16),
    pair_out=lambda t, w, b: pltpu.VMEM((t, w), BF16),
    pair_in=lambda t, w, b: pltpu.VMEM((t, w), BF16),
    back_out=lambda t, w, b: pltpu.VMEM((2, b, t // b, w), BF16),
    back_in=lambda t, w, b: pltpu.VMEM((2, b, t // b, w), BF16),
    homes=lambda t, w, b: pltpu.VMEM((2, t, w), BF16),
    sums=lambda t, w, b: pltpu.VMEM((3, 16, w), F32),
    got_sums=lambda t, w, b: pltpu.VMEM((3, 16, w), F32),
    got_z=lambda t, w, b: pltpu.VMEM((b // 8, 16, w), F32),
    send=lambda t, w, b: pltpu.SemaphoreType.DMA((UNITS, 8)),
    recv=lambda t, w, b: pltpu.SemaphoreType.DMA((UNITS, 8)),
    left_send=lambda t, w, b: pltpu.SemaphoreType.DMA((8, 4)),
    left_recv=lambda t, w, b: pltpu.SemaphoreType.DMA((8, 4)),
    left_own=lambda t, w, b: pltpu.SemaphoreType.DMA((8, 4)),
    right_send=lambda t, w, b: pltpu.SemaphoreType.DMA((9,)),
    right_recv=lambda t, w, b: pltpu.SemaphoreType.DMA((9,)),
    out_sem=lambda t, w, b: pltpu.SemaphoreType.DMA((UNITS,)),
    load_sem=lambda t, w, b: pltpu.SemaphoreType.DMA((20,)),
    probs_sem=lambda t, w, b: pltpu.SemaphoreType.DMA((2,)),
    kv_send=lambda t, w, b: pltpu.SemaphoreType.DMA((HEADS // 2, 2)),
    kv_recv=lambda t, w, b: pltpu.SemaphoreType.DMA((HEADS // 2, 2)),
    pair_send=lambda t, w, b: pltpu.SemaphoreType.DMA((2,)),
    pair_recv=lambda t, w, b: pltpu.SemaphoreType.DMA((2,)),
    back_send=lambda t, w, b: pltpu.SemaphoreType.DMA((2, b)),
    back_recv=lambda t, w, b: pltpu.SemaphoreType.DMA((2, b)),
    sum_send=lambda t, w, b: pltpu.SemaphoreType.DMA((3 + b // 8,)),
    sum_recv=lambda t, w, b: pltpu.SemaphoreType.DMA((3 + b // 8,)),
)


def backward_kernel(z_size, *refs):
    count = len(Kept._fields)
    given = Kept(*refs[:count])
    out_grads, out_homes, out_small = refs[count : count + 3]
    s = SimpleNamespace(**dict(zip(BACKWARD_SCRATCH, refs[count + 3 :])))
    route = Route(z_size)
    place = route.place
    rows, width = s.query.shape
    blocks = route.blocks
    grads = Grads(place, s, out_grads)
    head = width // HEADS
    pairs = HEADS // 2

    count = [0]

    def load(source, target):
        copy = pltpu.make_async_copy(source, target, s.load_sem.at[count[0]])
        count[0] += 1
        copy.start()
        return copy

    def loaded(*copies):
        for copy in copies:
            copy.wait()

    full = given.full
    l_ffn = load(given.grad_ffn, grads.own_right(0))
    l_routes = load(given.routes, s.routes)
    l_result = load(given.result, s.result)
    l_down = load(full.at[2 * 4 * width :, :], s.weight_a)
    l_up = load(full.at[4 * width : 8 * width, :], s.weight_b)
    l_slope = load(given.slope, s.slope)
    l_small = load(given.small, s.small)
    l_grad_res = load(given.grad_res, s.grad_res)
    l_scaled = load(given.scaled, s.scaled)
    l_inverse = load(given.inverse, s.inverse)
    l_query = load(given.query, s.query)
    l_context_t = load(given.context_t, s.context_t)
    l_keys_t = load(given.keys_t, s.keys_t)
    l_values = load(given.values, s.values)

    def probs_copy(pair):
        slot = pair % 2
        return pltpu.make_async_copy(
            given.probs.at[pl.ds(2 * pair, 2)], s.probs.at[slot], s.probs_sem.at[slot]
        )

    probs_copy(0).start()
    lefts = (given.act_t,) * 4 + (given.low_t, given.context_t)
    lefts += (given.packed_t.at[0], given.packed_t.at[1])
    route.greet_all()

    def each_other(start, action):
        def one(step, carry):
            action((start + step) % blocks)
            return carry

        lax.fori_loop(1, blocks, one, 0)

    loaded(l_ffn)
    grads.right_copy(0).start()
    for group in range(8):
        grads.give_left(group, lefts[group])

    def back_copy(which, other):
        return remote(
            s.back_out.at[which, other],
            s.back_in.at[which, route.block],
            s.back_send.at[which, other],
            s.back_recv.at[which, route.block],
            route.owner(other),
        )

    def back_arrival(which, block):
        ref = s.back_in.at[which, block]
        return remote(
            ref, ref, s.back_send.at[which, block], s.back_recv.at[which, block], route.worker(block)
        )

    def order_back(which, value):
        ordered = one_hot(iota((rows, rows), 0).astype(F32) == s.routes[0:1, :])
        s.back_out[which] = (
            dot(ordered, value).reshape(blocks, rows // blocks, width).astype(BF16)
        )
        s.back_in[which, route.block] = s.back_out[which, route.home]

    def send_back(which, part=0, parts=1):
        def one(step, carry):
            back_copy(which, (route.home + step) % blocks).start()
            return carry

        lax.fori_loop(max(1, blocks * part // parts), blocks * (part + 1) // parts, one, 0)

    def take_back(which):
        each_other(route.block, lambda block: back_arrival(which, block).wait_recv())
        placed = one_hot(iota((rows, rows), 0).astype(F32) == s.routes[1:2, :])
        flat = s.back_in[which].astype(F32).reshape(rows, width).astype(BF16)
        s.homes[which] = dot(placed, flat).astype(BF16)

    loaded(l_routes, l_result)
    order_back(0, s.result[...])
    send_back(0)
    grads.right_copy(0).wait_recv()
    for unit in range(4):
        grads.take_left(unit, lefts[unit])
        grads.multiply(unit)
        if unit < 2:
            grads.begin(unit)

    loaded(l_down, l_up, l_slope, l_small, l_grad_res, l_scaled, l_inverse)
    grad_ffn = s.right[0, :rows, :]
    grad_normed = s.grad_res[...]
    for part in range(4):
        block = slice(width * part, width * (part + 1))
        grad_act = dot_nt(grad_ffn, s.weight_a[block, :])
        grad_pre = (grad_act * s.slope[:, block].astype(F32)).astype(BF16)
        s.right[1 + part, :rows, :] = grad_pre
        s.small[8 + part : 9 + part, :] = jnp.sum(grad_pre.astype(F32), 0, keepdims=True)
        grad_normed = grad_normed + dot_nt(grad_pre, s.weight_b[block, :])
        grads.right_copy(1 + part).start()
    l_rest = load(full.at[: 4 * width, :], s.weight_a)

    grads.pass_on(0)
    grads.begin(2)
    scaled = s.scaled[...]
    s.small[3:4, :] = jnp.sum(grad_normed * scaled, 0, keepdims=True)
    s.small[4:5, :] = jnp.sum(grad_normed, 0, keepdims=True)
    grad_scaled = grad_normed * s.small[13:14, :]
    grad_res = s.inverse[:, :1] * (
        grad_scaled
        - jnp.mean(grad_scaled, -1, keepdims=True)
        - scaled * jnp.mean(grad_scaled * scaled, -1, keepdims=True)
    )
    s.grad_res[...] = grad_res
    grad_branch = grad_res.astype(BF16)
    s.right[5, :rows, :] = grad_branch
    s.small[2:3, :] = jnp.sum(grad_branch.astype(F32), 0, keepdims=True)
    grads.right_copy(5).start()
    loaded(l_rest)
    grad_context = dot_nt(grad_branch, s.weight_a[3 * width :, :]).astype(BF16)
    s.grad_context[...] = grad_context
    s.grad_context_t[...] = grad_context.T
    loaded(l_query, l_context_t, l_keys_t, l_values)

    def kv_copy(pair, kind):
        quarter = (route.mate_quarter, route.far_quarter)[kind]
        return remote(
            s.kv_out.at[pair, quarter],
            s.kv_mate.at[pair, kind],
            s.kv_send.at[pair, kind],
            s.kv_recv.at[pair, kind],
            place.mate,
        )

    def kv_sum(pair):
        lanes = pl.ds(pl.multiple_of(2 * head * pair, 2 * head), 2 * head)
        for kind, quarter in enumerate((route.quarter, route.pair_quarter)):
            kv_copy(pair, kind).wait_recv()
            summed = (
                s.kv_out[pair, quarter].astype(F32) + s.kv_mate[pair, kind].astype(F32)
            ).astype(BF16)
            block = slice(rows * kind, rows * (kind + 1))
            s.right_kv[0, block, lanes] = summed[:, : 2 * head]
            s.right_kv[1, block, lanes] = summed[:, 2 * head :]

    left_half = iota((rows, 2 * head), 1) < head
    scale = head**-0.5

    def pair_of_heads(pair, carry):
        @pl.when(pair < pairs - 1)
        def _():
            probs_copy(pair + 1).start()

        @pl.when(pair == 2)
        def _():
            grads.pass_on(1)
            grads.begin(3)
            grads.take_left(4, lefts[4])
            grads.right_copy(1).wait_recv()
            grads.multiply(4)

        @pl.when(pair == 4)
        def _():
            grads.line((0, 0))
            grads.pass_on(2)
            grads.begin(4)

        @pl.when(pair > 1)
        def _():
            kv_sum(pair - 2)

        probs_copy(pair).wait()
        slot = pair % 2
        lanes = pl.ds(pl.multiple_of(2 * head * pair, 2 * head), 2 * head)
        both_c = s.grad_context[:, lanes]
        both_q = s.query[:, lanes]
        chosen_c, chosen_q, delta, grad_q = [], [], [], []
        for side in range(2):
            keep_lane = left_half if side == 0 else jnp.logical_not(left_half)
            chosen_c.append(jnp.where(keep_lane, both_c, jnp.zeros_like(both_c)))
            chosen_q.append(jnp.where(keep_lane, both_q, jnp.zeros_like(both_q)))
            down = pl.ds(pl.multiple_of(head * (2 * pair + side), head), head)
            delta.append(
                jnp.sum(
                    s.grad_context_t[down, :].astype(F32) * s.context_t[down, :].astype(F32),
                    0,
                    keepdims=True,
                )
            )
            grad_q.append(jnp.zeros((head, rows), F32))
        for quarter in range(4):
            value = s.values[quarter, :, lanes]
            grad_k = jnp.zeros((rows, 2 * head), F32)
            grad_v = jnp.zeros((rows, 2 * head), F32)
            for side in range(2):
                down = pl.ds(pl.multiple_of(head * (2 * pair + side), head), head)
                probs = s.probs[slot, side, quarter]
                grad_probs = dot_nt(value, chosen_c[side])
                grad_scores = (probs.astype(F32) * (grad_probs - delta[side])).astype(BF16)
                grad_v = grad_v + dot(probs, chosen_c[side])
                grad_k = grad_k + dot(grad_scores, chosen_q[side])
                grad_q[side] = grad_q[side] + dot(s.keys_t[quarter, down, :], grad_scores)
            s.kv_out[pair, quarter, :, : 2 * head] = grad_k.astype(BF16)
            s.kv_out[pair, quarter, :, 2 * head :] = grad_v.astype(BF16)
        kv_copy(pair, 0).start()
        kv_copy(pair, 1).start()
        for side in range(2):
            down = pl.ds(pl.multiple_of(head * (2 * pair + side), head), head)
            s.grad_query_t[down, :] = (grad_q[side] * scale).astype(BF16)
        return carry

    lax.fori_loop(0, pairs, pair_of_heads, 0)
    grad_query = s.grad_query_t[...].T
    s.right[6, :rows, :] = grad_query
    s.small[0:1, :] = jnp.sum(grad_query.astype(F32), 0, keepdims=True)
    grads.right_copy(6).start()
    kv_sum(pairs - 2)
    kv_sum(pairs - 1)
    grads.right_copy(7).start()
    grads.right_copy(8).start()
    grad_value = s.right_kv[1, : 2 * rows, :]
    s.small[1:2, :] = jnp.sum(grad_value.astype(F32), 0, keepdims=True)
    grads.right_copy(2).wait_recv()
    grads.multiply(5)
    grads.line((1, 0), (0, 1))
    grads.pass_on(3)
    grads.begin(5)
    from_keys = dot_nt(s.right_kv[0, : 2 * rows, :], s.weight_a[:width, :])
    from_values = dot_nt(grad_value, s.weight_a[width : 2 * width, :])
    s.pair_out[...] = (from_keys[rows:] + from_values[rows:]).astype(BF16)
    s.grad_res[...] = (
        s.grad_res[...]
        + from_keys[:rows]
        + from_values[:rows]
        + dot_nt(s.right[6, :rows, :], s.weight_a[2 * width : 3 * width, :])
    )
    pair_copies = [
        remote(
            s.pair_out.at[block],
            s.pair_in.at[block],
            s.pair_send.at[i],
            s.pair_recv.at[i],
            route.pair,
        )
        for i, block in enumerate((slice(0, rows // 2), slice(rows // 2, rows)))
    ]
    pair_copies[0].start()

    def sum_copy(stage, to):
        return remote(
            s.small if stage == 0 else s.sums.at[stage - 1],
            s.got_sums.at[stage],
            s.sum_send.at[stage],
            s.sum_recv.at[stage],
            to,
        )

    sum_copies = [
        sum_copy(stage, to) for stage, to in enumerate((place.mate, place.across, place.along))
    ]
    def sum_stage(stage):
        sum_copies[stage].wait_recv()
        before = s.small[...] if stage == 0 else s.sums[stage - 1]
        s.sums[stage] = before + s.got_sums[stage]

    sum_copies[0].start()
    grads.right_copy(3).wait_recv()
    grads.multiply(6)
    grads.line((2, 0), (1, 1), (0, 2))
    grads.pass_on(4)
    grads.begin(6)
    pair_copies[1].start()
    sum_stage(0)
    sum_copies[1].start()
    grads.right_copy(4).wait_recv()
    grads.multiply(7)
    grads.line((3, 0), (2, 1), (1, 2), (0, 3))
    grads.pass_on(5)
    grads.begin(7)
    sum_stage(1)
    sum_copies[2].start()
    for copy in pair_copies:
        copy.wait_recv()
    order_back(1, (s.grad_res[...] + s.pair_in[...].astype(F32)).astype(BF16))
    grads.take_left(5, lefts[5])
    grads.right_copy(5).wait_recv()
    grads.multiply(8)
    grads.line((4, 0), (3, 1), (2, 2), (1, 3))
    grads.pass_on(6)
    grads.begin(8)
    send_back(1, 0, 5)
    sum_stage(2)

    def z_copy(step):
        other = (place.z + step) % z_size
        return remote(
            s.sums.at[2],
            s.got_z.at[place.z],
            s.sum_send.at[2 + step],
            s.sum_recv.at[2 + step],
            {"ctx": other},
        )

    for step in range(1, z_size):
        z_copy(step).start()
    s.got_z[place.z] = s.sums[2]
    take_back(0)
    grads.take_left(6, lefts[6])
    grads.take_left(7, lefts[7])
    grads.right_copy(6).wait_recv()
    grads.multiply(9)
    grads.line((5, 0), (4, 1), (3, 2), (2, 3))
    grads.pass_on(7)
    grads.begin(9)
    send_back(1, 1, 5)
    grads.right_copy(7).wait_recv()
    grads.multiply(10)
    grads.line((6, 0), (5, 1), (4, 2), (3, 3))
    grads.pass_on(8)
    grads.begin(10)
    send_back(1, 2, 5)
    grads.right_copy(8).wait_recv()
    grads.multiply(11)
    grads.line((7, 0), (6, 1), (5, 2), (4, 3))
    grads.pass_on(9)
    grads.begin(11)
    send_back(1, 3, 5)
    grads.line((8, 0), (7, 1), (6, 2), (5, 3))
    grads.pass_on(10)
    send_back(1, 4, 5)
    for step in range(1, z_size):
        z_copy(step).wait_recv()
    total = s.got_z[0]
    for z in range(1, z_size):
        total = total + s.got_z[z]
    out_small[...] = total
    grads.line((9, 0), (8, 1), (7, 2), (6, 3))
    grads.pass_on(11)
    grads.line((10, 0), (9, 1), (8, 2), (7, 3))
    grads.line((11, 0), (10, 1), (9, 2), (8, 3))
    take_back(1)
    home_copy = pltpu.make_async_copy(s.homes, out_homes, s.probs_sem.at[0])
    home_copy.start()
    grads.line((11, 1), (10, 2), (9, 3))
    grads.line((11, 2), (10, 3))
    grads.line((11, 3))

    grads.drain(lefts)
    for pair in range(pairs):
        for kind in range(2):
            kv_copy(pair, kind).wait_send()
    for copy in pair_copies:
        copy.wait_send()
    for which in range(2):
        each_other(route.home, lambda other: back_copy(which, other).wait_send())
    for copy in sum_copies:
        copy.wait_send()
    for step in range(1, z_size):
        z_copy(step).wait_send()
    home_copy.wait()


def encoder_backward(z_size, kept):
    rows, width = kept.query.shape
    blocks = 8 * z_size
    scratch = {name: make(rows, width, blocks) for name, make in BACKWARD_SCRATCH.items()}
    vmem, anywhere = pl.BlockSpec(memory_space=pltpu.VMEM), pl.BlockSpec(memory_space=pl.ANY)
    return pl.pallas_call(
        partial(backward_kernel, z_size),
        out_shape=(
            jax.ShapeDtypeStruct((UNITS, BLOCK, width), F32),
            jax.ShapeDtypeStruct((2, rows, width), BF16),
            jax.ShapeDtypeStruct((16, width), F32),
        ),
        in_specs=[anywhere] * len(Kept._fields),
        out_specs=(anywhere, anywhere, vmem),
        scratch_shapes=list(scratch.values()),
        compiler_params=pltpu.CompilerParams(
            collective_id=1, has_side_effects=True, vmem_limit_bytes=62 * 2**20
        ),
        name="encoder_backward",
    )(*kept)


norm_eps = 1e-12
floor_score = -1e30
masked_score = -1e32


def product(left, right):
    return jnp.dot(left, right, preferred_element_type=jnp.float32)


def inner_rows(left, right):
    return lax.dot_general(
        left, right, (((0,), (0,)), ((), ())), preferred_element_type=jnp.float32
    )


def against(left, right):
    return lax.dot_general(
        left, right, (((1,), (1,)), ((), ())), preferred_element_type=jnp.float32
    )


def layer_norm(value, gain, shift):
    centre = value - jnp.mean(value, -1, keepdims=True)
    spread = jnp.mean(centre * centre, -1, keepdims=True)
    inverse_dev = lax.rsqrt(spread + norm_eps)
    scaled = centre * inverse_dev
    return (scaled * gain + shift, scaled, inverse_dev)


def norm_back(grad_norm, scaled, inverse_dev, gain):
    grad_scaled = grad_norm * gain
    centred = grad_scaled - jnp.mean(grad_scaled, -1, keepdims=True)
    return inverse_dev * (centred - scaled * jnp.mean(grad_scaled * scaled, -1, keepdims=True))


def per_device(
    tokens,
    cotangent,
    token_order,
    sequence_ids,
    valid,
    teacher,
    w_query,
    b_query,
    w_key,
    w_value,
    b_value,
    w_out,
    b_out,
    norm1_gain,
    norm1_bias,
    w_up,
    b_up,
    w_down,
    b_down,
    norm2_gain,
    norm2_bias,
):
    tok_rows, model_width = tokens.shape
    peer_count = lax.axis_size(("dp", "ctx"))
    per_peer = tok_rows // peer_count
    head_count = HEADS
    head_size = model_width // head_count
    score_scale = head_size ** (-0.5)
    gelu_exact = partial(jax.nn.gelu, approximate=False)
    positions = lax.iota(jnp.int32, tok_rows)
    source = token_order // tok_rows
    slot_sort = jnp.argsort(source * tok_rows + positions)
    requests = (token_order[slot_sort] % tok_rows).reshape(peer_count, per_peer)
    wanted = lax.all_to_all(requests, ("dp", "ctx"), split_axis=0, concat_axis=0, tiled=True)
    wanted_flat = wanted.reshape(tok_rows)
    packed_x, packed_cot = (
        lax.all_to_all(
            tokens[wanted_flat].reshape(peer_count, per_peer, model_width),
            ("dp", "ctx"),
            split_axis=0,
            concat_axis=0,
            tiled=True,
        ),
        lax.all_to_all(
            cotangent[wanted_flat].reshape(peer_count, per_peer, model_width),
            ("dp", "ctx"),
            split_axis=0,
            concat_axis=0,
            tiled=True,
        ),
    )
    arrival = jnp.argsort(slot_sort)
    inputs = packed_x.reshape(tok_rows, model_width)[arrival]
    cot_rows = packed_cot.reshape(tok_rows, model_width)[arrival].astype(jnp.float32)
    valid_rows = valid.astype(jnp.float32)
    valid_count = lax.psum(jnp.sum(valid_rows), ("dp", "ctx"))
    (
        query_weight,
        query_bias,
        key_weight,
        value_weight,
        value_bias,
        out_weight,
        out_bias,
        gain_one,
        shift_one,
        up_weight,
        up_bias,
        down_weight,
        down_bias,
        gain_two,
        shift_two,
    ) = (
        lax.all_gather(w_query, "dp", axis=0, tiled=True),
        lax.all_gather(b_query, "dp", axis=0, tiled=True),
        lax.all_gather(w_key, "dp", axis=0, tiled=True),
        lax.all_gather(w_value, "dp", axis=0, tiled=True),
        lax.all_gather(b_value, "dp", axis=0, tiled=True),
        lax.all_gather(w_out, "dp", axis=0, tiled=True),
        lax.all_gather(b_out, "dp", axis=0, tiled=True),
        lax.all_gather(norm1_gain, "dp", axis=0, tiled=True),
        lax.all_gather(norm1_bias, "dp", axis=0, tiled=True),
        lax.all_gather(w_up, "dp", axis=0, tiled=True),
        lax.all_gather(b_up, "dp", axis=0, tiled=True),
        lax.all_gather(w_down, "dp", axis=0, tiled=True),
        lax.all_gather(b_down, "dp", axis=0, tiled=True),
        lax.all_gather(norm2_gain, "dp", axis=0, tiled=True),
        lax.all_gather(norm2_bias, "dp", axis=0, tiled=True),
    )
    queries = (product(inputs, query_weight) + query_bias).astype(jnp.bfloat16)
    key_rows = product(inputs, key_weight).astype(jnp.bfloat16)
    values = (product(inputs, value_weight) + value_bias).astype(jnp.bfloat16)
    group_ids = sequence_ids.reshape(-1)
    cycle_index = lax.axis_index("ctx")
    query_ids = lax.dynamic_slice_in_dim(group_ids, cycle_index * tok_rows, tok_rows)
    query_heads = queries.reshape(tok_rows, head_count, head_size)
    initial = (
        jnp.full((head_count, tok_rows), floor_score, jnp.float32),
        jnp.zeros((head_count, tok_rows), jnp.float32),
        jnp.zeros((tok_rows, head_count, head_size), jnp.float32),
    )
    folded = initial
    key_piece = lax.all_gather(key_rows, "ctx", axis=0, tiled=True)
    value_piece = lax.all_gather(values, "ctx", axis=0, tiled=True)
    length = key_piece.shape[0]
    attend_block_rows = math.gcd(length, 512)
    block_count = length // attend_block_rows

    def one_block(carried, inputs_block):
        running_max, running_sum, summed = carried
        key_block, value_block, key_start = inputs_block
        key_ids = lax.dynamic_slice_in_dim(group_ids, key_start, attend_block_rows)
        scores = (
            jnp.einsum("qhd,khd->hqk", query_heads, key_block, preferred_element_type=jnp.float32)
            * score_scale
        )
        scores = jnp.where((query_ids[:, None] == key_ids[None, :])[None], scores, masked_score)
        new_max = jnp.maximum(running_max, jnp.max(scores, -1))
        factor = jnp.exp(running_max - new_max)
        weights = jnp.exp(scores - new_max[:, :, None])
        running_sum = running_sum * factor + jnp.sum(weights, -1)
        update = jnp.einsum(
            "hqk,khd->qhd",
            weights.astype(jnp.bfloat16),
            value_block,
            preferred_element_type=jnp.float32,
        )
        summed = summed * jnp.transpose(factor)[:, :, None] + update
        return ((new_max, running_sum, summed), None)

    key_starts = attend_block_rows * lax.iota(jnp.int32, block_count)
    folded, _ = lax.scan(
        one_block,
        folded,
        (
            key_piece.reshape(block_count, attend_block_rows, head_count, head_size),
            value_piece.reshape(block_count, attend_block_rows, head_count, head_size),
            key_starts,
        ),
    )
    running_max, running_sum, summed = folded
    attended = summed / jnp.transpose(running_sum)[:, :, None]
    log_total = running_max + jnp.log(running_sum)
    context = attended.reshape(tok_rows, model_width).astype(jnp.bfloat16)
    branch = product(context, out_weight) + out_bias
    normed, scaled_one, inverse_one = layer_norm(
        inputs.astype(jnp.float32) + branch, gain_one, shift_one
    )
    normed_low = normed.astype(jnp.bfloat16)
    pre_act = product(normed_low, up_weight) + up_bias
    activated = gelu_exact(pre_act).astype(jnp.bfloat16)
    ffn_out = product(activated, down_weight) + down_bias
    result, scaled_two, inverse_two = layer_norm(normed + ffn_out, gain_two, shift_two)
    difference = result - teacher
    loss_total = lax.psum(jnp.sum(valid_rows[:, None] * difference * difference), ("dp", "ctx"))
    loss_value = loss_total / (valid_count * model_width)
    grad_out = cot_rows + 2.0 / (valid_count * model_width) * valid_rows[:, None] * difference
    grad_gain_two = jnp.sum(grad_out * scaled_two, 0)
    grad_shift_two = jnp.sum(grad_out, 0)
    grad_res_two = norm_back(grad_out, scaled_two, inverse_two, gain_two)
    grad_ffn = grad_res_two.astype(jnp.bfloat16)
    grad_down = inner_rows(activated, grad_ffn)
    grad_down_bias = jnp.sum(grad_ffn.astype(jnp.float32), 0)
    grad_act = against(grad_ffn, down_weight)
    _, gelu_pull = jax.vjp(gelu_exact, pre_act)
    grad_pre = gelu_pull(grad_act)[0].astype(jnp.bfloat16)
    grad_up = inner_rows(normed_low, grad_pre)
    grad_up_bias = jnp.sum(grad_pre.astype(jnp.float32), 0)
    grad_normed = grad_res_two + against(grad_pre, up_weight)
    ffn_shards = (
        lax.psum_scatter(
            grad_up.astype(jnp.bfloat16), "dp", scatter_dimension=0, tiled=True
        ).astype(jnp.float32),
        lax.psum_scatter(
            grad_up_bias.astype(jnp.bfloat16), "dp", scatter_dimension=0, tiled=True
        ).astype(jnp.float32),
        lax.psum_scatter(
            grad_down.astype(jnp.bfloat16), "dp", scatter_dimension=0, tiled=True
        ).astype(jnp.float32),
        lax.psum_scatter(
            grad_down_bias.astype(jnp.bfloat16), "dp", scatter_dimension=0, tiled=True
        ).astype(jnp.float32),
        lax.psum_scatter(
            grad_gain_two.astype(jnp.bfloat16), "dp", scatter_dimension=0, tiled=True
        ).astype(jnp.float32),
        lax.psum_scatter(
            grad_shift_two.astype(jnp.bfloat16), "dp", scatter_dimension=0, tiled=True
        ).astype(jnp.float32),
    )
    grad_gain_one = jnp.sum(grad_normed * scaled_one, 0)
    grad_shift_one = jnp.sum(grad_normed, 0)
    grad_res_one = norm_back(grad_normed, scaled_one, inverse_one, gain_one)
    grad_branch = grad_res_one.astype(jnp.bfloat16)
    grad_out_w = inner_rows(context, grad_branch)
    grad_out_bias = jnp.sum(grad_branch.astype(jnp.float32), 0)
    grad_context = against(grad_branch, out_weight).astype(jnp.bfloat16)
    grad_heads = grad_context.reshape(tok_rows, head_count, head_size)
    delta = jnp.transpose(jnp.sum(grad_heads.astype(jnp.float32) * attended, -1))
    all_keys, all_values = (
        lax.all_gather(key_rows, "ctx", axis=0, tiled=True),
        lax.all_gather(values, "ctx", axis=0, tiled=True),
    )
    group_len = all_keys.shape[0]
    block_rows = math.gcd(group_len, 512)
    block_count = group_len // block_rows
    key_starts = block_rows * lax.iota(jnp.int32, block_count)
    key_blocks = all_keys.reshape(block_count, block_rows, head_count, head_size)
    value_blocks = all_values.reshape(block_count, block_rows, head_count, head_size)

    def query_side(key_block, value_block, key_start):
        key_ids = lax.dynamic_slice_in_dim(group_ids, key_start, block_rows)
        scores = (
            jnp.einsum("qhd,khd->hqk", query_heads, key_block, preferred_element_type=jnp.float32)
            * score_scale
        )
        scores = jnp.where((query_ids[:, None] == key_ids[None, :])[None], scores, masked_score)
        probs = jnp.exp(scores - log_total[:, :, None])
        grad_probs = jnp.einsum(
            "qhd,khd->hqk", grad_heads, value_block, preferred_element_type=jnp.float32
        )
        grad_scores = (probs * (grad_probs - delta[:, :, None])).astype(jnp.bfloat16)
        return (probs, grad_scores)

    def back_block(grad_query, inputs_block):
        key_block, value_block, key_start = inputs_block
        probs, grad_scores = query_side(key_block, value_block, key_start)
        grad_query = (
            grad_query
            + jnp.einsum("hqk,khd->qhd", grad_scores, key_block, preferred_element_type=jnp.float32)
            * score_scale
        )
        grad_key = (
            jnp.einsum("hqk,qhd->khd", grad_scores, query_heads, preferred_element_type=jnp.float32)
            * score_scale
        )
        grad_value = jnp.einsum(
            "hqk,qhd->khd",
            probs.astype(jnp.bfloat16),
            grad_heads,
            preferred_element_type=jnp.float32,
        )
        return (grad_query, (grad_key, grad_value))

    grad_query, (key_parts, value_parts) = lax.scan(
        back_block,
        jnp.zeros((tok_rows, head_count, head_size), jnp.float32),
        (key_blocks, value_blocks, key_starts),
    )
    key_total, value_total = (
        lax.psum_scatter(
            key_parts.reshape(group_len, model_width).astype(jnp.bfloat16),
            "ctx",
            scatter_dimension=0,
            tiled=True,
        ).astype(jnp.float32),
        lax.psum_scatter(
            value_parts.reshape(group_len, model_width).astype(jnp.bfloat16),
            "ctx",
            scatter_dimension=0,
            tiled=True,
        ).astype(jnp.float32),
    )
    grad_keys = key_total.astype(jnp.bfloat16)
    grad_values = value_total.astype(jnp.bfloat16)
    grad_queries = grad_query.reshape(tok_rows, model_width).astype(jnp.bfloat16)
    grad_query_w = inner_rows(inputs, grad_queries)
    grad_query_bias = jnp.sum(grad_queries.astype(jnp.float32), 0)
    grad_key_w = inner_rows(inputs, grad_keys)
    grad_value_w = inner_rows(inputs, grad_values)
    grad_value_bias = jnp.sum(grad_values.astype(jnp.float32), 0)
    grad_inputs = (
        grad_res_one
        + against(grad_queries, query_weight)
        + against(grad_keys, key_weight)
        + against(grad_values, value_weight)
    )
    attn_shards = (
        lax.psum_scatter(
            grad_query_w.astype(jnp.bfloat16), "dp", scatter_dimension=0, tiled=True
        ).astype(jnp.float32),
        lax.psum_scatter(
            grad_query_bias.astype(jnp.bfloat16), "dp", scatter_dimension=0, tiled=True
        ).astype(jnp.float32),
        lax.psum_scatter(
            grad_key_w.astype(jnp.bfloat16), "dp", scatter_dimension=0, tiled=True
        ).astype(jnp.float32),
        lax.psum_scatter(
            grad_value_w.astype(jnp.bfloat16), "dp", scatter_dimension=0, tiled=True
        ).astype(jnp.float32),
        lax.psum_scatter(
            grad_value_bias.astype(jnp.bfloat16), "dp", scatter_dimension=0, tiled=True
        ).astype(jnp.float32),
        lax.psum_scatter(
            grad_out_w.astype(jnp.bfloat16), "dp", scatter_dimension=0, tiled=True
        ).astype(jnp.float32),
        lax.psum_scatter(
            grad_out_bias.astype(jnp.bfloat16), "dp", scatter_dimension=0, tiled=True
        ).astype(jnp.float32),
        lax.psum_scatter(
            grad_gain_one.astype(jnp.bfloat16), "dp", scatter_dimension=0, tiled=True
        ).astype(jnp.float32),
        lax.psum_scatter(
            grad_shift_one.astype(jnp.bfloat16), "dp", scatter_dimension=0, tiled=True
        ).astype(jnp.float32),
    )
    totals = (
        lax.psum(attn_shards[0].astype(jnp.bfloat16), "ctx").astype(jnp.float32),
        lax.psum(attn_shards[1].astype(jnp.bfloat16), "ctx").astype(jnp.float32),
        lax.psum(attn_shards[2].astype(jnp.bfloat16), "ctx").astype(jnp.float32),
        lax.psum(attn_shards[3].astype(jnp.bfloat16), "ctx").astype(jnp.float32),
        lax.psum(attn_shards[4].astype(jnp.bfloat16), "ctx").astype(jnp.float32),
        lax.psum(attn_shards[5].astype(jnp.bfloat16), "ctx").astype(jnp.float32),
        lax.psum(attn_shards[6].astype(jnp.bfloat16), "ctx").astype(jnp.float32),
        lax.psum(attn_shards[7].astype(jnp.bfloat16), "ctx").astype(jnp.float32),
        lax.psum(attn_shards[8].astype(jnp.bfloat16), "ctx").astype(jnp.float32),
        lax.psum(ffn_shards[0].astype(jnp.bfloat16), "ctx").astype(jnp.float32),
        lax.psum(ffn_shards[1].astype(jnp.bfloat16), "ctx").astype(jnp.float32),
        lax.psum(ffn_shards[2].astype(jnp.bfloat16), "ctx").astype(jnp.float32),
        lax.psum(ffn_shards[3].astype(jnp.bfloat16), "ctx").astype(jnp.float32),
        lax.psum(ffn_shards[4].astype(jnp.bfloat16), "ctx").astype(jnp.float32),
        lax.psum(ffn_shards[5].astype(jnp.bfloat16), "ctx").astype(jnp.float32),
    )
    back_out, back_grad = (
        lax.all_to_all(
            result[slot_sort].reshape(peer_count, per_peer, model_width).astype(jnp.bfloat16),
            ("dp", "ctx"),
            split_axis=0,
            concat_axis=0,
            tiled=True,
        ).astype(jnp.float32),
        lax.all_to_all(
            grad_inputs[slot_sort].reshape(peer_count, per_peer, model_width).astype(jnp.bfloat16),
            ("dp", "ctx"),
            split_axis=0,
            concat_axis=0,
            tiled=True,
        ).astype(jnp.float32),
    )
    homeward = jnp.argsort(wanted_flat)
    output = back_out.reshape(tok_rows, model_width)[homeward]
    input_grad = back_grad.reshape(tok_rows, model_width)[homeward]
    return (
        output,
        loss_value,
        input_grad,
        totals[0],
        totals[1],
        totals[2],
        totals[3],
        totals[4],
        totals[5],
        totals[6],
        totals[7],
        totals[8],
        totals[9],
        totals[10],
        totals[11],
        totals[12],
        totals[13],
        totals[14],
    )


def per_device_fast(
    tokens,
    cotangent,
    token_order,
    sequence_ids,
    valid,
    teacher,
    w_query,
    b_query,
    w_key,
    w_value,
    b_value,
    w_out,
    b_out,
    norm1_gain,
    norm1_bias,
    w_up,
    b_up,
    w_down,
    b_down,
    norm2_gain,
    norm2_bias,
):
    rows, width = tokens.shape
    z_size = lax.axis_size("ctx")
    ints = jnp.stack([token_order, valid])
    ids = sequence_ids.reshape(z_size, 1, rows)
    narrow = jnp.stack(
        [b_query, b_value, b_out, norm1_gain, norm1_bias, b_down, norm2_gain, norm2_bias]
    )
    pieces = jnp.concatenate(
        [
            jnp.pad(narrow, ((0, 0), (0, 3 * BLOCK))),
            b_up[None],
            jnp.zeros((7, 4 * BLOCK), BF16),
        ]
    )
    kept = encoder_forward(
        z_size,
        ints,
        ids,
        tokens,
        cotangent,
        teacher,
        pieces,
        w_query,
        w_key,
        w_value,
        w_out,
        w_up,
        w_down,
    )
    grads, homes, small = encoder_backward(z_size, kept)
    dp_index = lax.axis_index("dp")
    own = lax.dynamic_slice_in_dim(small[:8], dp_index * BLOCK, BLOCK, axis=1)
    own_up = lax.dynamic_slice_in_dim(
        small[8:12].reshape(-1), dp_index * 4 * BLOCK, 4 * BLOCK
    )
    homes = homes.astype(F32)
    return (
        homes[0],
        jnp.sum(small[12]),
        homes[1],
        grads[9],
        own[0],
        grads[10],
        grads[11],
        own[1],
        grads[8],
        own[2],
        own[3],
        own[4],
        jnp.concatenate(list(grads[4:8]), axis=1),
        own_up,
        grads[:4].reshape(4 * BLOCK, width),
        own[5],
        own[6],
        own[7],
    )


def solution(mesh):
    in_specs = (
        P(("dp", "ctx"), None),
        P(("dp", "ctx"), None),
        P(("dp", "ctx")),
        P("dp", None),
        P(("dp", "ctx")),
        P(("dp", "ctx"), None),
        P("dp", None),
        P("dp"),
        P("dp", None),
        P("dp", None),
        P("dp"),
        P("dp", None),
        P("dp"),
        P("dp"),
        P("dp"),
        P("dp", None),
        P("dp"),
        P("dp", None),
        P("dp"),
        P("dp"),
        P("dp"),
    )
    out_specs = (
        P(("dp", "ctx"), None),
        P(),
        P(("dp", "ctx"), None),
        P("dp", None),
        P("dp"),
        P("dp", None),
        P("dp", None),
        P("dp"),
        P("dp", None),
        P("dp"),
        P("dp"),
        P("dp"),
        P("dp", None),
        P("dp"),
        P("dp", None),
        P("dp"),
        P("dp"),
        P("dp"),
    )
    fast = dict(mesh.shape) == {"dp": 8, "ctx": 4}
    return jax.shard_map(
        per_device_fast if fast else per_device, mesh=mesh, in_specs=in_specs, out_specs=out_specs, check_vma=False
    )
```

```python
import math
from functools import partial
from types import SimpleNamespace
from typing import NamedTuple

import jax
import jax.numpy as jnp
from jax import lax
from jax.experimental import pallas as pl
from jax.experimental.pallas import tpu as pltpu
from jax.sharding import PartitionSpec as P

MESH = pl.DeviceIdType.MESH
F32, BF16 = jnp.float32, jnp.bfloat16


class Place:
    def __init__(self, z_size):
        dp, z = lax.axis_index("dp"), lax.axis_index("ctx")
        self.dp, self.z, self.z_size = dp, z, z_size
        core, x, y = dp % 2, dp // 2 % 2, dp // 4
        self.core = core
        self.mate = {"dp": dp + 1 - 2 * core}
        self.across = {"dp": dp + 2 - 4 * x}
        self.along = {"dp": dp + 4 - 8 * y}
        self.j_own = y * 2 + x
        self.j_x = y * 2 + 1 - x
        self.j_y = (1 - y) * 2 + x
        self.j_d = (1 - y) * 2 + 1 - x


def remote(src, dst, send, recv, to):
    return pltpu.make_async_remote_copy(
        src_ref=src, dst_ref=dst, send_sem=send, recv_sem=recv, device_id=to, device_id_type=MESH
    )


UNITS = 12
BLOCK = 96


class Route:
    def __init__(self, z_size):
        place = Place(z_size)
        self.place = place
        dp, z, core = place.dp, place.z, place.core
        self.blocks = 8 * z_size
        self.home = dp * z_size + z
        self.group_core = z // 2
        self.quarter = 2 * (z % 2) + core
        self.block = (dp - core + self.group_core) * z_size + self.quarter
        self.mate_quarter = self.quarter + 1 - 2 * core
        self.pair_quarter = self.quarter + 2 - 4 * (z % 2)
        self.far_quarter = self.pair_quarter + 1 - 2 * core
        self.pair = {"ctx": z + 1 - 2 * (z % 2)}

    def worker(self, block):
        group, quarter = block // self.place.z_size, block % self.place.z_size
        return {"dp": group - group % 2 + quarter % 2, "ctx": 2 * (group % 2) + quarter // 2}

    def owner(self, block):
        return {"dp": block // self.place.z_size, "ctx": block % self.place.z_size}

    def greet_all(self):
        barrier = pltpu.get_barrier_semaphore()

        def signal(step, carry):
            other = (self.home + step) % self.blocks
            pl.semaphore_signal(
                barrier, inc=1, device_id=self.owner(other), device_id_type=MESH
            )
            return carry

        lax.fori_loop(1, self.blocks, signal, 0)
        pl.semaphore_wait(barrier, self.blocks - 1)


def shard_rows(unit, shard, width):
    start = width * unit + BLOCK * shard
    start = start + unit // 8 * (3 * BLOCK * shard - (width - BLOCK) * (unit - 8))
    return pl.multiple_of(start, 32)


class Weights:
    def __init__(self, place, full, send, recv):
        self.place, self.full, self.send, self.recv = place, full, send, recv
        self.width = full.shape[1]

    def at(self, unit, shard, first=0, count=BLOCK):
        start = shard_rows(unit, shard, self.width)
        return self.full.at[pl.ds(pl.multiple_of(start + first, 16), count), :]

    def copy(self, unit, kind, arriving):
        place = self.place
        own, across, along = place.dp, place.across["dp"], place.along["dp"]
        corner = across + along - own
        half = BLOCK // 2
        mate = place.mate["dp"] - own
        shard, first, count, to = (
            (own, 0, BLOCK, place.across),
            (own, 0, BLOCK, place.along),
            (own, 0, BLOCK, place.mate),
            (across, 0, half, place.along),
            (along, half, half, place.across),
            (across, 0, BLOCK, place.mate),
            (along, 0, BLOCK, place.mate),
            (corner, 0, BLOCK, place.mate),
        )[kind]
        if arriving:
            shard = (across, along, own + mate, corner, corner, across + mate, along + mate, corner + mate)[kind]
        ref = self.at(unit, shard, first, count)
        slot = (0, 1, 3, 2, 2, 3, 3, 3)[kind]
        return remote(ref, ref, self.send, self.recv.at[unit, slot], to)

    def begin(self, unit):
        for kind in (0, 1, 2):
            self.copy(unit, kind, False).start()

    def pass_on(self, unit):
        self.copy(unit, 0, True).wait_recv()
        self.copy(unit, 3, False).start()
        self.copy(unit, 5, False).start()
        self.copy(unit, 1, True).wait_recv()
        self.copy(unit, 4, False).start()
        self.copy(unit, 6, False).start()

    def together(self, rows, recv):
        ref = self.full.at[:rows, :]
        return remote(ref, ref, self.send, recv, self.place.mate)

    def corner(self, unit):
        self.together(BLOCK, self.recv.at[unit, 2]).wait_recv()
        self.copy(unit, 7, False).start()

    def tick(self, step):
        self.begin(step)
        self.pass_on(step - 2)
        if not isinstance(step, int) or step >= 3:
            self.corner(step - 3)

    def ready(self, unit):
        self.together(4 * BLOCK, self.recv.at[unit, 3]).wait_recv()

    def drain(self):
        self.together(UNITS * 7 * BLOCK, self.recv.at[0, 0]).wait_send()


def iota(shape, axis):
    return lax.broadcasted_iota(jnp.int32, shape, axis)


def column(row):
    n = row.shape[1]
    return jnp.sum(jnp.where(iota((n, n), 0) == iota((n, n), 1), row, 0.0), 1, keepdims=True)


def dot(left, right):
    return jnp.dot(left, right, preferred_element_type=F32)


def dot_nt(left, right):
    return lax.dot_general(
        left, right, (((1,), (1,)), ((), ())), preferred_element_type=F32
    )


def one_hot(condition):
    return jnp.where(condition, 1.0, 0.0).astype(BF16)


FORWARD_SCRATCH = dict(
    ints=lambda t, w, b: pltpu.VMEM((b, 2, t), jnp.int32),
    order=lambda t, w, b: pltpu.VMEM((b, t), jnp.int32),
    ids=lambda t, w, b: pltpu.VMEM((2, 4, 1, t), jnp.int32),
    pieces=lambda t, w, b: pltpu.VMEM((8, 16, 128), F32),
    vectors=lambda t, w, b: pltpu.VMEM((16, w), F32),
    pack_out=lambda t, w, b: pltpu.VMEM((2, b, t // b, w), BF16),
    pack_in=lambda t, w, b: pltpu.VMEM((2, b, t // b, w), BF16),
    teach_out=lambda t, w, b: pltpu.VMEM((t, w), BF16),
    teach_in=lambda t, w, b: pltpu.VMEM((t, w), BF16),
    full=lambda t, w, b: pltpu.VMEM((12 * w, w), BF16),
    packed=lambda t, w, b: pltpu.VMEM((4, t, w), BF16),
    packed_t=lambda t, w, b: pltpu.VMEM((2, w, t), BF16),
    query=lambda t, w, b: pltpu.VMEM((t, w), BF16),
    keys=lambda t, w, b: pltpu.VMEM((4, t, w), BF16),
    values_t=lambda t, w, b: pltpu.VMEM((4, w, t), BF16),
    mask=lambda t, w, b: pltpu.VMEM((4, t, t), F32),
    scores=lambda t, w, b: pltpu.VMEM((2, 4, t, t), F32),
    probs=lambda t, w, b: pltpu.VMEM((HEADS, 4, t, t), BF16),
    keys_t=lambda t, w, b: pltpu.VMEM((4, w, t), BF16),
    values=lambda t, w, b: pltpu.VMEM((4, t, w), BF16),
    context_t=lambda t, w, b: pltpu.VMEM((w, t), BF16),
    scaled=lambda t, w, b: pltpu.VMEM((t, w), F32),
    inverse=lambda t, w, b: pltpu.VMEM((t, 128), F32),
    normed=lambda t, w, b: pltpu.VMEM((t, w), F32),
    low=lambda t, w, b: pltpu.VMEM((t, w), BF16),
    low_t=lambda t, w, b: pltpu.VMEM((w, t), BF16),
    act=lambda t, w, b: pltpu.VMEM((t, 4 * w), BF16),
    act_t=lambda t, w, b: pltpu.VMEM((4 * w, t), BF16),
    slope=lambda t, w, b: pltpu.VMEM((t, 4 * w), BF16),
    result=lambda t, w, b: pltpu.VMEM((t, w), BF16),
    grad_res=lambda t, w, b: pltpu.VMEM((t, w), F32),
    grad_ffn=lambda t, w, b: pltpu.VMEM((t, w), BF16),
    small=lambda t, w, b: pltpu.VMEM((16, w), F32),
    routes=lambda t, w, b: pltpu.VMEM((8, t), F32),
    all_send=lambda t, w, b: pltpu.SemaphoreType.DMA((5,)),
    all_recv=lambda t, w, b: pltpu.SemaphoreType.DMA((4,)),
    misc_send=lambda t, w, b: pltpu.SemaphoreType.DMA((5,)),
    misc_recv=lambda t, w, b: pltpu.SemaphoreType.DMA((5,)),
    weight_recv=lambda t, w, b: pltpu.SemaphoreType.DMA((UNITS, 4)),
    own_sem=lambda t, w, b: pltpu.SemaphoreType.DMA((2,)),
    store_sem=lambda t, w, b: pltpu.SemaphoreType.DMA((18,)),
)

class Kept(NamedTuple):
    full: object
    probs: object
    keys_t: object
    values: object
    packed_t: object
    query: object
    context_t: object
    scaled: object
    inverse: object
    low_t: object
    act_t: object
    slope: object
    result: object
    grad_res: object
    grad_ffn: object
    small: object
    routes: object


HEADS = 12
NORM_EPS = 1e-12


def normalize(value):
    centre = value - jnp.mean(value, -1, keepdims=True)
    spread = jnp.mean(centre * centre, -1, keepdims=True)
    inverse = lax.rsqrt(spread + NORM_EPS)
    return centre * inverse, inverse


def forward_kernel(z_size, *refs):
    order, valid, ids, tokens, cotangent, teacher = refs[:6]
    narrow, up_bias = refs[6:14], refs[14]
    w_query, w_key, w_value, w_out, w_up, w_down = refs[15:21]
    refs = refs[21:]
    outs = Kept(*refs[: len(Kept._fields)])
    s = SimpleNamespace(**dict(zip(FORWARD_SCRATCH, refs[len(Kept._fields) :])))
    route = Route(z_size)
    place = route.place
    rows, width = tokens.shape
    blocks = route.blocks
    full = s.full
    weights = Weights(place, full, s.all_send.at[4], s.weight_recv)
    stores = []

    def keep(source, target):
        copy = pltpu.make_async_copy(source, target, s.store_sem.at[len(stores)])
        copy.start()
        stores.append(copy)

    sources = (
        [w_key, w_value, w_query, w_out]
        + [w_up.at[:, width * i : width * (i + 1)] for i in range(4)]
        + [w_down.at[BLOCK * i : BLOCK * (i + 1), :] for i in range(4)]
    )
    own_copies = [
        pltpu.make_async_copy(source, weights.at(unit, place.dp), s.own_sem.at[min(unit // 2, 1)])
        for unit, source in enumerate(sources)
    ]
    for copy in own_copies:
        copy.start()
    s.ints[route.home, 0:1, :] = order[...]
    s.ints[route.home, 1:2, :] = valid[...]
    s.pieces[place.dp] = jnp.zeros((16, 128), F32)
    for index, ref in enumerate(narrow):
        s.pieces[place.dp, index : index + 1, :BLOCK] = ref[...].astype(F32)
    s.pieces[place.dp, 8:11, :] = up_bias[...].astype(F32)
    s.teach_out[...] = teacher[...].astype(BF16)
    route.greet_all()

    def ints_copy(other):
        return remote(
            s.ints.at[route.home],
            s.ints.at[route.home],
            s.all_send.at[0],
            s.all_recv.at[0],
            route.owner(other),
        )

    def all_others(ref, index):
        ref = ref.at[: ref.shape[0] - 1]
        return remote(ref, ref, s.all_send.at[index], s.all_recv.at[index], place.mate)

    def each_other(start, action):
        def one(step, carry):
            action((start + step) % blocks)
            return carry

        lax.fori_loop(1, blocks, one, 0)

    each_other(route.home, lambda other: ints_copy(other).start())
    def piece_copy(step):
        other = (place.dp + step) % 8
        return remote(
            s.pieces.at[place.dp],
            s.pieces.at[place.dp],
            s.all_send.at[1],
            s.all_recv.at[1],
            {"dp": other},
        )

    for step in range(1, 8):
        piece_copy(step).start()
    ids_copy = remote(ids, s.ids.at[1], s.misc_send.at[0], s.misc_recv.at[0], place.mate)
    ids_copy.start()
    s.ids[0] = ids[...]
    def own_wait(units, index):
        ref = full.at[: BLOCK * units, :]
        pltpu.make_async_copy(ref, ref, s.own_sem.at[index]).wait()

    own_wait(2, 0)
    weights.begin(0)
    weights.begin(1)
    own_wait(UNITS - 2, 1)

    all_others(s.ints, 0).wait_recv()
    count = jnp.zeros((1, rows), F32)
    for other in range(blocks):
        s.order[other : other + 1, :] = s.ints[other, 0:1, :]
        count = count + s.ints[other, 1:2, :].astype(F32)
    count = jnp.sum(count, 1, keepdims=True)
    orders = s.order[...]
    source = lax.shift_right_logical(orders, 8)
    local = (orders - source * rows).astype(F32)
    mine = source == route.home
    earlier = one_hot(iota((rows, rows), 0) < iota((rows, rows), 1))
    rank = dot(one_hot(mine), earlier)
    per_block = rows // blocks
    slots = jnp.zeros((blocks, 128), F32)
    for k in range(per_block):
        picked = jnp.sum(jnp.where(mine & (rank == k), local, 0.0), 1, keepdims=True)
        slots = jnp.where(iota((blocks, 128), 1) == k, picked, slots)
    spread = one_hot(
        lax.shift_right_logical(iota((rows, blocks), 0), 3) == iota((rows, blocks), 1)
    )
    picked = jnp.sum(
        jnp.where(
            iota((rows, 128), 1) == (iota((rows, 128), 0) & 7),
            dot(spread, slots.astype(BF16)),
            0.0,
        ),
        1,
        keepdims=True,
    )
    lane = iota((rows, rows), 1)
    diagonal = iota((rows, rows), 0) == lane
    ordered = one_hot(lane.astype(F32) == picked)

    def pack_copy(which, block):
        return remote(
            s.pack_out.at[which, block],
            s.pack_in.at[which, route.home],
            s.all_send.at[2 + which],
            s.all_recv.at[2 + which],
            route.worker(block),
        )

    def pack(which, value):
        s.pack_out[which] = (
            dot(ordered, value).reshape(blocks, per_block, width).astype(BF16)
        )

    def send_pack(which):
        each_other(route.block, lambda block: pack_copy(which, block).start())
        s.pack_in[which, route.home] = s.pack_out[which, route.block]

    def take_pack(which):
        all_others(s.pack_in.at[which], 2 + which).wait_recv()
        flat = s.pack_in[which].astype(F32).reshape(rows, width).astype(BF16)
        return dot(one_hot(lane.astype(F32) == place_col), flat).astype(BF16)

    pack(0, tokens[...])
    send_pack(0)
    weights.tick(2)
    pack(1, cotangent[...])
    s.routes[1:2, :] = jnp.sum(jnp.where(diagonal, picked, 0.0), 0, keepdims=True)

    moved_to = route.worker(route.home)
    stays = route.block == route.home
    teach_copy = remote(s.teach_out, s.teach_in, s.misc_send.at[1], s.misc_recv.at[1], moved_to)

    all_others(s.pieces, 1).wait_recv()
    wrapped = one_hot(
        iota((BLOCK, width), 0) == iota((BLOCK, width), 1) - BLOCK * (iota((BLOCK, width), 1) // BLOCK)
    )
    owner = iota((16, width), 1) // BLOCK
    vectors = jnp.zeros((16, width), F32)
    for k in range(8):
        vectors = vectors + jnp.where(owner == k, dot(s.pieces[k, :, :BLOCK].astype(BF16), wrapped), 0.0)
    s.vectors[...] = vectors
    for k in range(8):
        for i in range(3):
            first = 4 * BLOCK * (k % 2) + 128 * i
            s.vectors[8 + k // 2 : 9 + k // 2, first : first + 128] = s.pieces[k, 8 + i : 9 + i, :]

    def vector(index):
        return s.vectors[index : index + 1, :]

    ids_copy.wait_recv()
    here = s.ints[route.block, 0:1, :]
    source_row = lax.shift_right_logical(here, 8).astype(F32)
    source_col = column(source_row)
    same = source_col == source_row
    before = iota((rows, rows), 1) < iota((rows, rows), 0)
    rank_col = jnp.sum(jnp.where(same & before, 1.0, 0.0), 1, keepdims=True)
    rank_row = jnp.sum(
        jnp.where(same & jnp.logical_not(before | diagonal), 1.0, 0.0), 0, keepdims=True
    )
    s.routes[0:1, :] = source_row * 8 + rank_row
    place_col = source_col * 8 + rank_col
    from_own = place.core == route.group_core
    query_row = jnp.where(from_own, s.ids[0, route.quarter], s.ids[1, route.quarter]).astype(F32)
    for quarter in range(4):
        key_row = jnp.where(from_own, s.ids[0, quarter], s.ids[1, quarter]).astype(F32)
        s.mask[quarter] = jnp.where(column(key_row) == query_row, 0.0, -1e30)

    def rows_copy(kind, arriving):
        quarter, to = (
            (route.quarter, route.pair),
            (route.quarter, place.mate),
            (route.pair_quarter, place.mate),
        )[kind]
        if arriving:
            quarter = (route.pair_quarter, route.mate_quarter, route.far_quarter)[kind]
        ref = s.packed.at[quarter]
        return remote(ref, ref, s.misc_send.at[2 + kind], s.misc_recv.at[2 + kind], to)

    packed = take_pack(0)
    s.packed[route.quarter] = packed
    s.packed_t[0] = packed.T
    rows_copy(0, False).start()
    rows_copy(1, False).start()
    weights.tick(3)
    send_pack(1)

    @pl.when(jnp.logical_not(stays))
    def _():
        teach_copy.start()

    @pl.when(stays)
    def _():
        s.teach_in[...] = s.teach_out[...]

    weights.tick(4)
    weights.tick(5)

    def whole(unit):
        return full[width * unit : width * (unit + 1), :]

    def keys_values(quarter):
        value = s.packed[quarter]
        keys = dot(value, whole(0)).astype(BF16)
        s.keys[quarter] = keys
        s.keys_t[quarter] = keys.T
        values = (dot(value, whole(1)) + vector(1)).astype(BF16)
        s.values[quarter] = values
        s.values_t[quarter] = values.T

    rows_copy(0, True).wait_recv()
    rows_copy(2, False).start()
    weights.ready(0)
    weights.ready(1)
    keys_values(route.quarter)
    rows_copy(1, True).wait_recv()
    keys_values(route.mate_quarter)
    weights.tick(6)
    s.packed_t[1] = s.packed[route.pair_quarter].T
    keep(s.packed_t, outs.packed_t)
    keys_values(route.pair_quarter)
    rows_copy(2, True).wait_recv()
    keys_values(route.far_quarter)
    weights.ready(2)
    scale = (width // HEADS) ** -0.5
    s.query[...] = (
        (dot(packed, whole(2)) + vector(0)).astype(BF16).astype(F32) * scale
    ).astype(BF16)
    keep(s.query, outs.query)
    keep(s.keys_t, outs.keys_t)
    keep(s.values, outs.values)
    weights.tick(7)

    head = width // HEADS
    left_half = iota((rows, 2 * head), 1) < head

    def pair_of_heads(pair, carry):
        @pl.when(pair % 2 == 0)
        def _():
            weights.tick(pair // 2 + 8)

        lanes = pl.ds(pl.multiple_of(2 * head * pair, 2 * head), 2 * head)
        both = s.query[:, lanes]
        for side in range(2):
            keep_lane = left_half if side == 0 else jnp.logical_not(left_half)
            chosen = jnp.where(keep_lane, both, jnp.zeros_like(both))
            top = jnp.full((1, rows), -3e38, F32)
            for quarter in range(4):
                part = dot_nt(s.keys[quarter, :, lanes], chosen) + s.mask[quarter]
                s.scores[side, quarter] = part
                top = jnp.maximum(top, jnp.max(part, 0, keepdims=True))
            total = jnp.zeros((1, rows), F32)
            for quarter in range(4):
                part = jnp.exp(s.scores[side, quarter] - top)
                s.scores[side, quarter] = part
                total = total + jnp.sum(part, 0, keepdims=True)
            share = 1.0 / total
            index = 2 * pair + side
            down = pl.ds(pl.multiple_of(head * index, head), head)
            summed = jnp.zeros((head, rows), F32)
            for quarter in range(4):
                part = (s.scores[side, quarter] * share).astype(BF16)
                s.probs[index, quarter] = part
                summed = summed + dot(s.values_t[quarter, down, :], part)
            s.context_t[down, :] = summed.astype(BF16)
        return carry

    lax.fori_loop(0, HEADS // 2, pair_of_heads, 0)
    keep(s.probs, outs.probs)
    keep(s.context_t, outs.context_t)
    weights.tick(11)

    weights.ready(3)
    branch = dot(s.context_t[...].T, whole(3)) + vector(2)
    scaled, inverse = normalize(packed.astype(F32) + branch)
    s.scaled[...] = scaled
    s.inverse[...] = jnp.broadcast_to(inverse, (rows, 128))
    normed = scaled * vector(3) + vector(4)
    s.normed[...] = normed
    low = normed.astype(BF16)
    s.low[...] = low
    s.low_t[...] = low.T
    keep(s.scaled, outs.scaled)
    keep(s.inverse, outs.inverse)
    keep(s.low_t, outs.low_t)

    root_half, norm = 2.0**-0.5, (2.0 * math.pi) ** -0.5
    piece = width // 2

    def up(step, carry):
        lanes = pl.ds(pl.multiple_of(piece * (step % 2), piece), piece)
        wide = pl.ds(pl.multiple_of(piece * step, piece), piece)
        down = pl.ds(pl.multiple_of(width * (4 + step // 2), width), width)
        bias = s.vectors[pl.ds(8 + step // 2, 1), lanes]
        pre = dot(s.low[...], full[down, lanes]) + bias
        phi = 0.5 + 0.5 * lax.erf(pre * root_half)
        act = (pre * phi).astype(BF16)
        s.act[:, wide] = act
        s.act_t[wide, :] = act.T
        s.slope[:, wide] = (phi + pre * (norm * jnp.exp(-0.5 * pre * pre))).astype(BF16)
        return carry

    for part in range(4):
        weights.ready(4 + part)
        lax.fori_loop(2 * part, 2 * part + 2, up, 0)
        if part % 2 == 1:
            weights.pass_on(10 + part // 2)
            weights.corner(9 + part // 2)
    keep(full.at[: 8 * width, :], outs.full.at[: 8 * width, :])
    weights.corner(11)
    keep(s.act_t, outs.act_t)
    keep(s.slope, outs.slope)
    for part in range(4):
        weights.ready(8 + part)
    keep(full.at[8 * width :, :], outs.full.at[8 * width :, :])
    ffn = dot(s.act[...], full[8 * width :, :]) + vector(5)

    scaled, inverse = normalize(s.normed[...] + ffn)
    result = scaled * vector(6) + vector(7)
    s.result[...] = result.astype(BF16)
    keep(s.result, outs.result)

    @pl.when(jnp.logical_not(stays))
    def _():
        teach_copy.wait_recv()

    counts = column(s.ints[route.block, 1:2, :].astype(F32))
    miss = counts * (result - s.teach_in[...].astype(F32))
    factor = 1.0 / (count * width)
    s.small[...] = jnp.zeros((16, width), F32)
    s.small[12:13, :] = jnp.sum(miss * miss, 0, keepdims=True) * factor
    grad_out = take_pack(1).astype(F32) + (2.0 * factor) * miss
    s.small[6:7, :] = jnp.sum(grad_out * scaled, 0, keepdims=True)
    s.small[7:8, :] = jnp.sum(grad_out, 0, keepdims=True)
    s.small[13:14, :] = vector(3)
    grad_scaled = grad_out * vector(6)
    grad_res = inverse * (
        grad_scaled
        - jnp.mean(grad_scaled, -1, keepdims=True)
        - scaled * jnp.mean(grad_scaled * scaled, -1, keepdims=True)
    )
    s.grad_res[...] = grad_res
    grad_ffn = grad_res.astype(BF16)
    s.grad_ffn[...] = grad_ffn
    s.small[5:6, :] = jnp.sum(grad_ffn.astype(F32), 0, keepdims=True)
    keep(s.grad_res, outs.grad_res)
    keep(s.grad_ffn, outs.grad_ffn)
    keep(s.small, outs.small)
    keep(s.routes, outs.routes)

    weights.drain()
    for index, ref in enumerate((s.ints, s.pieces, s.pack_out.at[0], s.pack_out.at[1])):
        all_others(ref, index).wait_send()
    ids_copy.wait_send()
    for kind in range(3):
        rows_copy(kind, False).wait_send()

    @pl.when(jnp.logical_not(stays))
    def _():
        teach_copy.wait_send()

    for copy in stores:
        copy.wait()


def encoder_forward(z_size, *inputs):
    rows, width = inputs[3].shape
    blocks = 8 * z_size
    scratch = {name: make(rows, width, blocks) for name, make in FORWARD_SCRATCH.items()}
    vmem, anywhere = pl.BlockSpec(memory_space=pltpu.VMEM), pl.BlockSpec(memory_space=pl.ANY)
    results = pl.pallas_call(
        partial(forward_kernel, z_size),
        out_shape=tuple(
            jax.ShapeDtypeStruct(scratch[name].shape, scratch[name].dtype) for name in Kept._fields
        ),
        in_specs=[vmem] * 15 + [anywhere] * 6,
        out_specs=(anywhere,) * len(Kept._fields),
        scratch_shapes=list(scratch.values()),
        compiler_params=pltpu.CompilerParams(
            collective_id=0, has_side_effects=True, vmem_limit_bytes=62 * 2**20
        ),
        name="encoder_forward",
    )(*inputs)
    return Kept(*results)


LEFT = (0, 1, 2, 3, 4, 4, 4, 4, 5)
RIGHT = (0, 0, 0, 0, 1, 2, 3, 4, 5, 6)


class Grads:
    def __init__(self, place, s, out):
        self.place, self.s, self.out = place, s, out
        self.tok_rows = s.left.shape[2] // 2
        half = BLOCK // 2
        self.low, self.high = slice(0, half), slice(half, BLOCK)

    def source_rows(self, group, j, core):
        shard = 2 * j + core
        if group < 4:
            return pl.ds(pl.multiple_of(4 * BLOCK * shard + BLOCK * group, 32), BLOCK)
        return pl.ds(pl.multiple_of(BLOCK * shard, 32), BLOCK)

    def left_copy(self, group, j, source):
        if group < 6:
            target = self.s.left.at[group, BLOCK * j : BLOCK * (j + 1), self.tok_rows :]
        else:
            first = self.tok_rows * (group - 4)
            target = self.s.left_x.at[BLOCK * j : BLOCK * (j + 1), first : first + self.tok_rows]
        return remote(
            source.at[self.source_rows(group, j, 1 - self.place.core), :],
            target,
            self.s.end_send.at[4],
            self.s.left_recv.at[group],
            self.place.mate,
        )

    def left_own(self, group, j, source):
        if group < 6:
            target = self.s.left.at[group, BLOCK * j : BLOCK * (j + 1), : self.tok_rows]
        else:
            first = self.tok_rows * (group - 6)
            target = self.s.left_x.at[BLOCK * j : BLOCK * (j + 1), first : first + self.tok_rows]
        return pltpu.make_async_copy(
            source.at[self.source_rows(group, j, self.place.core), :],
            target,
            self.s.left_own.at[group],
        )

    def give_left(self, group, source):
        for j in range(4):
            self.left_copy(group, j, source).start()
            self.left_own(group, j, source).start()

    def take_left(self, group, source):
        if group < 6:
            mine = self.s.left.at[group, :, : self.tok_rows]
            theirs = self.s.left.at[group, :, self.tok_rows :]
        else:
            mine = self.s.left_x.at[:, : self.tok_rows]
            theirs = self.s.left_x.at[:, self.tok_rows * 2 : self.tok_rows * 3]
        remote(
            theirs, theirs, self.s.end_send.at[4], self.s.left_recv.at[group], self.place.mate
        ).wait_recv()
        pltpu.make_async_copy(mine, mine, self.s.left_own.at[group]).wait()

    def own_right(self, index):
        return self.s.right.at[index, : self.tok_rows, :]

    def right_copy(self, index):
        if index < 7:
            source, target = self.own_right(index), self.s.right.at[index, self.tok_rows :, :]
        else:
            half = 2 * self.tok_rows
            source = self.s.right_kv.at[index - 7, :half, :]
            target = self.s.right_kv.at[index - 7, half:, :]
        return remote(
            source,
            target,
            self.s.end_send.at[5] if index < 7 else self.s.end_send.at[3],
            self.s.right_recv.at[index],
            self.place.mate,
        )

    def copy(self, unit, kind):
        place, low, high, s = self.place, self.low, self.high, self.s
        source, target, to = (
            (s.out_d.at[unit, low], s.in_dx.at[unit], place.across),
            (s.out_d.at[unit, high], s.in_dy.at[unit], place.along),
            (s.out_x.at[unit, low], s.in_x.at[unit, low], place.across),
            (s.out_x.at[unit, high], s.in_x.at[unit, high], place.across),
            (s.out_y.at[unit, low], s.in_y.at[unit, low], place.along),
            (s.out_y.at[unit, high], s.in_y.at[unit, high], place.along),
            (s.out_x.at[unit], s.in_z.at[0, unit], {"ctx": place.z + 1}),
            (s.out_y.at[unit], s.in_z.at[1, unit], {"ctx": place.z - 1}),
        )[kind]
        if 2 <= kind < 6:
            send = s.send.at[unit]
        else:
            send = s.end_send.at[(0, 0, 0, 0, 0, 0, 1, 2)[kind]]
        recv = s.recv.at[unit, (0, 0, 1, 1, 1, 1, 2, 3)[kind]]
        return remote(source, target, send, recv, to)

    def together(self, ref, send, recv):
        return remote(ref, ref, send, recv, self.place.mate)

    def part(self, j):
        return pl.ds(pl.multiple_of(BLOCK * j, 32), BLOCK)

    def multiply(self, unit):
        place, s = self.place, self.s
        if unit < 9:
            s.partial[...] = dot(s.left[LEFT[unit]], s.right[RIGHT[unit]])
        elif unit == 9:
            n = self.tok_rows
            s.partial[...] = dot(s.left_x[:, :n], s.right[6, :n, :]) + dot(
                s.left_x[:, 2 * n : 3 * n], s.right[6, n:, :]
            )
        else:
            s.partial[...] = dot(s.left_x[...], s.right_kv[unit - 10])
        s.out_d[unit] = s.partial[self.part(place.j_d), :].astype(BF16)
        s.out_x[unit] = s.partial[self.part(place.j_x), :].astype(BF16)
        s.out_y[unit] = s.partial[self.part(place.j_y), :].astype(BF16)
        s.total[unit] = s.partial[self.part(place.j_own), :]

    def begin(self, unit):
        for kind in (0, 1, 2, 5):
            self.copy(unit, kind).start()

    def pass_on(self, unit):
        low, high, s = self.low, self.high, self.s
        self.together(s.out_d.at[unit], s.send.at[unit], s.recv.at[unit, 0]).wait_recv()
        s.out_y[unit, low] = (
            s.out_y[unit, low].astype(F32) + s.in_dx[unit].astype(F32)
        ).astype(BF16)
        s.out_x[unit, high] = (
            s.out_x[unit, high].astype(F32) + s.in_dy[unit].astype(F32)
        ).astype(BF16)
        self.copy(unit, 4).start()
        self.copy(unit, 3).start()

    def gather(self, unit):
        s = self.s
        both = self.together(s.in_x.at[:2], s.send.at[unit], s.recv.at[unit, 1])
        both.wait_recv()
        s.total[unit] = (
            s.total[unit] + s.in_x[unit].astype(F32) + s.in_y[unit].astype(F32)
        )
        both.wait_send()

    def hop(self, unit, step):
        place, s = self.place, self.s
        for way, turn in ((0, step), (1, place.z_size - 1 - step)):

            @pl.when(place.z == turn)
            def _():
                value = s.total[unit]
                if step > 0:
                    self.copy(unit, 6 + way).wait_recv()
                    value = value + s.in_z[way, unit].astype(F32)
                (s.out_x, s.out_y)[way][unit] = value.astype(BF16)
                self.copy(unit, 6 + way).start()

    def result(self, unit):
        return pltpu.make_async_copy(
            self.s.total.at[unit], self.out.at[unit], self.s.out_sem.at[0]
        )

    def finish(self, unit):
        place, s = self.place, self.s
        last = place.z_size - 1

        @pl.when(place.z == last)
        def _():
            self.copy(unit, 6).wait_recv()

        @pl.when(place.z == 0)
        def _():
            self.copy(unit, 7).wait_recv()

        for way, present in ((0, place.z > 0), (1, place.z < last)):

            @pl.when(present)
            def _():
                s.total[unit] = s.total[unit] + s.in_z[way, unit].astype(F32)

        self.result(unit).start()

    def line(self, *work):
        for unit, stage in work:
            if stage == 0:
                self.gather(unit)
            if stage < self.place.z_size - 1:
                self.hop(unit, stage)
            else:
                self.finish(unit)

    def drain(self, lefts):
        place, s = self.place, self.s

        def sent(ref, index):
            self.together(ref, s.end_send.at[index], s.recv.at[0, 0]).wait_send()

        sent(s.out_d, 0)

        @pl.when(place.z < place.z_size - 1)
        def _():
            sent(s.out_x, 1)

        @pl.when(place.z > 0)
        def _():
            sent(s.out_y, 2)

        pltpu.make_async_copy(s.total, s.total, s.out_sem.at[0]).wait()
        sent(s.right_kv.at[:, : 2 * self.tok_rows, :], 3)
        sent(lefts[0], 4)
        sent(s.right.at[:, : self.tok_rows, :], 5)


BACKWARD_SCRATCH = dict(
    left=lambda t, w, b: pltpu.VMEM((6, 4 * BLOCK, 2 * t), BF16),
    left_x=lambda t, w, b: pltpu.VMEM((4 * BLOCK, 4 * t), BF16),
    right=lambda t, w, b: pltpu.VMEM((7, 2 * t, w), BF16),
    right_kv=lambda t, w, b: pltpu.VMEM((2, 4 * t, w), BF16),
    partial=lambda t, w, b: pltpu.VMEM((4 * BLOCK, w), F32),
    out_d=lambda t, w, b: pltpu.VMEM((UNITS, BLOCK, w), BF16),
    out_x=lambda t, w, b: pltpu.VMEM((UNITS, BLOCK, w), BF16),
    out_y=lambda t, w, b: pltpu.VMEM((UNITS, BLOCK, w), BF16),
    in_dx=lambda t, w, b: pltpu.VMEM((UNITS, BLOCK // 2, w), BF16),
    in_dy=lambda t, w, b: pltpu.VMEM((UNITS, BLOCK // 2, w), BF16),
    in_x=lambda t, w, b: pltpu.VMEM((UNITS, BLOCK, w), BF16),
    in_y=lambda t, w, b: pltpu.VMEM((UNITS, BLOCK, w), BF16),
    total=lambda t, w, b: pltpu.VMEM((UNITS, BLOCK, w), F32),
    in_z=lambda t, w, b: pltpu.VMEM((2, UNITS, BLOCK, w), BF16),
    weight_a=lambda t, w, b: pltpu.VMEM((4 * w, w), BF16),
    weight_b=lambda t, w, b: pltpu.VMEM((4 * w, w), BF16),
    probs=lambda t, w, b: pltpu.VMEM((2, 2, 4, t, t), BF16),
    keys_t=lambda t, w, b: pltpu.VMEM((4, w, t), BF16),
    values=lambda t, w, b: pltpu.VMEM((4, t, w), BF16),
    query=lambda t, w, b: pltpu.VMEM((t, w), BF16),
    context_t=lambda t, w, b: pltpu.VMEM((w, t), BF16),
    scaled=lambda t, w, b: pltpu.VMEM((t, w), F32),
    inverse=lambda t, w, b: pltpu.VMEM((t, 128), F32),
    slope=lambda t, w, b: pltpu.VMEM((t, 4 * w), BF16),
    result=lambda t, w, b: pltpu.VMEM((t, w), BF16),
    grad_res=lambda t, w, b: pltpu.VMEM((t, w), F32),
    small=lambda t, w, b: pltpu.VMEM((16, w), F32),
    routes=lambda t, w, b: pltpu.VMEM((8, t), F32),
    grad_context=lambda t, w, b: pltpu.VMEM((t, w), BF16),
    grad_context_t=lambda t, w, b: pltpu.VMEM((w, t), BF16),
    grad_query_t=lambda t, w, b: pltpu.VMEM((w, t), BF16),
    kv_out=lambda t, w, b: pltpu.VMEM((HEADS // 2, 4, t, t), BF16),
    kv_mate=lambda t, w, b: pltpu.VMEM((HEADS // 2, 2, t, t), BF16),
    pair_out=lambda t, w, b: pltpu.VMEM((t, w), BF16),
    pair_in=lambda t, w, b: pltpu.VMEM((t, w), BF16),
    back_out=lambda t, w, b: pltpu.VMEM((2, b, t // b, w), BF16),
    back_in=lambda t, w, b: pltpu.VMEM((2, b, t // b, w), BF16),
    homes=lambda t, w, b: pltpu.VMEM((2, t, w), BF16),
    sums=lambda t, w, b: pltpu.VMEM((3, 16, w), F32),
    got_sums=lambda t, w, b: pltpu.VMEM((3, 16, w), F32),
    got_z=lambda t, w, b: pltpu.VMEM((b // 8, 16, w), F32),
    send=lambda t, w, b: pltpu.SemaphoreType.DMA((UNITS,)),
    end_send=lambda t, w, b: pltpu.SemaphoreType.DMA((6,)),
    recv=lambda t, w, b: pltpu.SemaphoreType.DMA((UNITS, 4)),
    left_recv=lambda t, w, b: pltpu.SemaphoreType.DMA((8,)),
    left_own=lambda t, w, b: pltpu.SemaphoreType.DMA((8,)),
    right_recv=lambda t, w, b: pltpu.SemaphoreType.DMA((9,)),
    out_sem=lambda t, w, b: pltpu.SemaphoreType.DMA((1,)),
    load_sem=lambda t, w, b: pltpu.SemaphoreType.DMA((15,)),
    probs_sem=lambda t, w, b: pltpu.SemaphoreType.DMA((2,)),
    kv_send=lambda t, w, b: pltpu.SemaphoreType.DMA((1,)),
    kv_recv=lambda t, w, b: pltpu.SemaphoreType.DMA((HEADS // 2,)),
    pair_sem=lambda t, w, b: pltpu.SemaphoreType.DMA((2,)),
    back_send=lambda t, w, b: pltpu.SemaphoreType.DMA((2,)),
    back_recv=lambda t, w, b: pltpu.SemaphoreType.DMA((2,)),
    sum_send=lambda t, w, b: pltpu.SemaphoreType.DMA((4,)),
    sum_recv=lambda t, w, b: pltpu.SemaphoreType.DMA((4,)),
)


def backward_kernel(z_size, *refs):
    count = len(Kept._fields)
    given = Kept(*refs[:count])
    out_grads, out_homes, out_small = refs[count : count + 3]
    s = SimpleNamespace(**dict(zip(BACKWARD_SCRATCH, refs[count + 3 :])))
    route = Route(z_size)
    place = route.place
    rows, width = s.query.shape
    blocks = route.blocks
    grads = Grads(place, s, out_grads)
    head = width // HEADS
    pairs = HEADS // 2

    count = [0]

    def load(source, target):
        copy = pltpu.make_async_copy(source, target, s.load_sem.at[count[0]])
        count[0] += 1
        copy.start()
        return copy

    def loaded(*copies):
        for copy in copies:
            copy.wait()

    full = given.full
    l_ffn = load(given.grad_ffn, grads.own_right(0))
    l_routes = load(given.routes, s.routes)
    l_result = load(given.result, s.result)
    l_down = load(full.at[2 * 4 * width :, :], s.weight_a)
    l_up = load(full.at[4 * width : 8 * width, :], s.weight_b)
    l_slope = load(given.slope, s.slope)
    l_small = load(given.small, s.small)
    l_grad_res = load(given.grad_res, s.grad_res)
    l_scaled = load(given.scaled, s.scaled)
    l_inverse = load(given.inverse, s.inverse)
    l_query = load(given.query, s.query)
    l_context_t = load(given.context_t, s.context_t)
    l_keys_t = load(given.keys_t, s.keys_t)
    l_values = load(given.values, s.values)

    def probs_copy(pair):
        slot = pair % 2
        return pltpu.make_async_copy(
            given.probs.at[pl.ds(2 * pair, 2)], s.probs.at[slot], s.probs_sem.at[slot]
        )

    probs_copy(0).start()
    lefts = (given.act_t,) * 4 + (given.low_t, given.context_t)
    lefts += (given.packed_t.at[0], given.packed_t.at[1])
    route.greet_all()

    def each_other(start, action):
        def one(step, carry):
            action((start + step) % blocks)
            return carry

        lax.fori_loop(1, blocks, one, 0)

    loaded(l_ffn)
    grads.right_copy(0).start()
    for group in range(8):
        grads.give_left(group, lefts[group])

    def back_copy(which, other):
        return remote(
            s.back_out.at[which, other],
            s.back_in.at[which, route.block],
            s.back_send.at[which],
            s.back_recv.at[which],
            route.owner(other),
        )

    def all_back(ref, which):
        ref = ref.at[which, : blocks - 1]
        return remote(ref, ref, s.back_send.at[which], s.back_recv.at[which], place.mate)

    def order_back(which, value):
        ordered = one_hot(iota((rows, rows), 0).astype(F32) == s.routes[0:1, :])
        s.back_out[which] = (
            dot(ordered, value).reshape(blocks, rows // blocks, width).astype(BF16)
        )
        s.back_in[which, route.block] = s.back_out[which, route.home]

    def send_back(which, part=0, parts=1):
        def one(step, carry):
            back_copy(which, (route.home + step) % blocks).start()
            return carry

        lax.fori_loop(max(1, blocks * part // parts), blocks * (part + 1) // parts, one, 0)

    def take_back(which):
        all_back(s.back_in, which).wait_recv()
        placed = one_hot(iota((rows, rows), 0).astype(F32) == s.routes[1:2, :])
        flat = s.back_in[which].astype(F32).reshape(rows, width).astype(BF16)
        s.homes[which] = dot(placed, flat).astype(BF16)

    loaded(l_routes, l_result)
    order_back(0, s.result[...])
    send_back(0)
    grads.right_copy(0).wait_recv()
    for unit in range(4):
        grads.take_left(unit, lefts[unit])
        grads.multiply(unit)
        if unit < 2:
            grads.begin(unit)

    loaded(l_down, l_up, l_slope, l_small, l_grad_res, l_scaled, l_inverse)
    grad_ffn = s.right[0, :rows, :]
    grad_normed = s.grad_res[...]
    for part in range(4):
        block = slice(width * part, width * (part + 1))
        grad_act = dot_nt(grad_ffn, s.weight_a[block, :])
        grad_pre = (grad_act * s.slope[:, block].astype(F32)).astype(BF16)
        s.right[1 + part, :rows, :] = grad_pre
        s.small[8 + part : 9 + part, :] = jnp.sum(grad_pre.astype(F32), 0, keepdims=True)
        grad_normed = grad_normed + dot_nt(grad_pre, s.weight_b[block, :])
        grads.right_copy(1 + part).start()
    l_rest = load(full.at[: 4 * width, :], s.weight_a)

    grads.pass_on(0)
    grads.begin(2)
    scaled = s.scaled[...]
    s.small[3:4, :] = jnp.sum(grad_normed * scaled, 0, keepdims=True)
    s.small[4:5, :] = jnp.sum(grad_normed, 0, keepdims=True)
    grad_scaled = grad_normed * s.small[13:14, :]
    grad_res = s.inverse[:, :1] * (
        grad_scaled
        - jnp.mean(grad_scaled, -1, keepdims=True)
        - scaled * jnp.mean(grad_scaled * scaled, -1, keepdims=True)
    )
    s.grad_res[...] = grad_res
    grad_branch = grad_res.astype(BF16)
    s.right[5, :rows, :] = grad_branch
    s.small[2:3, :] = jnp.sum(grad_branch.astype(F32), 0, keepdims=True)
    grads.right_copy(5).start()
    loaded(l_rest)
    grad_context = dot_nt(grad_branch, s.weight_a[3 * width :, :]).astype(BF16)
    s.grad_context[...] = grad_context
    s.grad_context_t[...] = grad_context.T
    loaded(l_query, l_context_t, l_keys_t, l_values)

    def kv_copy(pair, kind):
        quarter = (route.mate_quarter, route.far_quarter)[kind]
        return remote(
            s.kv_out.at[pair, quarter],
            s.kv_mate.at[pair, kind],
            s.kv_send.at[0],
            s.kv_recv.at[pair],
            place.mate,
        )

    def kv_sum(pair):
        lanes = pl.ds(pl.multiple_of(2 * head * pair, 2 * head), 2 * head)
        got = s.kv_mate.at[pair]
        remote(got, got, s.kv_send.at[0], s.kv_recv.at[pair], place.mate).wait_recv()
        for kind, quarter in enumerate((route.quarter, route.pair_quarter)):
            summed = (
                s.kv_out[pair, quarter].astype(F32) + s.kv_mate[pair, kind].astype(F32)
            ).astype(BF16)
            block = slice(rows * kind, rows * (kind + 1))
            s.right_kv[0, block, lanes] = summed[:, : 2 * head]
            s.right_kv[1, block, lanes] = summed[:, 2 * head :]

    left_half = iota((rows, 2 * head), 1) < head
    scale = head**-0.5

    def pair_of_heads(pair, carry):
        @pl.when(pair < pairs - 1)
        def _():
            probs_copy(pair + 1).start()

        @pl.when(pair == 2)
        def _():
            grads.pass_on(1)
            grads.begin(3)
            grads.take_left(4, lefts[4])
            grads.right_copy(1).wait_recv()
            grads.multiply(4)
            grads.line((0, 0))

        @pl.when(pair == 4)
        def _():
            grads.line((1, 0), (0, 1))
            grads.pass_on(2)
            grads.begin(4)

        @pl.when(pair > 1)
        def _():
            kv_sum(pair - 2)

        probs_copy(pair).wait()
        slot = pair % 2
        lanes = pl.ds(pl.multiple_of(2 * head * pair, 2 * head), 2 * head)
        both_c = s.grad_context[:, lanes]
        both_q = s.query[:, lanes]
        chosen_c, chosen_q, delta, grad_q = [], [], [], []
        for side in range(2):
            keep_lane = left_half if side == 0 else jnp.logical_not(left_half)
            chosen_c.append(jnp.where(keep_lane, both_c, jnp.zeros_like(both_c)))
            chosen_q.append(jnp.where(keep_lane, both_q, jnp.zeros_like(both_q)))
            down = pl.ds(pl.multiple_of(head * (2 * pair + side), head), head)
            delta.append(
                jnp.sum(
                    s.grad_context_t[down, :].astype(F32) * s.context_t[down, :].astype(F32),
                    0,
                    keepdims=True,
                )
            )
            grad_q.append(jnp.zeros((head, rows), F32))
        for quarter in range(4):
            value = s.values[quarter, :, lanes]
            grad_k = jnp.zeros((rows, 2 * head), F32)
            grad_v = jnp.zeros((rows, 2 * head), F32)
            for side in range(2):
                down = pl.ds(pl.multiple_of(head * (2 * pair + side), head), head)
                probs = s.probs[slot, side, quarter]
                grad_probs = dot_nt(value, chosen_c[side])
                grad_scores = (probs.astype(F32) * (grad_probs - delta[side])).astype(BF16)
                grad_v = grad_v + dot(probs, chosen_c[side])
                grad_k = grad_k + dot(grad_scores, chosen_q[side])
                grad_q[side] = grad_q[side] + dot(s.keys_t[quarter, down, :], grad_scores)
            s.kv_out[pair, quarter, :, : 2 * head] = grad_k.astype(BF16)
            s.kv_out[pair, quarter, :, 2 * head :] = grad_v.astype(BF16)
        kv_copy(pair, 0).start()
        kv_copy(pair, 1).start()
        for side in range(2):
            down = pl.ds(pl.multiple_of(head * (2 * pair + side), head), head)
            s.grad_query_t[down, :] = (grad_q[side] * scale).astype(BF16)
        return carry

    lax.fori_loop(0, pairs, pair_of_heads, 0)
    grad_query = s.grad_query_t[...].T
    s.right[6, :rows, :] = grad_query
    s.small[0:1, :] = jnp.sum(grad_query.astype(F32), 0, keepdims=True)
    grads.right_copy(6).start()
    kv_sum(pairs - 2)
    kv_sum(pairs - 1)
    grads.right_copy(7).start()
    grads.right_copy(8).start()
    grad_value = s.right_kv[1, : 2 * rows, :]
    s.small[1:2, :] = jnp.sum(grad_value.astype(F32), 0, keepdims=True)
    grads.right_copy(2).wait_recv()
    grads.multiply(5)
    grads.pass_on(3)
    grads.begin(5)
    grads.line((2, 0), (1, 1), (0, 2))
    from_keys = dot_nt(s.right_kv[0, : 2 * rows, :], s.weight_a[:width, :])
    from_values = dot_nt(grad_value, s.weight_a[width : 2 * width, :])
    s.pair_out[...] = (from_keys[rows:] + from_values[rows:]).astype(BF16)
    s.grad_res[...] = (
        s.grad_res[...]
        + from_keys[:rows]
        + from_values[:rows]
        + dot_nt(s.right[6, :rows, :], s.weight_a[2 * width : 3 * width, :])
    )
    pair_copies = [
        remote(
            s.pair_out.at[block],
            s.pair_in.at[block],
            s.pair_sem.at[0],
            s.pair_sem.at[1],
            route.pair,
        )
        for block in (slice(rows // 4 * j, rows // 4 * (j + 1)) for j in range(4))
    ]
    pair_copies[0].start()

    def sum_copy(stage, to):
        return remote(
            s.small if stage == 0 else s.sums.at[stage - 1],
            s.got_sums.at[stage],
            s.sum_send.at[stage],
            s.sum_recv.at[stage],
            to,
        )

    sum_copies = [
        sum_copy(stage, to) for stage, to in enumerate((place.mate, place.across, place.along))
    ]
    def sum_stage(stage):
        sum_copies[stage].wait_recv()
        before = s.small[...] if stage == 0 else s.sums[stage - 1]
        s.sums[stage] = before + s.got_sums[stage]

    sum_copies[0].start()
    pair_copies[1].start()
    grads.right_copy(3).wait_recv()
    grads.multiply(6)
    grads.pass_on(4)
    grads.begin(6)
    grads.line((3, 0), (2, 1), (1, 2))
    pair_copies[2].start()
    pair_copies[3].start()
    grads.right_copy(4).wait_recv()
    grads.multiply(7)
    grads.pass_on(5)
    grads.begin(7)
    grads.line((4, 0), (3, 1), (2, 2))
    grads.take_left(5, lefts[5])
    grads.right_copy(5).wait_recv()
    grads.multiply(8)
    grads.pass_on(6)
    grads.begin(8)
    grads.line((5, 0), (4, 1), (3, 2))
    sum_stage(0)
    sum_copies[1].start()
    remote(
        s.pair_out, s.pair_in, s.pair_sem.at[0], s.pair_sem.at[1], route.pair
    ).wait_recv()
    order_back(1, (s.grad_res[...] + s.pair_in[...].astype(F32)).astype(BF16))
    send_back(1, 0, 2)
    grads.take_left(6, lefts[6])
    grads.take_left(7, lefts[7])
    grads.right_copy(6).wait_recv()
    grads.multiply(9)
    grads.pass_on(7)
    grads.begin(9)
    grads.line((6, 0), (5, 1), (4, 2))
    grads.right_copy(7).wait_recv()
    grads.multiply(10)
    grads.pass_on(8)
    grads.begin(10)
    grads.line((7, 0), (6, 1), (5, 2))
    send_back(1, 1, 2)
    sum_stage(1)
    sum_copies[2].start()
    grads.right_copy(8).wait_recv()
    grads.multiply(11)
    grads.pass_on(9)
    grads.begin(11)
    grads.line((8, 0), (7, 1), (6, 2))
    grads.pass_on(10)
    grads.line((9, 0), (8, 1), (7, 2))
    sum_stage(2)

    def z_copy(step):
        other = (place.z + step) % z_size
        return remote(
            s.sums.at[2],
            s.got_z.at[place.z],
            s.sum_send.at[3],
            s.sum_recv.at[3],
            {"ctx": other},
        )

    for step in range(1, z_size):
        z_copy(step).start()
    s.got_z[place.z] = s.sums[2]
    grads.pass_on(11)
    grads.line((10, 0), (9, 1), (8, 2))
    take_back(0)
    grads.line((11, 0), (10, 1), (9, 2), (0, 3), (1, 3), (2, 3), (3, 3))
    grads.line((11, 1), (10, 2), (4, 3), (5, 3), (6, 3), (7, 3))
    take_back(1)
    home_copy = pltpu.make_async_copy(s.homes, out_homes, s.probs_sem.at[0])
    home_copy.start()
    grads.line((11, 2), (8, 3), (9, 3))
    z_all = s.got_z.at[: z_size - 1]
    z_all = remote(z_all, z_all, s.sum_send.at[3], s.sum_recv.at[3], place.mate)
    z_all.wait_recv()
    total = s.got_z[0]
    for z in range(1, z_size):
        total = total + s.got_z[z]
    out_small[...] = total
    grads.line((10, 3), (11, 3))

    grads.drain(lefts)
    remote(s.kv_mate, s.kv_mate, s.kv_send.at[0], s.kv_recv.at[0], place.mate).wait_send()
    pair_all = remote(s.pair_out, s.pair_in, s.pair_sem.at[0], s.pair_sem.at[1], route.pair)
    pair_all.wait_send()
    for which in range(2):
        all_back(s.back_out, which).wait_send()
    for copy in sum_copies:
        copy.wait_send()
    z_all.wait_send()
    home_copy.wait()


def encoder_backward(z_size, kept):
    rows, width = kept.query.shape
    blocks = 8 * z_size
    scratch = {name: make(rows, width, blocks) for name, make in BACKWARD_SCRATCH.items()}
    vmem, anywhere = pl.BlockSpec(memory_space=pltpu.VMEM), pl.BlockSpec(memory_space=pl.ANY)
    return pl.pallas_call(
        partial(backward_kernel, z_size),
        out_shape=(
            jax.ShapeDtypeStruct((UNITS, BLOCK, width), F32),
            jax.ShapeDtypeStruct((2, rows, width), BF16),
            jax.ShapeDtypeStruct((16, width), F32),
        ),
        in_specs=[anywhere] * len(Kept._fields),
        out_specs=(anywhere, anywhere, vmem),
        scratch_shapes=list(scratch.values()),
        compiler_params=pltpu.CompilerParams(
            collective_id=1, has_side_effects=True, vmem_limit_bytes=62 * 2**20
        ),
        name="encoder_backward",
    )(*kept)


def finish_kernel(grads, homes, small, *refs):
    out, loss, input_grad, g_query, g_key, g_value, g_out, g_up, g_down = refs[:9]
    narrow, up_bias = refs[9:17], refs[17]
    units, rows_in, rows_out, in_sem, out_sem = refs[18:]
    width = units.shape[2]
    row_loads = [
        pltpu.make_async_copy(homes.at[i], rows_in.at[i], in_sem.at[UNITS + i]) for i in range(2)
    ]
    unit_loads = [
        pltpu.make_async_copy(grads.at[i], units.at[i], in_sem.at[i]) for i in range(UNITS)
    ]
    for copy in row_loads + unit_loads:
        copy.start()
    dp = lax.axis_index("dp")
    turned = pltpu.roll(small[...], (width - BLOCK * dp) % width, 1)
    for index, ref in enumerate(narrow):
        ref[...] = turned[index : index + 1, :BLOCK]
    up_row = small[pl.ds(8 + dp // 2, 1), :]
    up_row = jnp.where(dp % 2 == 0, up_row[:, : 4 * BLOCK], up_row[:, 4 * BLOCK :])
    for i in range(3):
        up_bias[i : i + 1, :] = up_row[:, 128 * i : 128 * (i + 1)]
    loss[...] = jnp.sum(small[12:13, :], 1, keepdims=True)
    stores = []

    def store(source, target):
        copy = pltpu.make_async_copy(source, target, out_sem.at[len(stores)])
        copy.start()
        stores.append(copy)

    for i, target in enumerate((out, input_grad)):
        row_loads[i].wait()
        rows_out[i] = rows_in[i].astype(F32)
        store(rows_out.at[i], target)
    targets = [g_down.at[BLOCK * i : BLOCK * (i + 1), :] for i in range(4)]
    targets += [g_up.at[:, width * i : width * (i + 1)] for i in range(4)]
    targets += [g_out, g_query, g_key, g_value]
    for i, target in enumerate(targets):
        unit_loads[i].wait()
        store(units.at[i], target)
    for copy in stores:
        copy.wait()


def finish(grads, homes, small):
    _, rows, width = homes.shape
    vmem, anywhere = pl.BlockSpec(memory_space=pltpu.VMEM), pl.BlockSpec(memory_space=pl.ANY)
    row = jax.ShapeDtypeStruct((rows, width), F32)
    square = jax.ShapeDtypeStruct((BLOCK, width), F32)
    return pl.pallas_call(
        finish_kernel,
        out_shape=(
            row,
            jax.ShapeDtypeStruct((1, 1), F32),
            row,
            square,
            square,
            square,
            square,
            jax.ShapeDtypeStruct((BLOCK, 4 * width), F32),
            jax.ShapeDtypeStruct((4 * BLOCK, width), F32),
        )
        + (jax.ShapeDtypeStruct((1, BLOCK), F32),) * 8
        + (jax.ShapeDtypeStruct((3, 128), F32),),
        in_specs=[anywhere, anywhere, vmem],
        out_specs=(anywhere, vmem) + (anywhere,) * 7 + (vmem,) * 9,
        scratch_shapes=[
            pltpu.VMEM((UNITS, BLOCK, width), F32),
            pltpu.VMEM((2, rows, width), BF16),
            pltpu.VMEM((2, rows, width), F32),
            pltpu.SemaphoreType.DMA((UNITS + 2,)),
            pltpu.SemaphoreType.DMA((UNITS + 2,)),
        ],
        name="finish",
    )(grads, homes, small)


norm_eps = 1e-12
floor_score = -1e30
masked_score = -1e32


def product(left, right):
    return jnp.dot(left, right, preferred_element_type=jnp.float32)


def inner_rows(left, right):
    return lax.dot_general(
        left, right, (((0,), (0,)), ((), ())), preferred_element_type=jnp.float32
    )


def against(left, right):
    return lax.dot_general(
        left, right, (((1,), (1,)), ((), ())), preferred_element_type=jnp.float32
    )


def layer_norm(value, gain, shift):
    centre = value - jnp.mean(value, -1, keepdims=True)
    spread = jnp.mean(centre * centre, -1, keepdims=True)
    inverse_dev = lax.rsqrt(spread + norm_eps)
    scaled = centre * inverse_dev
    return (scaled * gain + shift, scaled, inverse_dev)


def norm_back(grad_norm, scaled, inverse_dev, gain):
    grad_scaled = grad_norm * gain
    centred = grad_scaled - jnp.mean(grad_scaled, -1, keepdims=True)
    return inverse_dev * (centred - scaled * jnp.mean(grad_scaled * scaled, -1, keepdims=True))


def per_device(
    tokens,
    cotangent,
    token_order,
    sequence_ids,
    valid,
    teacher,
    w_query,
    b_query,
    w_key,
    w_value,
    b_value,
    w_out,
    b_out,
    norm1_gain,
    norm1_bias,
    w_up,
    b_up,
    w_down,
    b_down,
    norm2_gain,
    norm2_bias,
):
    tok_rows, model_width = tokens.shape
    peer_count = lax.axis_size(("dp", "ctx"))
    per_peer = tok_rows // peer_count
    head_count = HEADS
    head_size = model_width // head_count
    score_scale = head_size ** (-0.5)
    gelu_exact = partial(jax.nn.gelu, approximate=False)
    positions = lax.iota(jnp.int32, tok_rows)
    source = token_order // tok_rows
    slot_sort = jnp.argsort(source * tok_rows + positions)
    requests = (token_order[slot_sort] % tok_rows).reshape(peer_count, per_peer)
    wanted = lax.all_to_all(requests, ("dp", "ctx"), split_axis=0, concat_axis=0, tiled=True)
    wanted_flat = wanted.reshape(tok_rows)
    packed_x, packed_cot = (
        lax.all_to_all(
            tokens[wanted_flat].reshape(peer_count, per_peer, model_width),
            ("dp", "ctx"),
            split_axis=0,
            concat_axis=0,
            tiled=True,
        ),
        lax.all_to_all(
            cotangent[wanted_flat].reshape(peer_count, per_peer, model_width),
            ("dp", "ctx"),
            split_axis=0,
            concat_axis=0,
            tiled=True,
        ),
    )
    arrival = jnp.argsort(slot_sort)
    inputs = packed_x.reshape(tok_rows, model_width)[arrival]
    cot_rows = packed_cot.reshape(tok_rows, model_width)[arrival].astype(jnp.float32)
    valid_rows = valid.astype(jnp.float32)
    valid_count = lax.psum(jnp.sum(valid_rows), ("dp", "ctx"))
    (
        query_weight,
        query_bias,
        key_weight,
        value_weight,
        value_bias,
        out_weight,
        out_bias,
        gain_one,
        shift_one,
        up_weight,
        up_bias,
        down_weight,
        down_bias,
        gain_two,
        shift_two,
    ) = (
        lax.all_gather(w_query, "dp", axis=0, tiled=True),
        lax.all_gather(b_query, "dp", axis=0, tiled=True),
        lax.all_gather(w_key, "dp", axis=0, tiled=True),
        lax.all_gather(w_value, "dp", axis=0, tiled=True),
        lax.all_gather(b_value, "dp", axis=0, tiled=True),
        lax.all_gather(w_out, "dp", axis=0, tiled=True),
        lax.all_gather(b_out, "dp", axis=0, tiled=True),
        lax.all_gather(norm1_gain, "dp", axis=0, tiled=True),
        lax.all_gather(norm1_bias, "dp", axis=0, tiled=True),
        lax.all_gather(w_up, "dp", axis=0, tiled=True),
        lax.all_gather(b_up, "dp", axis=0, tiled=True),
        lax.all_gather(w_down, "dp", axis=0, tiled=True),
        lax.all_gather(b_down, "dp", axis=0, tiled=True),
        lax.all_gather(norm2_gain, "dp", axis=0, tiled=True),
        lax.all_gather(norm2_bias, "dp", axis=0, tiled=True),
    )
    queries = (product(inputs, query_weight) + query_bias).astype(jnp.bfloat16)
    key_rows = product(inputs, key_weight).astype(jnp.bfloat16)
    values = (product(inputs, value_weight) + value_bias).astype(jnp.bfloat16)
    group_ids = sequence_ids.reshape(-1)
    cycle_index = lax.axis_index("ctx")
    query_ids = lax.dynamic_slice_in_dim(group_ids, cycle_index * tok_rows, tok_rows)
    query_heads = queries.reshape(tok_rows, head_count, head_size)
    initial = (
        jnp.full((head_count, tok_rows), floor_score, jnp.float32),
        jnp.zeros((head_count, tok_rows), jnp.float32),
        jnp.zeros((tok_rows, head_count, head_size), jnp.float32),
    )
    folded = initial
    key_piece = lax.all_gather(key_rows, "ctx", axis=0, tiled=True)
    value_piece = lax.all_gather(values, "ctx", axis=0, tiled=True)
    length = key_piece.shape[0]
    attend_block_rows = math.gcd(length, 512)
    block_count = length // attend_block_rows

    def one_block(carried, inputs_block):
        running_max, running_sum, summed = carried
        key_block, value_block, key_start = inputs_block
        key_ids = lax.dynamic_slice_in_dim(group_ids, key_start, attend_block_rows)
        scores = (
            jnp.einsum("qhd,khd->hqk", query_heads, key_block, preferred_element_type=jnp.float32)
            * score_scale
        )
        scores = jnp.where((query_ids[:, None] == key_ids[None, :])[None], scores, masked_score)
        new_max = jnp.maximum(running_max, jnp.max(scores, -1))
        factor = jnp.exp(running_max - new_max)
        weights = jnp.exp(scores - new_max[:, :, None])
        running_sum = running_sum * factor + jnp.sum(weights, -1)
        update = jnp.einsum(
            "hqk,khd->qhd",
            weights.astype(jnp.bfloat16),
            value_block,
            preferred_element_type=jnp.float32,
        )
        summed = summed * jnp.transpose(factor)[:, :, None] + update
        return ((new_max, running_sum, summed), None)

    key_starts = attend_block_rows * lax.iota(jnp.int32, block_count)
    folded, _ = lax.scan(
        one_block,
        folded,
        (
            key_piece.reshape(block_count, attend_block_rows, head_count, head_size),
            value_piece.reshape(block_count, attend_block_rows, head_count, head_size),
            key_starts,
        ),
    )
    running_max, running_sum, summed = folded
    attended = summed / jnp.transpose(running_sum)[:, :, None]
    log_total = running_max + jnp.log(running_sum)
    context = attended.reshape(tok_rows, model_width).astype(jnp.bfloat16)
    branch = product(context, out_weight) + out_bias
    normed, scaled_one, inverse_one = layer_norm(
        inputs.astype(jnp.float32) + branch, gain_one, shift_one
    )
    normed_low = normed.astype(jnp.bfloat16)
    pre_act = product(normed_low, up_weight) + up_bias
    activated = gelu_exact(pre_act).astype(jnp.bfloat16)
    ffn_out = product(activated, down_weight) + down_bias
    result, scaled_two, inverse_two = layer_norm(normed + ffn_out, gain_two, shift_two)
    difference = result - teacher
    loss_total = lax.psum(jnp.sum(valid_rows[:, None] * difference * difference), ("dp", "ctx"))
    loss_value = loss_total / (valid_count * model_width)
    grad_out = cot_rows + 2.0 / (valid_count * model_width) * valid_rows[:, None] * difference
    grad_gain_two = jnp.sum(grad_out * scaled_two, 0)
    grad_shift_two = jnp.sum(grad_out, 0)
    grad_res_two = norm_back(grad_out, scaled_two, inverse_two, gain_two)
    grad_ffn = grad_res_two.astype(jnp.bfloat16)
    grad_down = inner_rows(activated, grad_ffn)
    grad_down_bias = jnp.sum(grad_ffn.astype(jnp.float32), 0)
    grad_act = against(grad_ffn, down_weight)
    _, gelu_pull = jax.vjp(gelu_exact, pre_act)
    grad_pre = gelu_pull(grad_act)[0].astype(jnp.bfloat16)
    grad_up = inner_rows(normed_low, grad_pre)
    grad_up_bias = jnp.sum(grad_pre.astype(jnp.float32), 0)
    grad_normed = grad_res_two + against(grad_pre, up_weight)
    ffn_shards = (
        lax.psum_scatter(
            grad_up.astype(jnp.bfloat16), "dp", scatter_dimension=0, tiled=True
        ).astype(jnp.float32),
        lax.psum_scatter(
            grad_up_bias.astype(jnp.bfloat16), "dp", scatter_dimension=0, tiled=True
        ).astype(jnp.float32),
        lax.psum_scatter(
            grad_down.astype(jnp.bfloat16), "dp", scatter_dimension=0, tiled=True
        ).astype(jnp.float32),
        lax.psum_scatter(
            grad_down_bias.astype(jnp.bfloat16), "dp", scatter_dimension=0, tiled=True
        ).astype(jnp.float32),
        lax.psum_scatter(
            grad_gain_two.astype(jnp.bfloat16), "dp", scatter_dimension=0, tiled=True
        ).astype(jnp.float32),
        lax.psum_scatter(
            grad_shift_two.astype(jnp.bfloat16), "dp", scatter_dimension=0, tiled=True
        ).astype(jnp.float32),
    )
    grad_gain_one = jnp.sum(grad_normed * scaled_one, 0)
    grad_shift_one = jnp.sum(grad_normed, 0)
    grad_res_one = norm_back(grad_normed, scaled_one, inverse_one, gain_one)
    grad_branch = grad_res_one.astype(jnp.bfloat16)
    grad_out_w = inner_rows(context, grad_branch)
    grad_out_bias = jnp.sum(grad_branch.astype(jnp.float32), 0)
    grad_context = against(grad_branch, out_weight).astype(jnp.bfloat16)
    grad_heads = grad_context.reshape(tok_rows, head_count, head_size)
    delta = jnp.transpose(jnp.sum(grad_heads.astype(jnp.float32) * attended, -1))
    all_keys, all_values = (
        lax.all_gather(key_rows, "ctx", axis=0, tiled=True),
        lax.all_gather(values, "ctx", axis=0, tiled=True),
    )
    group_len = all_keys.shape[0]
    block_rows = math.gcd(group_len, 512)
    block_count = group_len // block_rows
    key_starts = block_rows * lax.iota(jnp.int32, block_count)
    key_blocks = all_keys.reshape(block_count, block_rows, head_count, head_size)
    value_blocks = all_values.reshape(block_count, block_rows, head_count, head_size)

    def query_side(key_block, value_block, key_start):
        key_ids = lax.dynamic_slice_in_dim(group_ids, key_start, block_rows)
        scores = (
            jnp.einsum("qhd,khd->hqk", query_heads, key_block, preferred_element_type=jnp.float32)
            * score_scale
        )
        scores = jnp.where((query_ids[:, None] == key_ids[None, :])[None], scores, masked_score)
        probs = jnp.exp(scores - log_total[:, :, None])
        grad_probs = jnp.einsum(
            "qhd,khd->hqk", grad_heads, value_block, preferred_element_type=jnp.float32
        )
        grad_scores = (probs * (grad_probs - delta[:, :, None])).astype(jnp.bfloat16)
        return (probs, grad_scores)

    def back_block(grad_query, inputs_block):
        key_block, value_block, key_start = inputs_block
        probs, grad_scores = query_side(key_block, value_block, key_start)
        grad_query = (
            grad_query
            + jnp.einsum("hqk,khd->qhd", grad_scores, key_block, preferred_element_type=jnp.float32)
            * score_scale
        )
        grad_key = (
            jnp.einsum("hqk,qhd->khd", grad_scores, query_heads, preferred_element_type=jnp.float32)
            * score_scale
        )
        grad_value = jnp.einsum(
            "hqk,qhd->khd",
            probs.astype(jnp.bfloat16),
            grad_heads,
            preferred_element_type=jnp.float32,
        )
        return (grad_query, (grad_key, grad_value))

    grad_query, (key_parts, value_parts) = lax.scan(
        back_block,
        jnp.zeros((tok_rows, head_count, head_size), jnp.float32),
        (key_blocks, value_blocks, key_starts),
    )
    key_total, value_total = (
        lax.psum_scatter(
            key_parts.reshape(group_len, model_width).astype(jnp.bfloat16),
            "ctx",
            scatter_dimension=0,
            tiled=True,
        ).astype(jnp.float32),
        lax.psum_scatter(
            value_parts.reshape(group_len, model_width).astype(jnp.bfloat16),
            "ctx",
            scatter_dimension=0,
            tiled=True,
        ).astype(jnp.float32),
    )
    grad_keys = key_total.astype(jnp.bfloat16)
    grad_values = value_total.astype(jnp.bfloat16)
    grad_queries = grad_query.reshape(tok_rows, model_width).astype(jnp.bfloat16)
    grad_query_w = inner_rows(inputs, grad_queries)
    grad_query_bias = jnp.sum(grad_queries.astype(jnp.float32), 0)
    grad_key_w = inner_rows(inputs, grad_keys)
    grad_value_w = inner_rows(inputs, grad_values)
    grad_value_bias = jnp.sum(grad_values.astype(jnp.float32), 0)
    grad_inputs = (
        grad_res_one
        + against(grad_queries, query_weight)
        + against(grad_keys, key_weight)
        + against(grad_values, value_weight)
    )
    attn_shards = (
        lax.psum_scatter(
            grad_query_w.astype(jnp.bfloat16), "dp", scatter_dimension=0, tiled=True
        ).astype(jnp.float32),
        lax.psum_scatter(
            grad_query_bias.astype(jnp.bfloat16), "dp", scatter_dimension=0, tiled=True
        ).astype(jnp.float32),
        lax.psum_scatter(
            grad_key_w.astype(jnp.bfloat16), "dp", scatter_dimension=0, tiled=True
        ).astype(jnp.float32),
        lax.psum_scatter(
            grad_value_w.astype(jnp.bfloat16), "dp", scatter_dimension=0, tiled=True
        ).astype(jnp.float32),
        lax.psum_scatter(
            grad_value_bias.astype(jnp.bfloat16), "dp", scatter_dimension=0, tiled=True
        ).astype(jnp.float32),
        lax.psum_scatter(
            grad_out_w.astype(jnp.bfloat16), "dp", scatter_dimension=0, tiled=True
        ).astype(jnp.float32),
        lax.psum_scatter(
            grad_out_bias.astype(jnp.bfloat16), "dp", scatter_dimension=0, tiled=True
        ).astype(jnp.float32),
        lax.psum_scatter(
            grad_gain_one.astype(jnp.bfloat16), "dp", scatter_dimension=0, tiled=True
        ).astype(jnp.float32),
        lax.psum_scatter(
            grad_shift_one.astype(jnp.bfloat16), "dp", scatter_dimension=0, tiled=True
        ).astype(jnp.float32),
    )
    totals = (
        lax.psum(attn_shards[0].astype(jnp.bfloat16), "ctx").astype(jnp.float32),
        lax.psum(attn_shards[1].astype(jnp.bfloat16), "ctx").astype(jnp.float32),
        lax.psum(attn_shards[2].astype(jnp.bfloat16), "ctx").astype(jnp.float32),
        lax.psum(attn_shards[3].astype(jnp.bfloat16), "ctx").astype(jnp.float32),
        lax.psum(attn_shards[4].astype(jnp.bfloat16), "ctx").astype(jnp.float32),
        lax.psum(attn_shards[5].astype(jnp.bfloat16), "ctx").astype(jnp.float32),
        lax.psum(attn_shards[6].astype(jnp.bfloat16), "ctx").astype(jnp.float32),
        lax.psum(attn_shards[7].astype(jnp.bfloat16), "ctx").astype(jnp.float32),
        lax.psum(attn_shards[8].astype(jnp.bfloat16), "ctx").astype(jnp.float32),
        lax.psum(ffn_shards[0].astype(jnp.bfloat16), "ctx").astype(jnp.float32),
        lax.psum(ffn_shards[1].astype(jnp.bfloat16), "ctx").astype(jnp.float32),
        lax.psum(ffn_shards[2].astype(jnp.bfloat16), "ctx").astype(jnp.float32),
        lax.psum(ffn_shards[3].astype(jnp.bfloat16), "ctx").astype(jnp.float32),
        lax.psum(ffn_shards[4].astype(jnp.bfloat16), "ctx").astype(jnp.float32),
        lax.psum(ffn_shards[5].astype(jnp.bfloat16), "ctx").astype(jnp.float32),
    )
    back_out, back_grad = (
        lax.all_to_all(
            result[slot_sort].reshape(peer_count, per_peer, model_width).astype(jnp.bfloat16),
            ("dp", "ctx"),
            split_axis=0,
            concat_axis=0,
            tiled=True,
        ).astype(jnp.float32),
        lax.all_to_all(
            grad_inputs[slot_sort].reshape(peer_count, per_peer, model_width).astype(jnp.bfloat16),
            ("dp", "ctx"),
            split_axis=0,
            concat_axis=0,
            tiled=True,
        ).astype(jnp.float32),
    )
    homeward = jnp.argsort(wanted_flat)
    output = back_out.reshape(tok_rows, model_width)[homeward]
    input_grad = back_grad.reshape(tok_rows, model_width)[homeward]
    return (
        output,
        loss_value,
        input_grad,
        totals[0],
        totals[1],
        totals[2],
        totals[3],
        totals[4],
        totals[5],
        totals[6],
        totals[7],
        totals[8],
        totals[9],
        totals[10],
        totals[11],
        totals[12],
        totals[13],
        totals[14],
    )


def per_device_fast(
    tokens,
    cotangent,
    token_order,
    sequence_ids,
    valid,
    teacher,
    w_query,
    b_query,
    w_key,
    w_value,
    b_value,
    w_out,
    b_out,
    norm1_gain,
    norm1_bias,
    w_up,
    b_up,
    w_down,
    b_down,
    norm2_gain,
    norm2_bias,
):
    rows, width = tokens.shape
    z_size = lax.axis_size("ctx")
    narrow = (b_query, b_value, b_out, norm1_gain, norm1_bias, b_down, norm2_gain, norm2_bias)
    kept = encoder_forward(
        z_size,
        token_order.reshape(1, rows),
        valid.reshape(1, rows),
        sequence_ids.reshape(z_size, 1, rows),
        tokens,
        cotangent,
        teacher,
        *(vector.reshape(1, BLOCK) for vector in narrow),
        b_up.reshape(3, 128),
        w_query,
        w_key,
        w_value,
        w_out,
        w_up,
        w_down,
    )
    results = finish(*encoder_backward(z_size, kept))
    output, loss, input_grad, g_query, g_key, g_value, g_out, g_up, g_down = results[:9]
    g_b_query, g_b_value, g_b_out, g_gain1, g_bias1, g_b_down, g_gain2, g_bias2, g_b_up = (
        vector.reshape(-1) for vector in results[9:]
    )
    return (
        output,
        loss.reshape(()),
        input_grad,
        g_query,
        g_b_query,
        g_key,
        g_value,
        g_b_value,
        g_out,
        g_b_out,
        g_gain1,
        g_bias1,
        g_up,
        g_b_up,
        g_down,
        g_b_down,
        g_gain2,
        g_bias2,
    )


def solution(mesh):
    in_specs = (
        P(("dp", "ctx"), None),
        P(("dp", "ctx"), None),
        P(("dp", "ctx")),
        P("dp", None),
        P(("dp", "ctx")),
        P(("dp", "ctx"), None),
        P("dp", None),
        P("dp"),
        P("dp", None),
        P("dp", None),
        P("dp"),
        P("dp", None),
        P("dp"),
        P("dp"),
        P("dp"),
        P("dp", None),
        P("dp"),
        P("dp", None),
        P("dp"),
        P("dp"),
        P("dp"),
    )
    out_specs = (
        P(("dp", "ctx"), None),
        P(),
        P(("dp", "ctx"), None),
        P("dp", None),
        P("dp"),
        P("dp", None),
        P("dp", None),
        P("dp"),
        P("dp", None),
        P("dp"),
        P("dp"),
        P("dp"),
        P("dp", None),
        P("dp"),
        P("dp", None),
        P("dp"),
        P("dp"),
        P("dp"),
    )
    fast = dict(mesh.shape) == {"dp": 8, "ctx": 4}
    return jax.shard_map(
        per_device_fast if fast else per_device, mesh=mesh, in_specs=in_specs, out_specs=out_specs, check_vma=False
    )
```
